32 devices in a mesh: tm: 16 (over z, y, x), head: 2 (over core).
Axes of the slice: x: 2, y: 2, z: 4, core: 2. Of those that a mesh axis runs over, the one named last changes fastest.
Arguments:
- patches: bfloat16 [192, 256, 1152], P('tm', None, 'head'), may hold values from -6 to 6
- grid_rows: int32 [192], P('tm'), may hold values from 8 to 16
- frame_ids: int32 [192], P('tm'), may hold values from 0 to 191, as said below
- ln_gain: float32 [1152], replicated, may hold values from 0.1 to 1.9
- w_qkv: bfloat16 [3, 1152, 1152], P(None, None, 'head'), may hold values from -5.9514821 to 5.9514821
- w_out: bfloat16 [1152, 1152], P('head'), may hold values from -0.1875 to 0.1875
- w_conn: bfloat16 [1152, 4096], P(None, 'head'), may hold values from -0.1875 to 0.1875
- norm_gain: float32 [4096], replicated, may hold values from 0.1 to 1.9
- w_x: bfloat16 [4096, 4096], P(None, 'head'), may hold values from -0.09375 to 0.09375
- w_b: bfloat16 [4096, 1024], P(None, 'head'), may hold values from -0.09375 to 0.09375
- w_c: bfloat16 [4096, 1024], P(None, 'head'), may hold values from -0.09375 to 0.09375
- w_dt: bfloat16 [4096, 64], P(None, 'head'), may hold values from -0.09375 to 0.09375
- dt_bias: float32 [64], P('head'), may hold values from -1 to 1
- a_log: float32 [64], P('head'), may hold values from -14 to -3.2
- d_skip: float32 [64], P('head'), may hold values from 0.5 to 1.5
- out_gain: float32 [4096], P('head'), may hold values from 0.1 to 1.9
Outputs:
- stream: bfloat16 [12288, 4096], P('tm', 'head')
- ssd_out: bfloat16 [12288, 4096], P('tm', 'head')
The draws below stay inside these ranges and needn't reach their ends.
Inputs may be any that keep to these rules, and one draw needn't show every extreme that they name: frame_ids is a permutation of the frames; the 12 slots of one tm index hold frames of 12 different time shards, time shard of a frame being frame // 12.
All inputs are finite; a program needn't handle non-finite values.
Results may differ from the reference program's by a relative error of at most 0.013.
Values may be sent and summed in bfloat16 or wider, within the bound.
A program may use at most 128 MiB of HBM per device.

```python
import math
import jax
import jax.numpy as jnp
from jax import lax

GRID = 16
POOL = 4
P_SIZE = 256
PT = 64
VHEADS = 16
VHD = 72
DV = 1152
D = 4096
HEADS = 64
HDIM = 64
STATE = 128
GROUPS = 8
FR_DEV = 12
FRAMES = 192
TOKENS = 12288
STRETCH = 256
N_TM = 16


def draw_frame_ids(key, part):
    offset_key, owner_key, order_key, slot_key = jax.random.split(key, 4)
    offsets = jax.random.permutation(offset_key, N_TM)[:FR_DEV]
    owners = jax.random.permutation(owner_key, N_TM)
    within = jax.vmap(lambda subkey: jax.random.permutation(subkey, FR_DEV))(jax.random.split(order_key, N_TM))
    slot_order = jax.vmap(lambda subkey: jax.random.permutation(subkey, FR_DEV))(jax.random.split(slot_key, N_TM))
    sender = jnp.arange(N_TM)[:, None]
    column = jnp.broadcast_to(jnp.arange(FR_DEV)[None, :], (N_TM, FR_DEV))
    target = (sender + offsets[None, :]) % N_TM
    frames = target * FR_DEV + within[target, column]
    placed = jnp.zeros((N_TM, FR_DEV), jnp.int32).at[jnp.broadcast_to(owners[:, None], (N_TM, FR_DEV)), slot_order].set(frames.astype(jnp.int32))
    return placed.reshape(N_TM * FR_DEV)


def draw_w_qkv(key, part):
    base = jnp.clip(jax.random.normal(key, (3, DV, DV), jnp.float32), -5.0, 5.0) * DV ** (-0.5)
    return base.astype(jnp.bfloat16)


def draw_a_log(key, part):
    pick_key, fast_key, slow_key = jax.random.split(key, 3)
    fast_share = 5
    fast = jax.random.randint(pick_key, (HEADS,), 0, 10) < fast_share
    quick = jax.random.uniform(fast_key, (HEADS,), jnp.float32, math.log(1.0 / 50.0), math.log(1.0 / 25.0))
    gentle = jax.random.uniform(slow_key, (HEADS,), jnp.float32, math.log(0.2), math.log(2.0)) - math.log(TOKENS)
    return jnp.where(fast, quick, gentle)


def place_ends(array, rng, least, high):
    longest = array.shape.index(max(array.shape))
    spots = []
    for shift in (0, 1):
        where = [jax.random.randint(jax.random.fold_in(rng, axis), (), 0, length) for axis, length in enumerate(array.shape)]
        where[longest] = (where[longest] + shift) % array.shape[longest]
        spots.append(tuple(where))
    return array.at[spots[0]].set(least).at[spots[1]].set(high)


def levels(stream_key, dims, cuts, smallest, largest):
    loudness, own = 1.0, jax.random.fold_in(stream_key, 6)
    for position, parts in cuts:
        heights = jnp.exp(jax.random.uniform(jax.random.fold_in(own, position), (parts,), jnp.float32, smallest / len(cuts), largest / len(cuts)))
        loudness = loudness * jnp.repeat(heights, dims[position] // parts).reshape([-1 if axis == position else 1 for axis in range(len(dims))])
    return loudness


def gaussian(own_key, dims, deviation, limit, cuts=(), kind=jnp.bfloat16):
    level = levels(own_key, dims, cuts, -0.22, 0.18) if cuts else 1.0
    result = jax.random.normal(own_key, dims, jnp.float32) * deviation * level
    return jnp.minimum(jnp.maximum(result, -limit), limit).astype(kind)


def setup_inputs(seed: int = 0) -> dict:
    seeds = jax.random.split(jax.random.key(seed), 17)
    patches = gaussian(seeds[0], (FRAMES, P_SIZE, DV), 1.0, 6.0, ((0, 16), (2, 2)))
    grid_rows = place_ends(jax.random.randint(seeds[1], (FRAMES,), GRID // 2, GRID + 1), jax.random.fold_in(seeds[1], 1), GRID // 2, GRID).astype(jnp.int32)
    frame_ids = draw_frame_ids(jax.random.fold_in(seeds[16], 71), 0)
    ln_gain = jnp.clip(1.0 + 0.18 * jax.random.normal(seeds[3], (DV,), jnp.float32), 0.1, 1.9)
    w_qkv = draw_w_qkv(jax.random.fold_in(seeds[16], 71), 0)
    w_out = gaussian(seeds[5], (DV, DV), DV ** -0.5, 0.1875, ((0, 2),))
    w_conn = gaussian(seeds[6], (DV, D), DV ** -0.5, 0.1875, ((1, 2),))
    norm_gain = jnp.clip(1.0 + 0.18 * jax.random.normal(seeds[7], (D,), jnp.float32), 0.1, 1.9)
    w_x = gaussian(seeds[8], (D, HEADS * HDIM), D ** -0.5, 0.09375, ((1, 2),))
    w_b = gaussian(seeds[9], (D, GROUPS * STATE), D ** -0.5, 0.09375, ((1, 2),))
    w_c = gaussian(seeds[10], (D, GROUPS * STATE), D ** -0.5, 0.09375, ((1, 2),))
    w_dt = gaussian(seeds[11], (D, HEADS), D ** -0.5, 0.09375, ((1, 2),))
    dt_bias = jnp.clip(jax.random.uniform(seeds[12], (HEADS,), jnp.float32, -1.0, 1.0) * levels(seeds[12], (HEADS,), ((0, 2),), -0.4, 0.0), -1.0, 1.0)
    a_log = draw_a_log(jax.random.fold_in(seeds[16], 71), 0)
    d_skip = jnp.clip(0.5 + 1.0 * jax.random.uniform(seeds[14], (HEADS,), jnp.float32) ** levels(seeds[14], (HEADS,), ((0, 2),), -0.2, 0.2), 0.5, 1.5)
    out_gain = jnp.clip(1.0 + 0.18 * jax.random.normal(seeds[15], (HEADS * HDIM,), jnp.float32), 0.1, 1.9)
    return dict(patches=patches, grid_rows=grid_rows, frame_ids=frame_ids, ln_gain=ln_gain, w_qkv=w_qkv, w_out=w_out, w_conn=w_conn, norm_gain=norm_gain, w_x=w_x, w_b=w_b, w_c=w_c, w_dt=w_dt, dt_bias=dt_bias, a_log=a_log, d_skip=d_skip, out_gain=out_gain)


highest = lax.Precision.HIGHEST

def layer_norm(rows, gain):
    values = rows.astype(jnp.float32)
    centre = lax.optimization_barrier(jnp.mean(values, axis=-1, keepdims=True))
    spread = lax.optimization_barrier(jnp.mean(jnp.square(values - centre), axis=-1, keepdims=True))
    return ((values - centre) * lax.rsqrt(spread + 1e-06) * gain).astype(jnp.bfloat16)

def vision_frames(frames, grid_rows, ln_gain, w_qkv, w_out):
    frame_count = frames.shape[0]
    normed = layer_norm(frames, ln_gain).reshape(frame_count * P_SIZE, DV)
    queries, keys_all, values_all = [jnp.dot(normed, w_qkv[member], preferred_element_type=jnp.float32).astype(jnp.bfloat16).reshape(frame_count, P_SIZE, VHEADS, VHD) for member in range(3)]
    scores = jnp.einsum('fqhd,fkhd->fhqk', queries.astype(jnp.float32), keys_all.astype(jnp.float32)) * VHD ** (-0.5)
    valid_count = grid_rows * GRID
    usable = jnp.arange(P_SIZE)[None, :] < valid_count[:, None]
    scores = jnp.where(usable[:, None, None, :], scores, -1e+30)
    row_max = lax.optimization_barrier(jnp.max(scores, axis=-1, keepdims=True))
    powered = jnp.exp(scores - row_max)
    weights_soft = (powered / lax.optimization_barrier(jnp.sum(powered, axis=-1, keepdims=True))).astype(jnp.bfloat16)
    context = jnp.einsum('fhqk,fkhd->fqhd', weights_soft.astype(jnp.float32), values_all.astype(jnp.float32)).astype(jnp.bfloat16)
    attended = jnp.dot(context.reshape(frame_count * P_SIZE, DV), w_out, preferred_element_type=jnp.float32)
    summed = frames.astype(jnp.float32).reshape(frame_count * P_SIZE, DV) + attended
    pooled = lax.optimization_barrier(jnp.mean(summed.reshape(frame_count, PT, POOL, DV), axis=2))
    kept_tokens = jnp.arange(PT)[None, :] * POOL < valid_count[:, None]
    return jnp.where(kept_tokens[:, :, None], pooled, 0.0).astype(jnp.bfloat16)

def project(stream_rows, norm_gain, w_x, w_b, w_c, w_dt, dt_bias, a_log):
    values = stream_rows.astype(jnp.float32)
    normed = (values * lax.rsqrt(lax.optimization_barrier(jnp.mean(values * values, axis=-1, keepdims=True)) + 1e-05) * norm_gain).astype(jnp.bfloat16)
    inner_rows = jnp.dot(normed, w_x, preferred_element_type=jnp.float32).astype(jnp.bfloat16)
    write_keys = jnp.dot(normed, w_b, preferred_element_type=jnp.float32).astype(jnp.bfloat16)
    read_keys = jnp.dot(normed, w_c, preferred_element_type=jnp.float32).astype(jnp.bfloat16)
    step_size = jax.nn.softplus(jnp.dot(normed, w_dt, preferred_element_type=jnp.float32) + dt_bias)
    log_decay = -jnp.exp(a_log) * step_size
    return (inner_rows, write_keys, read_keys, step_size, log_decay)

def ssd_stretch(inner_rows, write_keys, read_keys, step_size, log_decay, d_skip, state):
    length = inner_rows.shape[0]
    head_count = step_size.shape[1]
    groups = write_keys.shape[1] // STATE
    per_group = head_count // groups
    cumul = jnp.cumsum(log_decay, axis=0)
    scaled = inner_rows.astype(jnp.float32).reshape(length, head_count, HDIM) * step_size[:, :, None]
    writers = write_keys.astype(jnp.float32).reshape(length, groups, STATE)
    readers = read_keys.astype(jnp.float32).reshape(length, groups, STATE)
    intersection = jnp.einsum('tgn,sgn->gts', readers, writers, precision=highest)
    causal = (jnp.arange(length)[:, None] >= jnp.arange(length)[None, :])[:, :, None]
    spans = cumul[:, None, :] - cumul[None, :, :]
    decays = jnp.where(causal, jnp.exp(jnp.where(causal, spans, 0.0)), 0.0)
    mixing = jnp.repeat(intersection, per_group, axis=0) * jnp.transpose(decays, (2, 0, 1))
    within = jnp.einsum('hts,shp->thp', mixing, scaled, precision=highest)
    carried = jnp.einsum('tgn,gkpn->tgkp', readers, state.reshape(groups, per_group, HDIM, STATE), precision=highest).reshape(length, head_count, HDIM) * jnp.exp(cumul)[:, :, None]
    remaining = jnp.exp(cumul[-1][None, :] - cumul)
    fresh_state = jnp.einsum('sgkp,sgn->gkpn', (scaled * remaining[:, :, None]).reshape(length, groups, per_group, HDIM), writers, precision=highest).reshape(head_count, HDIM, STATE)
    new_state = jnp.exp(cumul[-1])[:, None, None] * state + fresh_state
    outputs = within + carried + d_skip[None, :, None] * inner_rows.astype(jnp.float32).reshape(length, head_count, HDIM)
    return (outputs, new_state, cumul)

def group_norm(outputs, out_gain, groups):
    length = outputs.shape[0]
    grouped = outputs.reshape(length, groups, -1)
    normed = grouped * lax.rsqrt(lax.optimization_barrier(jnp.mean(grouped * grouped, axis=-1, keepdims=True)) + 1e-05)
    return (normed.reshape(length, -1) * out_gain).astype(jnp.bfloat16)

def reference(patches, grid_rows, frame_ids, ln_gain, w_qkv, w_out, w_conn, norm_gain, w_x, w_b, w_c, w_dt, dt_bias, a_log, d_skip, out_gain):

    def vision_block(block_id):
        first = (block_id * FR_DEV).astype(jnp.int32)
        frames = lax.dynamic_slice_in_dim(patches, first, FR_DEV, 0)
        rows_valid = lax.dynamic_slice_in_dim(grid_rows, first, FR_DEV, 0)
        return vision_frames(frames, rows_valid, ln_gain, w_qkv, w_out)
    owned = lax.map(vision_block, jnp.arange(FRAMES // FR_DEV, dtype=jnp.int32)).reshape(FRAMES, PT, DV)
    placement = jnp.zeros((FRAMES,), jnp.int32).at[frame_ids].set(jnp.arange(FRAMES, dtype=jnp.int32))
    in_time = owned[placement].reshape(TOKENS, DV)
    stream = jnp.dot(in_time, w_conn, preferred_element_type=jnp.float32).astype(jnp.bfloat16)

    def stretch_step(state, rows):
        inner_rows, write_keys, read_keys, step_size, log_decay = project(rows, norm_gain, w_x, w_b, w_c, w_dt, dt_bias, a_log)
        outputs, new_state, cumul = ssd_stretch(inner_rows, write_keys, read_keys, step_size, log_decay, d_skip, state)
        return (new_state, group_norm(outputs, out_gain, GROUPS))
    zero_state = jnp.zeros((HEADS, HDIM, STATE), jnp.float32)
    final_state, mixed = lax.scan(stretch_step, zero_state, stream.reshape(TOKENS // STRETCH, STRETCH, D))
    return (stream, mixed.reshape(TOKENS, HEADS * HDIM))
```

```python
import math

import jax
import jax.numpy as jnp
from jax import lax
from jax.experimental import pallas as pl
from jax.experimental.pallas import tpu as pltpu
from jax.sharding import PartitionSpec as P

GRID = 16
POOL = 4
VHD = 72
HDIM = 64
STATE = 128
CHUNK = 128
LANES = 128

f32 = jnp.float32
bf16 = jnp.bfloat16
VMEM = pltpu.VMEM
MESH = pl.DeviceIdType.MESH
CONTRACT_LAST = (((1,), (1,)), ((), ()))
CONTRACT_FIRST = (((0,), (0,)), ((), ()))


def flipped(index, mask, count):
    result, bit = 0, 1
    while bit < count:
        result = result + bit * ((index // bit + mask // bit) % 2)
        bit *= 2
    return result


def partners(index, spot, count):
    if count & (count - 1):
        return (index + spot + 1) % count, (index + 2 * count - spot - 1) % count
    other = flipped(index, count - 1 - spot, count)
    return other, other


def vision_kernel(
    order_ref,
    valid_ref,
    rank_ref,
    present_ref,
    patches_ref,
    gain_ref,
    wqkv_ref,
    wout_ref,
    out_ref,
    full,
    normed,
    qkv,
    context,
    partial,
    partial_in,
    mine,
    pooled_frames,
    outbox,
    patch_send,
    patch_recv,
    partial_send,
    partial_recv,
    frame_send,
    frame_recv,
    forward_send,
    forward_recv,
):
    parts, frames, part_width, patch_count = full.shape
    shards = out_ref.shape[1]
    width = parts * part_width
    local_width = wqkv_ref.shape[1]
    heads = local_width // VHD
    tokens = patch_count // POOL
    batch = normed.shape[1] // patch_count
    factor = VHD ** (-0.5) * math.log2(math.e)
    tm, head = lax.axis_index("tm"), lax.axis_index("head")
    peers = [(head + step) % parts for step in range(1, parts)]
    sources = [(head + parts - step) % parts for step in range(1, parts)]

    def remote(source, target, send, recv, to):
        return pltpu.make_async_remote_copy(
            src_ref=source,
            dst_ref=target,
            send_sem=send,
            recv_sem=recv,
            device_id=to,
            device_id_type=MESH,
        )

    def patch_copy(step, rank, part):
        return remote(
            full.at[part, rank],
            full.at[part, rank],
            patch_send.at[step, rank],
            patch_recv.at[step, rank],
            (tm, peers[step]),
        )

    def partial_copy(step, rank):
        return remote(
            partial.at[rank, peers[step]],
            partial_in.at[rank, step],
            partial_send.at[step, rank],
            partial_recv.at[step, rank],
            (tm, peers[step]),
        )

    def frame_copy(spot):
        return remote(
            outbox.at[spot],
            out_ref.at[head, spot],
            frame_send.at[spot],
            frame_recv.at[spot],
            (partners(tm, spot, shards)[0], head),
        )

    def forward_copy(step, spot, part):
        return remote(
            out_ref.at[part, spot],
            out_ref.at[part, spot],
            forward_send.at[step, spot],
            forward_recv.at[step, spot],
            (tm, peers[step]),
        )

    barrier = pltpu.get_barrier_semaphore()
    for peer in peers:
        pl.semaphore_signal(barrier, inc=1, device_id=(tm, peer), device_id_type=MESH)

    def greet(spot, carry):
        pl.semaphore_signal(
            barrier,
            inc=1,
            device_id=(partners(tm, spot, shards)[1], head),
            device_id_type=MESH,
        )
        return carry

    lax.fori_loop(0, shards - 1, greet, 0)

    def stage(rank, carry):
        full[head, rank] = patches_ref[order_ref[rank]]
        return carry

    lax.fori_loop(0, frames, stage, 0)
    pl.semaphore_wait(barrier, parts - 1 + shards - 1)

    def share(rank, carry):
        for step in range(parts - 1):
            patch_copy(step, rank, head).start()
        return carry

    lax.fori_loop(0, frames, share, 0)

    def normalise(rank, columns):
        total = 0.0
        for part in range(parts):
            total = total + jnp.sum(full[part, rank].astype(f32), axis=0, keepdims=True)
        centre = total / width
        spread = 0.0
        for part in range(parts):
            moved = full[part, rank].astype(f32) - centre
            spread = spread + jnp.sum(moved * moved, axis=0, keepdims=True)
        scale = lax.rsqrt(spread / width + 1e-06)
        for part in range(parts):
            normed[part * part_width : (part + 1) * part_width, columns] = (
                (full[part, rank].astype(f32) - centre) * scale * gain_ref[part]
            ).astype(bf16)

    spot_row = lax.broadcasted_iota(jnp.int32, (8, patch_count), 0)
    spot_key = lax.broadcasted_iota(jnp.int32, (8, patch_count), 1)
    ones_row = jnp.where(spot_row == 0, 1.0, 0.0).astype(f32)

    def extended(member, head_id, columns, extra):
        rows = slice(head_id * VHD, (head_id + 1) * VHD)
        return jnp.concatenate([qkv[member, rows, columns], extra], axis=0).astype(bf16)

    def score(head_id, columns, key_row):
        return lax.dot_general(
            extended(1, head_id, columns, key_row),
            extended(0, head_id, columns, ones_row),
            CONTRACT_FIRST,
            preferred_element_type=f32,
        )

    def mix(head_id, columns, scores):
        powered = jnp.exp2((scores - jnp.max(scores, axis=0, keepdims=True)) * factor)
        mixed = jnp.dot(
            extended(2, head_id, columns, ones_row),
            powered.astype(bf16),
            preferred_element_type=f32,
        )
        context[head_id * VHD : (head_id + 1) * VHD, columns] = mixed[:VHD] * (
            1.0 / mixed[VHD : VHD + 1]
        )

    pool_row = lax.broadcasted_iota(jnp.int32, (tokens, patch_count), 0)
    pool_column = lax.broadcasted_iota(jnp.int32, (tokens, patch_count), 1)
    pooling = jnp.where(pool_column // POOL == pool_row, 1.0 / POOL, 0.0).astype(bf16)
    token_spot = lax.broadcasted_iota(jnp.int32, (tokens, part_width), 0) * POOL
    spans = [slice(b * patch_count, (b + 1) * patch_count) for b in range(batch)]

    def post(spot):
        kept = pooled_frames[rank_ref[spot]]
        outbox[spot] = jnp.where(present_ref[spot] > 0, kept, jnp.zeros_like(kept))

    def settle(rank):
        for step in range(parts - 1):
            partial_copy(step, rank).wait_recv()
        total = mine[rank]
        for step in range(parts - 1):
            total = total + partial_in[rank, step].astype(f32)
        pooled_frames[rank] = jnp.where(token_spot < valid_ref[rank], total, 0.0).astype(bf16)
        post(rank)
        frame_copy(rank).start()

    def forward(spot):
        frame_copy(spot).wait_recv()
        for step in range(parts - 1):
            forward_copy(step, spot, head).start()

    def body(turn, carry):
        ranks = [turn * batch + b for b in range(batch)]
        for rank, span in zip(ranks, spans):
            for step in range(parts - 1):
                patch_copy(step, rank, sources[step]).wait_recv()
            normalise(rank, span)
        for member in range(3):
            qkv[member] = jnp.dot(wqkv_ref[member], normed[...], preferred_element_type=f32)

        @pl.when(turn >= 1)
        def _():
            for b in range(batch):
                settle((turn - 1) * batch + b)

        @pl.when(turn >= 3)
        def _():
            for b in range(batch):
                forward((turn - 3) * batch + b)

        key_rows = [
            jnp.where((spot_row == 0) & (spot_key >= valid_ref[rank]), -1e30, 0.0).astype(f32)
            for rank in ranks
        ]
        todo = [(head_id, b) for head_id in range(heads) for b in range(batch)]
        ahead = 2
        ready = [score(h, spans[b], key_rows[b]) for h, b in todo[:ahead]]
        for at, (h, b) in enumerate(todo):
            if at + ahead < len(todo):
                later, which = todo[at + ahead]
                ready.append(score(later, spans[which], key_rows[which]))
            mix(h, spans[b], ready[at])
        pooled = jnp.concatenate(
            [
                lax.dot_general(
                    pooling,
                    context[:, span].astype(bf16),
                    CONTRACT_LAST,
                    preferred_element_type=f32,
                ).astype(bf16)
                for span in spans
            ],
            axis=0,
        )
        attended = jnp.dot(pooled, wout_ref[...], preferred_element_type=f32)
        for b, rank in enumerate(ranks):
            own = lax.dot_general(
                pooling, full[head, rank], CONTRACT_LAST, preferred_element_type=f32
            )
            for part in range(parts):
                block = attended[
                    b * tokens : (b + 1) * tokens, part * part_width : (part + 1) * part_width
                ]
                partial[rank, part] = block.astype(bf16)
                own = own + jnp.where(head == part, block, 0.0)
            mine[rank] = own
            for step in range(parts - 1):
                partial_copy(step, rank).start()
        return carry

    turns = frames // batch
    lax.fori_loop(0, turns, body, 0)
    for rank in range(frames - batch, frames):
        settle(rank)
    for spot in range(frames, shards):
        post(spot)
        if spot < shards - 1:
            frame_copy(spot).start()
    out_ref[head, shards - 1] = outbox[shards - 1]
    for step in range(parts - 1):
        forward_copy(step, shards - 1, head).start()

    def late_forward(spot, carry):
        forward(spot)
        return carry

    lax.fori_loop(max(turns - 3, 0) * batch, shards - 1, late_forward, 0)

    def drain_ranks(rank, carry):
        for step in range(parts - 1):
            patch_copy(step, rank, head).wait_send()
            partial_copy(step, rank).wait_send()
        return carry

    lax.fori_loop(0, frames, drain_ranks, 0)

    def drain_frames(spot, carry):
        frame_copy(spot).wait_send()
        return carry

    lax.fori_loop(0, shards - 1, drain_frames, 0)

    def drain_forwards(spot, carry):
        for step in range(parts - 1):
            forward_copy(step, spot, sources[step]).wait_recv()
            forward_copy(step, spot, head).wait_send()
        return carry

    lax.fori_loop(0, shards, drain_forwards, 0)


def vision(patches, order, valid, rank, present, gain, w_qkv, w_out, parts, shards):
    frames, part_width, patch_count = patches.shape
    width = parts * part_width
    local_width = w_qkv.shape[1]
    tokens = patch_count // POOL
    batch = math.gcd(frames, 2)
    in_smem = pl.BlockSpec(memory_space=pltpu.SMEM)
    in_vmem = pl.BlockSpec(memory_space=VMEM)
    peers = parts - 1
    dma = pltpu.SemaphoreType.DMA
    return pl.pallas_call(
        vision_kernel,
        out_shape=jax.ShapeDtypeStruct((parts, shards, tokens, part_width), bf16),
        in_specs=[in_smem] * 4 + [in_vmem] * 4,
        out_specs=in_vmem,
        scratch_shapes=[
            VMEM((parts, frames, part_width, patch_count), bf16),
            VMEM((width, batch * patch_count), bf16),
            VMEM((3, local_width, batch * patch_count), f32),
            VMEM((local_width, batch * patch_count), f32),
            VMEM((frames, parts, tokens, part_width), bf16),
            VMEM((frames, peers, tokens, part_width), bf16),
            VMEM((frames, tokens, part_width), f32),
            VMEM((frames, tokens, part_width), bf16),
            VMEM((shards, tokens, part_width), bf16),
            dma((peers, frames)),
            dma((peers, frames)),
            dma((peers, frames)),
            dma((peers, frames)),
            dma((shards,)),
            dma((shards,)),
            dma((peers, shards)),
            dma((peers, shards)),
        ],
        compiler_params=pltpu.CompilerParams(
            collective_id=0, has_side_effects=True, vmem_limit_bytes=56 << 20
        ),
        cost_estimate=pl.CostEstimate(
            flops=frames * patch_count * width * local_width * 10,
            bytes_accessed=12_000_000,
            transcendentals=4_000_000,
        ),
        name="vision",
    )(order, valid, rank, present, patches, gain, w_qkv, w_out)


def routes(frame_ids, grid_rows, shards):
    frames = frame_ids.shape[0]
    tm = lax.axis_index("tm").astype(jnp.int32)
    spots = jnp.arange(shards, dtype=jnp.int32)
    targets, sources = partners(tm, spots, shards)
    slots = jnp.arange(frames, dtype=jnp.int32)
    total = lambda chosen, member, axis: jnp.sum(
        jnp.where(chosen, member, 0), axis=axis
    ).astype(jnp.int32)
    goes = (frame_ids // frames)[:, None] == targets[None, :]
    spot_of = total(goes, spots[None, :], 1)
    rank_of = jnp.sum(spot_of[None, :] < spot_of[:, None], axis=1).astype(jnp.int32)
    holds = rank_of[None, :] == slots[:, None]
    order = total(holds, slots[None, :], 1)
    valid = total(holds, (grid_rows * GRID)[None, :], 1)
    rank = total(goes, rank_of[:, None], 0)
    present = jnp.sum(goes, axis=0).astype(jnp.int32)
    every = lax.all_gather(frame_ids, "tm")
    sender = total(every[None] == tm * frames + slots[:, None, None], spots[None, :, None], (1, 2))
    senders = total(sender[:, None] == sources[None, :], spots[None, :], 1)
    return order, valid, rank, present, senders


def connect_kernel(
    sender_ref, my_ref, arrived_ref, weight_ref, gain_ref, stream_ref, normed_ref, rows, wide
):
    parts, _, tokens, _ = arrived_ref.shape
    width, columns = weight_ref.shape[1:]
    part_width = width // parts
    block_frames = rows.shape[0] // tokens
    for spot in range(block_frames):
        sender = sender_ref[pl.program_id(0) * block_frames + spot]
        for part in range(parts):
            rows[
                spot * tokens : (spot + 1) * tokens, part * part_width : (part + 1) * part_width
            ] = arrived_ref[part, sender, :, :part_width]
    squares = 0.0
    for part in range(parts):
        piece = jnp.dot(rows[...], weight_ref[part], preferred_element_type=f32).astype(bf16)

        @pl.when(my_ref[0] == part)
        def _():
            stream_ref[...] = piece

        piece = piece.astype(f32)
        wide[:, part * columns : (part + 1) * columns] = piece
        squares = squares + jnp.sum(piece * piece, axis=-1, keepdims=True)
    scale = lax.rsqrt(squares / (parts * columns) + 1e-05)
    normed_ref[...] = (wide[...] * scale * gain_ref[...]).astype(bf16)


def connect(arrived, senders, my, weights, norm_gain):
    parts, shards, tokens, padded = arrived.shape
    width, columns = weights.shape[1:]
    frames = senders.shape[0]
    block = math.gcd(frames, 4)
    return pl.pallas_call(
        connect_kernel,
        out_shape=(
            jax.ShapeDtypeStruct((frames * tokens, columns), bf16),
            jax.ShapeDtypeStruct((frames * tokens, parts * columns), bf16),
        ),
        grid_spec=pltpu.PrefetchScalarGridSpec(
            num_scalar_prefetch=2,
            grid=(frames // block,),
            in_specs=[
                pl.BlockSpec((parts, shards, tokens, padded), lambda i, *_: (0, 0, 0, 0)),
                pl.BlockSpec((parts, width, columns), lambda i, *_: (0, 0, 0)),
                pl.BlockSpec((1, parts * columns), lambda i, *_: (0, 0)),
            ],
            out_specs=(
                pl.BlockSpec((block * tokens, columns), lambda i, *_: (i, 0)),
                pl.BlockSpec((block * tokens, parts * columns), lambda i, *_: (i, 0)),
            ),
            scratch_shapes=[
                VMEM((block * tokens, width), bf16),
                VMEM((block * tokens, parts * columns), f32),
            ],
        ),
        name="connect",
    )(senders, my, arrived, weights, norm_gain.reshape(1, -1))


def paired(columns, pair, rows):
    lane = lax.broadcasted_iota(jnp.int32, (rows, LANES), 1)
    return jnp.where(
        lane < HDIM, columns[:, 2 * pair : 2 * pair + 1], columns[:, 2 * pair + 1 : 2 * pair + 2]
    )


def final_state_kernel(inner_ref, write_ref, weight_ref, out_ref, scaled):
    length, features = inner_ref.shape
    weights = weight_ref[0]
    for pair in range(features // LANES):
        at = slice(pair * LANES, (pair + 1) * LANES)
        scaled[:, at] = (inner_ref[:, at].astype(f32) * paired(weights, pair, length)).astype(bf16)
    sideways = lax.dot_general(
        write_ref[...], scaled[...], CONTRACT_FIRST, preferred_element_type=f32
    )
    out_ref[...] = sideways.T.astype(bf16)


def final_state(inner, write, weights):
    length = inner.shape[0]
    groups = weights.shape[0]
    features = inner.shape[1] // groups
    return pl.pallas_call(
        final_state_kernel,
        out_shape=jax.ShapeDtypeStruct((groups * features, STATE), bf16),
        grid=(groups,),
        in_specs=[
            pl.BlockSpec((length, features), lambda g: (0, g)),
            pl.BlockSpec((length, STATE), lambda g: (0, g)),
            pl.BlockSpec((1, length, weights.shape[2]), lambda g: (g, 0, 0)),
        ],
        out_specs=pl.BlockSpec((features, STATE), lambda g: (g, 0)),
        scratch_shapes=[VMEM((length, features), bf16)],
        name="final_state",
    )(inner, write, weights)


def local_kernel(
    inner_ref, write_ref, read_ref, down_ref, across_ref, step_ref, skip_ref, out_ref, state, scaled
):
    length, features = inner_ref.shape

    @pl.when(pl.program_id(1) == 0)
    def _():
        state[...] = jnp.zeros_like(state)

    readers, writers = read_ref[...], write_ref[...]
    crossing = lax.dot_general(readers, writers, CONTRACT_LAST, preferred_element_type=f32)
    causal = lax.broadcasted_iota(jnp.int32, (length, length), 0) >= lax.broadcasted_iota(
        jnp.int32, (length, length), 1
    )
    crossing = jnp.where(causal, crossing, 0.0)
    down, across, steps = down_ref[0], across_ref[0], step_ref[0]
    grown = jnp.exp2(down)
    left = jnp.exp2(down[length - 1 :, :] - down)
    lane = lax.broadcasted_iota(jnp.int32, (length, LANES), 1)
    held = state[...]
    carried = jnp.dot(readers, held.astype(bf16), preferred_element_type=f32)
    for pair in range(features // LANES):
        at = slice(pair * LANES, (pair + 1) * LANES)
        inner = inner_ref[:, at].astype(f32)
        weighted = inner * paired(steps, pair, length)
        halves = []
        for head in (2 * pair, 2 * pair + 1):
            spans = jnp.minimum(down[:, head : head + 1] - across[head : head + 1, :], 0.0)
            halves.append((crossing * jnp.exp2(spans)).astype(bf16))
        stacked = jnp.concatenate(
            [jnp.where(lane < HDIM, weighted, 0.0), jnp.where(lane < HDIM, 0.0, weighted)], axis=0
        ).astype(bf16)
        within = jnp.dot(
            jnp.concatenate(halves, axis=1), stacked, preferred_element_type=f32
        )
        faded = paired(grown, pair, length)
        out_ref[:, at] = within + carried[:, at] * faded + skip_ref[:, at] * inner
        scaled[:, at] = (weighted * paired(left, pair, length)).astype(bf16)
        state[:, at] = held[:, at] * faded[length - 1 :, :]
    state[...] += lax.dot_general(
        writers, scaled[...], CONTRACT_FIRST, preferred_element_type=f32
    )


def local_outputs(inner, write, read, down, across, steps, skip):
    length = inner.shape[0]
    groups, _, per_group = down.shape
    features = inner.shape[1] // groups
    tall = pl.BlockSpec((1, CHUNK, per_group), lambda g, c: (g, c, 0))
    flat = pl.BlockSpec((1, per_group, CHUNK), lambda g, c: (g, 0, c))
    return pl.pallas_call(
        local_kernel,
        out_shape=jax.ShapeDtypeStruct(inner.shape, f32),
        grid=(groups, length // CHUNK),
        in_specs=[
            pl.BlockSpec((CHUNK, features), lambda g, c: (c, g)),
            pl.BlockSpec((CHUNK, STATE), lambda g, c: (c, g)),
            pl.BlockSpec((CHUNK, STATE), lambda g, c: (c, g)),
            tall,
            flat,
            tall,
            pl.BlockSpec((1, features), lambda g, c: (0, g)),
        ],
        out_specs=pl.BlockSpec((CHUNK, features), lambda g, c: (c, g)),
        scratch_shapes=[VMEM((STATE, features), f32), VMEM((CHUNK, features), bf16)],
        cost_estimate=pl.CostEstimate(
            flops=20_000_000_000, bytes_accessed=20_000_000, transcendentals=4_000_000
        ),
        name="local_outputs",
    )(inner, write, read, down, across, steps, skip)


def prefix_kernel(arrived_ref, decay_ref, out_ref):
    shards, rows, _ = out_ref.shape
    current = jnp.zeros(out_ref.shape[1:], f32)
    for shard in range(shards):
        out_ref[shard] = current.astype(bf16)
        current = decay_ref[shard] * current + arrived_ref[shard, :rows].astype(f32)


def incoming_state(state, row_log, shards):
    rows = state.shape[0] // shards
    room = 8 * LANES
    logs = row_log.reshape(shards, rows)
    high = logs.astype(bf16)
    low = (logs - high.astype(f32)).astype(bf16)
    widen = lambda part: jnp.pad(part, ((0, 0), (0, room - rows))).reshape(shards, 8, LANES)
    outgoing = jnp.concatenate(
        [state.reshape(shards, rows, STATE), widen(high), widen(low)], axis=1
    )
    arrived = lax.all_to_all(outgoing, "tm", split_axis=0, concat_axis=0, tiled=True)
    tail = arrived[:, rows:].astype(f32).reshape(shards, 2, room)[:, :, :rows]
    decay = jnp.exp(tail[:, 0] + tail[:, 1])[:, :, None]
    before = pl.pallas_call(
        prefix_kernel,
        out_shape=jax.ShapeDtypeStruct((shards, rows, STATE), bf16),
        in_specs=[pl.BlockSpec(memory_space=VMEM)] * 2,
        out_specs=pl.BlockSpec(memory_space=VMEM),
        name="prefix",
    )(arrived, decay)
    return lax.all_to_all(before, "tm", split_axis=0, concat_axis=0, tiled=True).reshape(
        shards * rows, STATE
    )


def finish_kernel(local_ref, read_ref, state_ref, grown_ref, gain_ref, out_ref, total):
    length, features = local_ref.shape
    grown = grown_ref[0]
    squares = 0.0
    carried = lax.dot_general(
        read_ref[...], state_ref[...], CONTRACT_LAST, preferred_element_type=f32
    )
    for pair in range(features // LANES):
        at = slice(pair * LANES, (pair + 1) * LANES)
        summed = local_ref[:, at] + carried[:, at] * paired(grown, pair, length)
        total[:, at] = summed
        squares = squares + jnp.sum(summed * summed, axis=-1, keepdims=True)
    scale = lax.rsqrt(squares / features + 1e-05)
    out_ref[...] = (total[...] * scale * gain_ref[...]).astype(bf16)


def finish(local, read, state, grown, out_gain):
    length = local.shape[0]
    groups, _, per_group = grown.shape
    features = local.shape[1] // groups
    block = 2 * CHUNK
    return pl.pallas_call(
        finish_kernel,
        out_shape=jax.ShapeDtypeStruct(local.shape, bf16),
        grid=(groups, length // block),
        in_specs=[
            pl.BlockSpec((block, features), lambda g, c: (c, g)),
            pl.BlockSpec((block, STATE), lambda g, c: (c, g)),
            pl.BlockSpec((features, STATE), lambda g, c: (g, 0)),
            pl.BlockSpec((1, block, per_group), lambda g, c: (g, c, 0)),
            pl.BlockSpec((1, features), lambda g, c: (0, g)),
        ],
        out_specs=pl.BlockSpec((block, features), lambda g, c: (c, g)),
        scratch_shapes=[VMEM((block, features), f32)],
        name="finish",
    )(local, read, state, grown, out_gain.reshape(1, -1))


def running(values):
    length = values.shape[1]
    lower = jnp.tril(jnp.ones((length, length), f32))
    return jnp.einsum("ts,csh->cth", lower, values, precision=lax.Precision.HIGHEST)


def on_device(
    patches,
    grid_rows,
    frame_ids,
    ln_gain,
    w_qkv,
    w_out,
    w_conn,
    norm_gain,
    w_x,
    w_b,
    w_c,
    w_dt,
    dt_bias,
    a_log,
    d_skip,
    out_gain,
):
    part_width = patches.shape[2]
    shards = lax.axis_size("tm")
    my = lax.axis_index("head").astype(jnp.int32).reshape(1)
    parts = lax.axis_size("head")
    all_conn = lax.all_gather(w_conn, "head")
    order, valid, rank, present, senders = routes(frame_ids, grid_rows, shards)
    arrived = vision(
        patches.swapaxes(1, 2),
        order,
        valid,
        rank,
        present,
        ln_gain.reshape(-1, part_width, 1),
        w_qkv.swapaxes(1, 2),
        w_out,
        parts,
        shards,
    )
    stream_rows, normed = connect(arrived, senders, my, all_conn, norm_gain)

    tokens = stream_rows.shape[0]
    heads = w_dt.shape[1]
    groups = w_b.shape[1] // STATE
    per_group = heads // groups
    chunks = tokens // CHUNK
    step_size = jax.nn.softplus(jnp.dot(normed, w_dt, preferred_element_type=f32) + dt_bias)
    log_decay = -jnp.exp(a_log) * step_size
    inner = jnp.dot(normed, w_x, preferred_element_type=f32).astype(bf16)
    write = jnp.dot(normed, w_b, preferred_element_type=f32).astype(bf16)
    read = jnp.dot(normed, w_c, preferred_element_type=f32).astype(bf16)

    cumul = running(log_decay.reshape(chunks, CHUNK, heads))
    ends = cumul[:, -1, :]
    offsets = running(ends[None])[0] - ends
    total_log = jnp.sum(ends, axis=0)
    from_start = (cumul + offsets[:, None, :]).reshape(tokens, heads)
    tall = lambda member: member.reshape(tokens, groups, per_group).transpose(1, 0, 2)
    flat = lambda member: member.reshape(tokens, groups, per_group).transpose(1, 2, 0)
    state = final_state(inner, write, tall(step_size * jnp.exp(total_log - from_start)))
    before = incoming_state(state, jnp.repeat(total_log, HDIM), shards)
    doubling = cumul * math.log2(math.e)
    local = local_outputs(
        inner,
        write,
        read,
        tall(doubling),
        flat(doubling),
        tall(step_size),
        jnp.repeat(d_skip, HDIM).reshape(1, -1),
    )
    return stream_rows, finish(local, read, before, tall(jnp.exp(from_start)), out_gain)


def solution(mesh):
    in_specs = (
        P("tm", None, "head"),
        P("tm"),
        P("tm"),
        P(),
        P(None, None, "head"),
        P("head", None),
        P(None, "head"),
        P(),
        P(None, "head"),
        P(None, "head"),
        P(None, "head"),
        P(None, "head"),
        P("head"),
        P("head"),
        P("head"),
        P("head"),
    )
    out_specs = (P("tm", "head"), P("tm", "head"))
    return jax.shard_map(
        on_device, mesh=mesh, in_specs=in_specs, out_specs=out_specs, check_vma=False
    )
```

```python
import math

import jax
import jax.numpy as jnp
from jax import lax
from jax.experimental import pallas as pl
from jax.experimental.pallas import tpu as pltpu
from jax.sharding import PartitionSpec as P

GRID = 16
POOL = 4
VHD = 72
HDIM = 64
STATE = 128
CHUNK = 128
LANES = 128

f32 = jnp.float32
bf16 = jnp.bfloat16
VMEM = pltpu.VMEM
MESH = pl.DeviceIdType.MESH
CONTRACT_LAST = (((1,), (1,)), ((), ()))
CONTRACT_FIRST = (((0,), (0,)), ((), ()))


def flipped(index, mask, count):
    result, bit = 0, 1
    while bit < count:
        result = result + bit * ((index // bit + mask // bit) % 2)
        bit *= 2
    return result


def partners(index, spot, count):
    if count & (count - 1):
        return (index + spot + 1) % count, (index + 2 * count - spot - 1) % count
    other = flipped(index, count - 1 - spot, count)
    return other, other


def vision_kernel(
    order_ref,
    valid_ref,
    rank_ref,
    label_ref,
    patches_ref,
    gain_ref,
    wqkv_ref,
    wout_ref,
    out_ref,
    full,
    normed,
    qkv,
    context,
    partial,
    partial_in,
    mine,
    pooled_frames,
    outbox,
    patch_send,
    patch_recv,
    partial_send,
    partial_recv,
    frame_send,
    frame_recv,
    forward_send,
    forward_recv,
):
    parts, frames, part_width, patch_count = full.shape
    shards = out_ref.shape[1]
    width = parts * part_width
    local_width = wqkv_ref.shape[1]
    heads = local_width // VHD
    tokens = patch_count // POOL
    batch = normed.shape[1] // patch_count
    factor = VHD ** (-0.5) * math.log2(math.e)
    tm, head = lax.axis_index("tm"), lax.axis_index("head")
    peers = [(head + step) % parts for step in range(1, parts)]
    sources = [(head + parts - step) % parts for step in range(1, parts)]

    def remote(source, target, send, recv, to):
        return pltpu.make_async_remote_copy(
            src_ref=source,
            dst_ref=target,
            send_sem=send,
            recv_sem=recv,
            device_id=to,
            device_id_type=MESH,
        )

    def patch_copy(step, rank, part):
        return remote(
            full.at[part, rank],
            full.at[part, rank],
            patch_send.at[step, rank],
            patch_recv.at[step, rank],
            (tm, peers[step]),
        )

    def partial_copy(step, rank):
        return remote(
            partial.at[rank, peers[step]],
            partial_in.at[rank, step],
            partial_send.at[step, rank],
            partial_recv.at[step, rank],
            (tm, peers[step]),
        )

    def frame_copy(spot):
        return remote(
            outbox.at[spot],
            out_ref.at[head, spot],
            frame_send.at[spot],
            frame_recv.at[spot],
            (partners(tm, spot, shards)[0], head),
        )

    def forward_copy(step, spot, part):
        return remote(
            out_ref.at[part, spot],
            out_ref.at[part, spot],
            forward_send.at[step, spot],
            forward_recv.at[step, spot],
            (tm, peers[step]),
        )

    barrier = pltpu.get_barrier_semaphore()
    for peer in peers:
        pl.semaphore_signal(barrier, inc=1, device_id=(tm, peer), device_id_type=MESH)

    def greet(spot, carry):
        pl.semaphore_signal(
            barrier,
            inc=1,
            device_id=(partners(tm, spot, shards)[1], head),
            device_id_type=MESH,
        )
        return carry

    lax.fori_loop(0, shards - 1, greet, 0)

    def stage(rank, carry):
        full[head, rank] = patches_ref[order_ref[rank]]
        return carry

    lax.fori_loop(0, frames, stage, 0)
    pl.semaphore_wait(barrier, parts - 1 + shards - 1)

    def share(rank, carry):
        for step in range(parts - 1):
            patch_copy(step, rank, head).start()
        return carry

    lax.fori_loop(0, frames, share, 0)

    def normalise(rank, columns):
        total = 0.0
        for part in range(parts):
            total = total + jnp.sum(full[part, rank].astype(f32), axis=0, keepdims=True)
        centre = total / width
        spread = 0.0
        for part in range(parts):
            moved = full[part, rank].astype(f32) - centre
            spread = spread + jnp.sum(moved * moved, axis=0, keepdims=True)
        scale = lax.rsqrt(spread / width + 1e-06)
        for part in range(parts):
            normed[part * part_width : (part + 1) * part_width, columns] = (
                (full[part, rank].astype(f32) - centre) * scale * gain_ref[part]
            ).astype(bf16)

    spot_row = lax.broadcasted_iota(jnp.int32, (8, patch_count), 0)
    spot_key = lax.broadcasted_iota(jnp.int32, (8, patch_count), 1)
    ones_row = jnp.where(spot_row == 0, 1.0, 0.0).astype(f32)

    def extended(member, head_id, columns, extra):
        rows = slice(head_id * VHD, (head_id + 1) * VHD)
        return jnp.concatenate([qkv[member, rows, columns], extra], axis=0).astype(bf16)

    def score(head_id, columns, key_row):
        return lax.dot_general(
            extended(1, head_id, columns, key_row),
            extended(0, head_id, columns, ones_row),
            CONTRACT_FIRST,
            preferred_element_type=f32,
        )

    def mix(head_id, columns, scores):
        powered = jnp.exp2((scores - jnp.max(scores, axis=0, keepdims=True)) * factor)
        mixed = jnp.dot(
            extended(2, head_id, columns, ones_row),
            powered.astype(bf16),
            preferred_element_type=f32,
        )
        context[head_id * VHD : (head_id + 1) * VHD, columns] = mixed[:VHD] * (
            1.0 / mixed[VHD : VHD + 1]
        )

    pool_row = lax.broadcasted_iota(jnp.int32, (tokens, patch_count), 0)
    pool_column = lax.broadcasted_iota(jnp.int32, (tokens, patch_count), 1)
    pooling = jnp.where(pool_column // POOL == pool_row, 1.0 / POOL, 0.0).astype(bf16)
    token_spot = lax.broadcasted_iota(jnp.int32, (tokens, part_width), 0) * POOL
    spans = [slice(b * patch_count, (b + 1) * patch_count) for b in range(batch)]

    def post(spot):
        outbox[spot, :, :part_width] = pooled_frames[rank_ref[spot]]
        outbox[spot, :, part_width:] = jnp.full(
            (tokens, outbox.shape[2] - part_width), label_ref[spot].astype(f32)
        ).astype(bf16)

    def settle(rank):
        for step in range(parts - 1):
            partial_copy(step, rank).wait_recv()
        total = mine[rank]
        for step in range(parts - 1):
            total = total + partial_in[rank, step].astype(f32)
        pooled_frames[rank] = jnp.where(token_spot < valid_ref[rank], total, 0.0).astype(bf16)
        post(rank)
        frame_copy(rank).start()

    def forward(spot):
        frame_copy(spot).wait_recv()
        for step in range(parts - 1):
            forward_copy(step, spot, head).start()

    def body(turn, carry):
        ranks = [turn * batch + b for b in range(batch)]
        for rank, span in zip(ranks, spans):
            for step in range(parts - 1):
                patch_copy(step, rank, sources[step]).wait_recv()
            normalise(rank, span)
        for member in range(3):
            qkv[member] = jnp.dot(wqkv_ref[member], normed[...], preferred_element_type=f32)

        @pl.when(turn >= 1)
        def _():
            for b in range(batch):
                settle((turn - 1) * batch + b)

        @pl.when(turn >= 3)
        def _():
            for b in range(batch):
                forward((turn - 3) * batch + b)

        key_rows = [
            jnp.where((spot_row == 0) & (spot_key >= valid_ref[rank]), -1e30, 0.0).astype(f32)
            for rank in ranks
        ]
        todo = [(head_id, b) for head_id in range(heads) for b in range(batch)]
        ahead = 2
        ready = [score(h, spans[b], key_rows[b]) for h, b in todo[:ahead]]
        for at, (h, b) in enumerate(todo):
            if at + ahead < len(todo):
                later, which = todo[at + ahead]
                ready.append(score(later, spans[which], key_rows[which]))
            mix(h, spans[b], ready[at])
        pooled = jnp.concatenate(
            [
                lax.dot_general(
                    pooling,
                    context[:, span].astype(bf16),
                    CONTRACT_LAST,
                    preferred_element_type=f32,
                ).astype(bf16)
                for span in spans
            ],
            axis=0,
        )
        attended = jnp.dot(pooled, wout_ref[...], preferred_element_type=f32)
        for b, rank in enumerate(ranks):
            own = lax.dot_general(
                pooling, full[head, rank], CONTRACT_LAST, preferred_element_type=f32
            )
            for part in range(parts):
                block = attended[
                    b * tokens : (b + 1) * tokens, part * part_width : (part + 1) * part_width
                ]
                partial[rank, part] = block.astype(bf16)
                own = own + jnp.where(head == part, block, 0.0)
            mine[rank] = own
            for step in range(parts - 1):
                partial_copy(step, rank).start()
        return carry

    turns = frames // batch
    lax.fori_loop(0, turns, body, 0)
    for rank in range(frames - batch, frames):
        settle(rank)
    for spot in range(frames, shards):
        post(spot)
        if spot < shards - 1:
            frame_copy(spot).start()
    out_ref[head, shards - 1] = outbox[shards - 1]
    for step in range(parts - 1):
        forward_copy(step, shards - 1, head).start()

    def late_forward(spot, carry):
        forward(spot)
        return carry

    lax.fori_loop(max(turns - 3, 0) * batch, shards - 1, late_forward, 0)

    def drain_ranks(rank, carry):
        for step in range(parts - 1):
            patch_copy(step, rank, head).wait_send()
            partial_copy(step, rank).wait_send()
        return carry

    lax.fori_loop(0, frames, drain_ranks, 0)

    def drain_frames(spot, carry):
        frame_copy(spot).wait_send()
        return carry

    lax.fori_loop(0, shards - 1, drain_frames, 0)

    def drain_forwards(spot, carry):
        for step in range(parts - 1):
            forward_copy(step, spot, sources[step]).wait_recv()
            forward_copy(step, spot, head).wait_send()
        return carry

    lax.fori_loop(0, shards, drain_forwards, 0)


def vision(patches, order, valid, rank, label, gain, w_qkv, w_out, parts, shards):
    frames, part_width, patch_count = patches.shape
    width = parts * part_width
    local_width = w_qkv.shape[1]
    tokens = patch_count // POOL
    batch = math.gcd(frames, 2)
    in_smem = pl.BlockSpec(memory_space=pltpu.SMEM)
    in_vmem = pl.BlockSpec(memory_space=VMEM)
    peers = parts - 1
    padded = (part_width // LANES + 1) * LANES
    dma = pltpu.SemaphoreType.DMA
    return pl.pallas_call(
        vision_kernel,
        out_shape=jax.ShapeDtypeStruct((parts, shards, tokens, padded), bf16),
        in_specs=[in_smem] * 4 + [in_vmem] * 4,
        out_specs=in_vmem,
        scratch_shapes=[
            VMEM((parts, frames, part_width, patch_count), bf16),
            VMEM((width, batch * patch_count), bf16),
            VMEM((3, local_width, batch * patch_count), f32),
            VMEM((local_width, batch * patch_count), f32),
            VMEM((frames, parts, tokens, part_width), bf16),
            VMEM((frames, peers, tokens, part_width), bf16),
            VMEM((frames, tokens, part_width), f32),
            VMEM((frames, tokens, part_width), bf16),
            VMEM((shards, tokens, padded), bf16),
            dma((peers, frames)),
            dma((peers, frames)),
            dma((peers, frames)),
            dma((peers, frames)),
            dma((shards,)),
            dma((shards,)),
            dma((peers, shards)),
            dma((peers, shards)),
        ],
        compiler_params=pltpu.CompilerParams(
            collective_id=0, has_side_effects=True, vmem_limit_bytes=56 << 20
        ),
        cost_estimate=pl.CostEstimate(
            flops=frames * patch_count * width * local_width * 10,
            bytes_accessed=12_000_000,
            transcendentals=4_000_000,
        ),
        name="vision",
    )(order, valid, rank, label, patches, gain, w_qkv, w_out)


def routes(frame_ids, grid_rows, shards):
    frames = frame_ids.shape[0]
    tm = lax.axis_index("tm").astype(jnp.int32)
    spots = jnp.arange(shards, dtype=jnp.int32)
    targets = partners(tm, spots, shards)[0]
    slots = jnp.arange(frames, dtype=jnp.int32)
    total = lambda chosen, member, axis: jnp.sum(
        jnp.where(chosen, member, 0), axis=axis
    ).astype(jnp.int32)
    goes = (frame_ids // frames)[:, None] == targets[None, :]
    spot_of = total(goes, spots[None, :], 1)
    rank_of = jnp.sum(spot_of[None, :] < spot_of[:, None], axis=1).astype(jnp.int32)
    holds = rank_of[None, :] == slots[:, None]
    order = total(holds, slots[None, :], 1)
    valid = total(holds, (grid_rows * GRID)[None, :], 1)
    rank = total(goes, rank_of[:, None], 0)
    label = total(goes, (frame_ids % frames + 1)[:, None], 0)
    return order, valid, rank, label


def spread(rows, width, copies):
    heads = rows // copies
    row = lax.broadcasted_iota(jnp.int32, (rows, heads * width), 0) % heads
    block = lax.broadcasted_iota(jnp.int32, (rows, heads * width), 1) // width
    return jnp.where(row == block, 1.0, 0.0).astype(bf16)


def split(values, copies):
    terms = []
    for _ in range(copies):
        terms.append(values.astype(bf16).astype(f32))
        values = values - terms[-1]
    return jnp.concatenate(terms, axis=0).astype(bf16)


def column(row):
    count = row.shape[1]
    same = lax.broadcasted_iota(jnp.int32, (count, count), 0) == lax.broadcasted_iota(
        jnp.int32, (count, count), 1
    )
    return jnp.sum(jnp.where(same, row, 0.0), axis=1, keepdims=True)


def mix_kernel(
    sender_ref,
    arrived_ref,
    norm_gain_ref,
    wdt_ref,
    bias_ref,
    alog_ref,
    skip_ref,
    out_gain_ref,
    conn_hbm,
    wx_hbm,
    wb_hbm,
    wc_hbm,
    stream_hbm,
    out_hbm,
    conn,
    ring,
    rows,
    normed,
    squares,
    inner,
    write,
    read,
    result,
    local_out,
    staged,
    down,
    across,
    state,
    state_out,
    state_in,
    before,
    incoming,
    decay_out,
    decay_in,
    conn_sem,
    ring_sem,
    stream_sem,
    out_sem,
    decay_send,
    decay_recv,
    first_send,
    first_recv,
    second_send,
    second_recv,
):
    parts, _, frame_tokens, _ = arrived_ref.shape
    tokens, full_width = normed.shape
    conn_count, width, conn_width = conn.shape
    part_width = width // parts
    per_part = conn_count // parts
    frames = tokens // frame_tokens
    heads = wdt_ref.shape[0]
    groups = write.shape[1] // STATE
    per_group = heads // groups
    features = per_group * HDIM
    chunks = tokens // CHUNK
    block = 2 * CHUNK
    batches, shards, slice_rows, _ = state_in.shape
    batch_groups = groups // batches
    piece = features // shards
    unit = min(piece, HDIM)
    pieces = piece // unit
    tm, head = lax.axis_index("tm"), lax.axis_index("head")
    log2e = math.log2(math.e)

    def remote(source, target, send, recv, spot):
        return pltpu.make_async_remote_copy(
            src_ref=source,
            dst_ref=target,
            send_sem=send,
            recv_sem=recv,
            device_id=(partners(tm, spot, shards)[0], head),
            device_id_type=MESH,
        )

    def target_of(spot):
        return partners(tm, spot, shards)[0]

    def decay_copy(spot):
        return remote(
            decay_out.at[target_of(spot)],
            decay_in.at[tm],
            decay_send.at[spot],
            decay_recv.at[spot],
            spot,
        )

    def first_copy(batch, spot):
        return remote(
            state_out.at[batch, target_of(spot)],
            state_in.at[batch, tm],
            first_send.at[batch, spot],
            first_recv.at[batch, spot],
            spot,
        )

    def second_copy(batch, spot):
        return remote(
            before.at[batch, target_of(spot)],
            incoming.at[batch, tm],
            second_send.at[batch, spot],
            second_recv.at[batch, spot],
            spot,
        )

    def over_spots(act):
        def step(spot, carry):
            act(spot)
            return carry

        lax.fori_loop(0, shards - 1, step, 0)

    barrier = pltpu.get_barrier_semaphore()
    over_spots(
        lambda spot: pl.semaphore_signal(
            barrier,
            inc=1,
            device_id=(partners(tm, spot, shards)[1], head),
            device_id_type=MESH,
        )
    )

    def conn_load(at):
        return pltpu.make_async_copy(
            conn_hbm.at[
                at // per_part,
                :,
                pl.ds(pl.multiple_of((at % per_part) * conn_width, conn_width), conn_width),
            ],
            conn.at[at],
            conn_sem.at[at],
        )

    def weight_load(which):
        slot = which % ring.shape[0]
        if which == 0 or which == groups + 1:
            source = wb_hbm if which == 0 else wc_hbm
            target = ring.at[slot, :, : groups * STATE]
        else:
            source = wx_hbm.at[:, (which - 1) * features : which * features]
            target = ring.at[slot]
        return pltpu.make_async_copy(source, target, ring_sem.at[slot])

    def conn_start(at, carry):
        conn_load(at).start()
        return carry

    lax.fori_loop(0, conn_count, conn_start, 0)
    for which in range(ring.shape[0]):
        weight_load(which).start()

    def gather(frame, carry):
        place = pl.ds(pl.multiple_of(frame * frame_tokens, frame_tokens), frame_tokens)
        for part in range(parts):
            rows[place, part * part_width : (part + 1) * part_width] = arrived_ref[
                part, sender_ref[frame], :, :part_width
            ]
        return carry

    lax.fori_loop(0, frames, gather, 0)
    squares[...] = jnp.zeros_like(squares)

    def connect(at, carry):
        conn_load(at).wait()
        columns = pl.ds(pl.multiple_of(at * conn_width, conn_width), conn_width)
        mine = pl.ds(
            pl.multiple_of((at % per_part) * conn_width, conn_width), conn_width
        )
        for first in range(0, tokens, block):
            span = slice(first, first + block)
            made = jnp.dot(rows[span, :], conn[at], preferred_element_type=f32).astype(bf16)
            normed[span, columns] = made

            @pl.when(at // per_part == head)
            def _():
                result[span, mine] = made

            made = made.astype(f32)
            made = made * made
            squares[span, :] += sum(
                made[:, lane : lane + LANES] for lane in range(0, conn_width, LANES)
            )
        return carry

    lax.fori_loop(0, conn_count, connect, 0)
    stream_copy = pltpu.make_async_copy(result, stream_hbm, stream_sem)
    stream_copy.start()

    def normalise(at, carry):
        span = pl.ds(pl.multiple_of(at * 64, 64), 64)
        total = jnp.sum(squares[span, :], axis=1, keepdims=True)
        scale = lax.rsqrt(total / full_width + 1e-05)
        normed[span, :] = (normed[span, :].astype(f32) * scale * norm_gain_ref[...]).astype(bf16)
        return carry

    lax.fori_loop(0, tokens // 64, normalise, 0)

    raw = lax.dot_general(wdt_ref[...], normed[...], CONTRACT_LAST, preferred_element_type=f32)
    raw = raw + column(bias_ref[...])
    step_size = jnp.maximum(raw, 0.0) + jnp.log1p(jnp.exp(-jnp.abs(raw)))
    rate = -jnp.exp(column(alog_ref[...])) * log2e
    log_decay = step_size * rate
    log_step = jnp.log(step_size) * log2e
    upper = jnp.where(
        lax.broadcasted_iota(jnp.int32, (CHUNK, CHUNK), 0)
        <= lax.broadcasted_iota(jnp.int32, (CHUNK, CHUNK), 1),
        1.0,
        0.0,
    ).astype(f32)
    ends = []
    for chunk in range(chunks):
        span = slice(chunk * CHUNK, (chunk + 1) * CHUNK)
        sums = jnp.dot(
            log_decay[:, span],
            upper,
            preferred_element_type=f32,
            precision=lax.Precision.HIGHEST,
        )
        down[chunk] = sums
        across[chunk] = sums - log_step[:, span]
        ends.append(sums[:, CHUNK - 1 :])
    total = jnp.zeros_like(ends[0])
    for chunk in range(chunks):
        staged[chunk] = jnp.broadcast_to(total, (heads, LANES))
        total = total + ends[chunk]
    staged[chunks] = jnp.broadcast_to(jnp.exp2(total), (heads, LANES))
    decay_out[...] = jnp.zeros_like(decay_out)
    for target in range(shards):
        for group in range(groups):
            for part in range(pieces):
                at = group * per_group + (target * piece + part * unit) // HDIM
                row = group * pieces + part
                decay_out[target, row : row + 1] = staged[chunks, at : at + 1]
    decay_in[tm] = decay_out[tm]
    pl.semaphore_wait(barrier, shards - 1)
    over_spots(lambda spot: decay_copy(spot).start())

    def project(which, target, first_column, count):
        slot = which % ring.shape[0]
        weight_load(which).wait()

        def part(at, carry):
            span = pl.ds(pl.multiple_of(at * block, block), block)
            target[span, first_column : first_column + count] = jnp.dot(
                normed[span, :], ring[slot, :, :count], preferred_element_type=f32
            ).astype(bf16)
            return carry

        lax.fori_loop(0, tokens // block, part, 0)
        if which + ring.shape[0] <= groups + 1:
            weight_load(which + ring.shape[0]).start()

    per_buffer = width // STATE

    def saved(group, chunk):
        at = group * chunks + chunk
        return at // per_buffer, pl.ds(
            pl.multiple_of((at % per_buffer) * STATE, STATE), STATE
        )

    spread_narrow = spread(2 * per_group, HDIM, 2)
    spread_wide = spread(3 * per_group, CHUNK, 3)
    head_row = lax.broadcasted_iota(jnp.int32, (per_group, features), 0)
    head_lane = lax.broadcasted_iota(jnp.int32, (per_group, features), 1) // HDIM

    def widen(values):
        return lax.dot_general(
            split(values, 2), spread_narrow, CONTRACT_FIRST, preferred_element_type=f32
        )

    def widen_row(values):
        return jnp.sum(jnp.where(head_row == head_lane, values, 0.0), axis=0, keepdims=True)

    def at_group(group, chunk):
        own = slice(group * per_group, (group + 1) * per_group)
        return (
            pl.ds(pl.multiple_of(chunk * CHUNK, CHUNK), CHUNK),
            slice(group * features, (group + 1) * features),
            slice(group * STATE, (group + 1) * STATE),
            own,
        )

    def states(group):
        state[...] = jnp.zeros_like(state)

        def step(chunk, carry):
            span, lanes, keys, own = at_group(group, chunk)
            sums, shifted = down[chunk, own], across[chunk, own]
            end = sums[:, CHUNK - 1 :]
            buffer, place = saved(group, chunk)
            held = state[...]
            conn[buffer, place, :features] = held.astype(bf16)
            scaled = (inner[span, lanes].astype(f32) * widen(jnp.exp2(end - shifted))).astype(bf16)
            state[...] = held * widen_row(jnp.exp2(end)) + lax.dot_general(
                write[span, keys], scaled, CONTRACT_FIRST, preferred_element_type=f32
            )
            return carry

        lax.fori_loop(0, chunks, step, 0)
        batch, inside = group // batch_groups, group % batch_groups
        sideways = state[...].T.astype(bf16)
        for target in range(shards):
            state_out[batch, target, inside * piece : (inside + 1) * piece] = sideways[
                target * piece : (target + 1) * piece
            ]

    def send_first(batch):
        state_in[batch, tm] = state_out[batch, tm]
        over_spots(lambda spot: first_copy(batch, spot).start())

    def send_second(batch):
        if batch == 0:
            over_spots(lambda spot: decay_copy(spot).wait_recv())
        over_spots(lambda spot: first_copy(batch, spot).wait_recv())
        for inside in range(batch_groups):
            group = batch * batch_groups + inside
            for part in range(pieces):
                span = slice(inside * piece + part * unit, inside * piece + (part + 1) * unit)
                row = group * pieces + part
                current = jnp.zeros((unit, STATE), f32)
                for shard in range(shards):
                    before[batch, shard, span] = current.astype(bf16)
                    current = decay_in[shard, row : row + 1] * current + state_in[
                        batch, shard, span
                    ].astype(f32)
        incoming[batch, tm] = before[batch, tm]
        over_spots(lambda spot: second_copy(batch, spot).start())

    causal = lax.broadcasted_iota(jnp.int32, (CHUNK, CHUNK), 0) >= lax.broadcasted_iota(
        jnp.int32, (CHUNK, CHUNK), 1
    )
    lane = lax.broadcasted_iota(jnp.int32, (CHUNK, LANES), 1)
    skip_column = column(skip_ref[...])

    def local(group):
        skip = widen_row(skip_column[group * per_group : (group + 1) * per_group])

        def step(chunk, carry):
            span, lanes, keys, own = at_group(group, chunk)
            sums, shifted = down[chunk, own], across[chunk, own]
            readers = read[span, keys]
            crossing = lax.dot_general(
                readers, write[span, keys], CONTRACT_LAST, preferred_element_type=f32
            )
            crossing = jnp.where(causal, crossing, 0.0)
            downs = lax.dot_general(
                split(sums, 3), spread_wide, CONTRACT_FIRST, preferred_element_type=f32
            )
            grown = widen(jnp.exp2(sums))
            buffer, place = saved(group, chunk)
            carried = jnp.dot(
                readers, conn[buffer, place, :features], preferred_element_type=f32
            )
            for pair in range(features // LANES):
                at = slice(pair * LANES, (pair + 1) * LANES)
                here = slice(lanes.start + pair * LANES, lanes.start + (pair + 1) * LANES)
                values = inner[span, here]
                halves = []
                for one in (2 * pair, 2 * pair + 1):
                    spans = downs[:, one * CHUNK : (one + 1) * CHUNK] - shifted[one : one + 1]
                    halves.append((crossing * jnp.exp2(jnp.minimum(spans, 100.0))).astype(bf16))
                wide = values.astype(f32)
                stacked = jnp.concatenate(
                    [jnp.where(lane < HDIM, wide, 0.0), jnp.where(lane < HDIM, 0.0, wide)], axis=0
                ).astype(bf16)
                within = jnp.dot(
                    jnp.concatenate(halves, axis=1), stacked, preferred_element_type=f32
                )
                local_out[span, here] = within + carried[:, at] * grown[:, at] + skip[:, at] * wide
            return carry

        lax.fori_loop(0, chunks, step, 0)

    def finish(group):
        batch, inside = group // batch_groups, group % batch_groups
        held = jnp.concatenate(
            [
                incoming[batch, shard, inside * piece : (inside + 1) * piece]
                for shard in range(shards)
            ],
            axis=0,
        )

        def step(chunk, carry):
            span, lanes, keys, own = at_group(group, chunk)
            grown = widen(jnp.exp2(down[chunk, own] + staged[chunk, own]))
            carried = lax.dot_general(
                read[span, keys], held, CONTRACT_LAST, preferred_element_type=f32
            )
            summed = local_out[span, lanes] + carried * grown
            mean = jnp.sum(summed * summed, axis=1, keepdims=True) / features
            result[span, lanes] = (
                summed * lax.rsqrt(mean + 1e-05) * out_gain_ref[:, lanes]
            ).astype(bf16)
            return carry

        lax.fori_loop(0, chunks, step, 0)

    def out_copy(group):
        lanes = slice(group * features, (group + 1) * features)
        return pltpu.make_async_copy(
            result.at[:, lanes], out_hbm.at[:, lanes], out_sem.at[group]
        )

    project(0, write, 0, groups * STATE)
    for group in range(groups):
        project(group + 1, inner, group * features, features)
        states(group)
        if (group + 1) % batch_groups == 0:
            send_first(group // batch_groups)
    if batches > 1:
        send_second(0)
    project(groups + 1, read, 0, groups * STATE)
    for group in range(groups):
        if group == groups // 2:
            send_second(batches - 1)
        local(group)
    stream_copy.wait()
    for group in range(groups):
        if group % batch_groups == 0:
            batch = group // batch_groups
            over_spots(lambda spot: second_copy(batch, spot).wait_recv())
        finish(group)
        out_copy(group).start()
    over_spots(lambda spot: decay_copy(spot).wait_send())
    for batch in range(batches):
        over_spots(lambda spot: first_copy(batch, spot).wait_send())
        over_spots(lambda spot: second_copy(batch, spot).wait_send())
    for group in range(groups):
        out_copy(group).wait()


def mix(arrived, senders, weights, norm_gain, w_x, w_b, w_c, w_dt, dt_bias, a_log, d_skip, out_gain):
    parts, shards, frame_tokens, _ = arrived.shape
    _, width, columns = weights.shape
    tokens = senders.shape[0] * frame_tokens
    full_width = parts * columns
    heads = w_dt.shape[1]
    groups = w_b.shape[1] // STATE
    features = heads // groups * HDIM
    chunks = tokens // CHUNK
    conn_width = math.gcd(columns, features)
    conn_count = full_width // conn_width
    batches = math.gcd(groups, 2)
    piece = features // shards
    slice_rows = groups // batches * piece
    pieces = max(piece // HDIM, 1)
    decay_rows = -(-groups * pieces // 8) * 8
    in_smem = pl.BlockSpec(memory_space=pltpu.SMEM)
    in_vmem = pl.BlockSpec(memory_space=VMEM)
    in_hbm = pl.BlockSpec(memory_space=pl.ANY)
    dma = pltpu.SemaphoreType.DMA
    shape = jax.ShapeDtypeStruct((tokens, heads * HDIM), bf16)
    row = lambda member: member.reshape(1, -1)
    return pl.pallas_call(
        mix_kernel,
        out_shape=(jax.ShapeDtypeStruct((tokens, columns), bf16), shape),
        in_specs=[in_smem] + [in_vmem] * 7 + [in_hbm] * 4,
        out_specs=(in_hbm, in_hbm),
        scratch_shapes=[
            VMEM((conn_count, width, conn_width), bf16),
            VMEM((min(3, groups + 2), w_x.shape[0], features), bf16),
            VMEM((tokens, width), bf16),
            VMEM((tokens, full_width), bf16),
            VMEM((tokens, LANES), f32),
            VMEM((tokens, heads * HDIM), bf16),
            VMEM((tokens, groups * STATE), bf16),
            VMEM((tokens, groups * STATE), bf16),
            VMEM((tokens, columns), bf16),
            VMEM((tokens, heads * HDIM), f32),
            VMEM((chunks + 1, heads, LANES), f32),
            VMEM((chunks, heads, CHUNK), f32),
            VMEM((chunks, heads, CHUNK), f32),
            VMEM((STATE, features), f32),
            VMEM((batches, shards, slice_rows, STATE), bf16),
            VMEM((batches, shards, slice_rows, STATE), bf16),
            VMEM((batches, shards, slice_rows, STATE), bf16),
            VMEM((batches, shards, slice_rows, STATE), bf16),
            VMEM((shards, decay_rows, LANES), f32),
            VMEM((shards, decay_rows, LANES), f32),
            dma((conn_count,)),
            dma((min(3, groups + 2),)),
            dma(()),
            dma((groups,)),
            dma((shards,)),
            dma((shards,)),
            dma((batches, shards)),
            dma((batches, shards)),
            dma((batches, shards)),
            dma((batches, shards)),
        ],
        compiler_params=pltpu.CompilerParams(
            collective_id=1, has_side_effects=True, vmem_limit_bytes=62 << 20
        ),
        name="mix",
    )(
        senders,
        arrived,
        row(norm_gain),
        w_dt.T,
        row(dt_bias),
        row(a_log),
        row(d_skip),
        row(out_gain),
        weights,
        w_x,
        w_b,
        w_c,
    )


def on_device(
    patches,
    grid_rows,
    frame_ids,
    ln_gain,
    w_qkv,
    w_out,
    w_conn,
    norm_gain,
    w_x,
    w_b,
    w_c,
    w_dt,
    dt_bias,
    a_log,
    d_skip,
    out_gain,
):
    part_width = patches.shape[2]
    shards = lax.axis_size("tm")
    my = lax.axis_index("head").astype(jnp.int32).reshape(1)
    parts = lax.axis_size("head")
    all_conn = lax.all_gather(w_conn, "head")
    order, valid, rank, label = routes(frame_ids, grid_rows, shards)
    arrived = vision(
        patches.swapaxes(1, 2),
        order,
        valid,
        rank,
        label,
        ln_gain.reshape(-1, part_width, 1),
        w_qkv.swapaxes(1, 2),
        w_out,
        parts,
        shards,
    )
    labels = arrived[0, :, 0, part_width].astype(jnp.int32)
    frames = frame_ids.shape[0]
    senders = jnp.sum(
        jnp.where(
            labels[None, :] == jnp.arange(1, frames + 1)[:, None],
            jnp.arange(shards, dtype=jnp.int32)[None, :],
            0,
        ),
        axis=1,
    ).astype(jnp.int32)
    return mix(
        arrived,
        senders,
        all_conn,
        norm_gain,
        w_x,
        w_b,
        w_c,
        w_dt,
        dt_bias,
        a_log,
        d_skip,
        out_gain,
    )


def solution(mesh):
    in_specs = (
        P("tm", None, "head"),
        P("tm"),
        P("tm"),
        P(),
        P(None, None, "head"),
        P("head", None),
        P(None, "head"),
        P(),
        P(None, "head"),
        P(None, "head"),
        P(None, "head"),
        P(None, "head"),
        P("head"),
        P("head"),
        P("head"),
        P("head"),
    )
    out_specs = (P("tm", "head"), P("tm", "head"))
    return jax.shard_map(
        on_device, mesh=mesh, in_specs=in_specs, out_specs=out_specs, check_vma=False
    )
```

```python
import math

import jax
import jax.numpy as jnp
from jax import lax
from jax.experimental import pallas as pl
from jax.experimental.pallas import tpu as pltpu
from jax.sharding import PartitionSpec as P

GRID = 16
POOL = 4
VHD = 72
HDIM = 64
STATE = 128
CHUNK = 128
LANES = 128

f32 = jnp.float32
bf16 = jnp.bfloat16
VMEM = pltpu.VMEM
MESH = pl.DeviceIdType.MESH
CONTRACT_LAST = (((1,), (1,)), ((), ()))
CONTRACT_FIRST = (((0,), (0,)), ((), ()))


def flipped(index, mask, count):
    result, bit = 0, 1
    while bit < count:
        result = result + bit * ((index // bit + mask // bit) % 2)
        bit *= 2
    return result


def partners(index, spot, count):
    if count & (count - 1):
        return (index + spot + 1) % count, (index + 2 * count - spot - 1) % count
    other = flipped(index, count - 1 - spot, count)
    return other, other


def vision_kernel(
    order_ref,
    valid_ref,
    rank_ref,
    label_ref,
    patches_ref,
    gain_ref,
    wqkv_ref,
    wout_ref,
    out_ref,
    full,
    gain,
    normed,
    qkv,
    context,
    partial,
    partial_in,
    mine,
    pooled_frames,
    outbox,
    patch_send,
    patch_recv,
    partial_send,
    partial_recv,
    frame_send,
    frame_recv,
    forward_send,
    forward_recv,
):
    parts, frames, part_width, patch_count = full.shape
    shards = out_ref.shape[1]
    width = parts * part_width
    local_width = wqkv_ref.shape[1]
    heads = local_width // VHD
    tokens = patch_count // POOL
    batch = normed.shape[1] // patch_count
    factor = VHD ** (-0.5) * math.log2(math.e)
    tm, head = lax.axis_index("tm"), lax.axis_index("head")
    peers = [(head + step) % parts for step in range(1, parts)]
    sources = [(head + parts - step) % parts for step in range(1, parts)]

    def remote(source, target, send, recv, to):
        return pltpu.make_async_remote_copy(
            src_ref=source,
            dst_ref=target,
            send_sem=send,
            recv_sem=recv,
            device_id=to,
            device_id_type=MESH,
        )

    def patch_copy(step, rank, part):
        return remote(
            full.at[part, rank],
            full.at[part, rank],
            patch_send.at[step, rank],
            patch_recv.at[step, rank],
            (tm, peers[step]),
        )

    def partial_copy(step, rank):
        return remote(
            partial.at[rank, peers[step]],
            partial_in.at[rank, step],
            partial_send.at[step, rank],
            partial_recv.at[step, rank],
            (tm, peers[step]),
        )

    def frame_copy(spot):
        return remote(
            outbox.at[spot],
            out_ref.at[head, spot],
            frame_send.at[spot],
            frame_recv.at[spot],
            (partners(tm, spot, shards)[0], head),
        )

    def forward_copy(step, spot, part):
        return remote(
            out_ref.at[part, spot],
            out_ref.at[part, spot],
            forward_send.at[step, spot],
            forward_recv.at[step, spot],
            (tm, peers[step]),
        )

    barrier = pltpu.get_barrier_semaphore()
    for peer in peers:
        pl.semaphore_signal(barrier, inc=1, device_id=(tm, peer), device_id_type=MESH)

    def greet(spot, carry):
        pl.semaphore_signal(
            barrier,
            inc=1,
            device_id=(partners(tm, spot, shards)[1], head),
            device_id_type=MESH,
        )
        return carry

    lax.fori_loop(0, shards - 1, greet, 0)

    def stage(rank, carry):
        full[head, rank] = patches_ref[order_ref[rank]]
        return carry

    lax.fori_loop(0, frames, stage, 0)
    for first in range(0, width, LANES):
        tile = jnp.broadcast_to(gain_ref[:, first : first + LANES], (LANES, LANES))
        gain[first : first + LANES] = tile.T
    pl.semaphore_wait(barrier, parts - 1 + shards - 1)

    def share(rank, carry):
        for step in range(parts - 1):
            patch_copy(step, rank, head).start()
        return carry

    lax.fori_loop(0, frames, share, 0)

    def normalise(rank, columns):
        total = 0.0
        for part in range(parts):
            total = total + jnp.sum(full[part, rank].astype(f32), axis=0, keepdims=True)
        centre = total / width
        spread = 0.0
        for part in range(parts):
            moved = full[part, rank].astype(f32) - centre
            spread = spread + jnp.sum(moved * moved, axis=0, keepdims=True)
        scale = lax.rsqrt(spread / width + 1e-06)
        for part in range(parts):
            rows = slice(part * part_width, (part + 1) * part_width)
            wide = jnp.concatenate([gain[rows]] * (patch_count // LANES), axis=1)
            normed[rows, columns] = (
                (full[part, rank].astype(f32) - centre) * scale * wide
            ).astype(bf16)

    spot_row = lax.broadcasted_iota(jnp.int32, (8, patch_count), 0)
    spot_key = lax.broadcasted_iota(jnp.int32, (8, patch_count), 1)
    ones_row = jnp.where(spot_row == 0, 1.0, 0.0).astype(f32)

    def extended(member, head_id, columns, extra):
        rows = slice(head_id * VHD, (head_id + 1) * VHD)
        return jnp.concatenate([qkv[member, rows, columns], extra], axis=0).astype(bf16)

    def score(head_id, columns, key_row):
        return lax.dot_general(
            extended(1, head_id, columns, key_row),
            extended(0, head_id, columns, ones_row),
            CONTRACT_FIRST,
            preferred_element_type=f32,
        )

    def mix(head_id, columns, scores):
        powered = jnp.exp2((scores - jnp.max(scores, axis=0, keepdims=True)) * factor)
        mixed = jnp.dot(
            extended(2, head_id, columns, ones_row),
            powered.astype(bf16),
            preferred_element_type=f32,
        )
        context[head_id * VHD : (head_id + 1) * VHD, columns] = mixed[:VHD] * (
            1.0 / mixed[VHD : VHD + 1]
        )

    pool_row = lax.broadcasted_iota(jnp.int32, (tokens, patch_count), 0)
    pool_column = lax.broadcasted_iota(jnp.int32, (tokens, patch_count), 1)
    pooling = jnp.where(pool_column // POOL == pool_row, 1.0 / POOL, 0.0).astype(bf16)
    token_spot = lax.broadcasted_iota(jnp.int32, (tokens, part_width), 0) * POOL
    spans = [slice(b * patch_count, (b + 1) * patch_count) for b in range(batch)]

    def post(spot):
        outbox[spot, :, :part_width] = pooled_frames[rank_ref[spot]]
        outbox[spot, :, part_width:] = jnp.full(
            (tokens, outbox.shape[2] - part_width), label_ref[spot].astype(f32)
        ).astype(bf16)

    def settle(rank):
        for step in range(parts - 1):
            partial_copy(step, rank).wait_recv()
        total = mine[rank]
        for step in range(parts - 1):
            total = total + partial_in[rank, step].astype(f32)
        pooled_frames[rank] = jnp.where(token_spot < valid_ref[rank], total, 0.0).astype(bf16)
        post(rank)
        frame_copy(rank).start()

    def forward(spot):
        frame_copy(spot).wait_recv()
        for step in range(parts - 1):
            forward_copy(step, spot, head).start()

    def body(turn, carry):
        ranks = [turn * batch + b for b in range(batch)]
        for rank, span in zip(ranks, spans):
            for step in range(parts - 1):
                patch_copy(step, rank, sources[step]).wait_recv()
            normalise(rank, span)
        for member in range(3):
            qkv[member] = jnp.dot(wqkv_ref[member], normed[...], preferred_element_type=f32)

        @pl.when(turn >= 1)
        def _():
            for b in range(batch):
                settle((turn - 1) * batch + b)

        @pl.when(turn >= 3)
        def _():
            for b in range(batch):
                forward((turn - 3) * batch + b)

        key_rows = [
            jnp.where((spot_row == 0) & (spot_key >= valid_ref[rank]), -1e30, 0.0).astype(f32)
            for rank in ranks
        ]
        todo = [(head_id, b) for head_id in range(heads) for b in range(batch)]
        ahead = 2
        ready = [score(h, spans[b], key_rows[b]) for h, b in todo[:ahead]]
        for at, (h, b) in enumerate(todo):
            if at + ahead < len(todo):
                later, which = todo[at + ahead]
                ready.append(score(later, spans[which], key_rows[which]))
            mix(h, spans[b], ready[at])
        pooled = jnp.concatenate(
            [
                lax.dot_general(
                    pooling,
                    context[:, span].astype(bf16),
                    CONTRACT_LAST,
                    preferred_element_type=f32,
                ).astype(bf16)
                for span in spans
            ],
            axis=0,
        )
        attended = jnp.dot(pooled, wout_ref[...], preferred_element_type=f32)
        for b, rank in enumerate(ranks):
            own = lax.dot_general(
                pooling, full[head, rank], CONTRACT_LAST, preferred_element_type=f32
            )
            for part in range(parts):
                block = attended[
                    b * tokens : (b + 1) * tokens, part * part_width : (part + 1) * part_width
                ]
                partial[rank, part] = block.astype(bf16)
                own = own + jnp.where(head == part, block, 0.0)
            mine[rank] = own
            for step in range(parts - 1):
                partial_copy(step, rank).start()
        return carry

    turns = frames // batch
    lax.fori_loop(0, turns, body, 0)
    for rank in range(frames - batch, frames):
        settle(rank)
    for spot in range(frames, shards):
        post(spot)
        if spot < shards - 1:
            frame_copy(spot).start()
    out_ref[head, shards - 1] = outbox[shards - 1]
    for step in range(parts - 1):
        forward_copy(step, shards - 1, head).start()

    def late_forward(spot, carry):
        forward(spot)
        return carry

    lax.fori_loop(max(turns - 3, 0) * batch, shards - 1, late_forward, 0)

    def drain_ranks(rank, carry):
        for step in range(parts - 1):
            patch_copy(step, rank, head).wait_send()
            partial_copy(step, rank).wait_send()
        return carry

    lax.fori_loop(0, frames, drain_ranks, 0)

    def drain_frames(spot, carry):
        frame_copy(spot).wait_send()
        return carry

    lax.fori_loop(0, shards - 1, drain_frames, 0)

    def drain_forwards(spot, carry):
        for step in range(parts - 1):
            forward_copy(step, spot, sources[step]).wait_recv()
            forward_copy(step, spot, head).wait_send()
        return carry

    lax.fori_loop(0, shards, drain_forwards, 0)


def vision(patches, order, valid, rank, label, gain, w_qkv, w_out, parts, shards):
    frames, part_width, patch_count = patches.shape
    width = parts * part_width
    local_width = w_qkv.shape[1]
    tokens = patch_count // POOL
    batch = math.gcd(frames, 2)
    in_smem = pl.BlockSpec(memory_space=pltpu.SMEM)
    in_vmem = pl.BlockSpec(memory_space=VMEM)
    peers = parts - 1
    padded = (part_width // LANES + 1) * LANES
    dma = pltpu.SemaphoreType.DMA
    return pl.pallas_call(
        vision_kernel,
        out_shape=jax.ShapeDtypeStruct((parts, shards, tokens, padded), bf16),
        in_specs=[in_smem] * 4 + [in_vmem] * 4,
        out_specs=in_vmem,
        scratch_shapes=[
            VMEM((parts, frames, part_width, patch_count), bf16),
            VMEM((width, LANES), f32),
            VMEM((width, batch * patch_count), bf16),
            VMEM((3, local_width, batch * patch_count), f32),
            VMEM((local_width, batch * patch_count), f32),
            VMEM((frames, parts, tokens, part_width), bf16),
            VMEM((frames, peers, tokens, part_width), bf16),
            VMEM((frames, tokens, part_width), f32),
            VMEM((frames, tokens, part_width), bf16),
            VMEM((shards, tokens, padded), bf16),
            dma((peers, frames)),
            dma((peers, frames)),
            dma((peers, frames)),
            dma((peers, frames)),
            dma((shards,)),
            dma((shards,)),
            dma((peers, shards)),
            dma((peers, shards)),
        ],
        compiler_params=pltpu.CompilerParams(
            collective_id=0, has_side_effects=True, vmem_limit_bytes=56 << 20
        ),
        cost_estimate=pl.CostEstimate(
            flops=frames * patch_count * width * local_width * 10,
            bytes_accessed=12_000_000,
            transcendentals=4_000_000,
        ),
        name="vision",
    )(order, valid, rank, label, patches, gain, w_qkv, w_out)


def routes(frame_ids, grid_rows, shards):
    frames = frame_ids.shape[0]
    tm = lax.axis_index("tm").astype(jnp.int32)
    spots = jnp.arange(shards, dtype=jnp.int32)
    targets = partners(tm, spots, shards)[0]
    slots = jnp.arange(frames, dtype=jnp.int32)
    total = lambda chosen, member, axis: jnp.sum(
        jnp.where(chosen, member, 0), axis=axis
    ).astype(jnp.int32)
    goes = (frame_ids // frames)[:, None] == targets[None, :]
    spot_of = total(goes, spots[None, :], 1)
    rank_of = jnp.sum(spot_of[None, :] < spot_of[:, None], axis=1).astype(jnp.int32)
    holds = rank_of[None, :] == slots[:, None]
    order = total(holds, slots[None, :], 1)
    valid = total(holds, (grid_rows * GRID)[None, :], 1)
    rank = total(goes, rank_of[:, None], 0)
    label = total(goes, (frame_ids % frames + 1)[:, None], 0)
    return order, valid, rank, label


def spread(rows, width, copies):
    heads = rows // copies
    row = lax.broadcasted_iota(jnp.int32, (rows, heads * width), 0) % heads
    block = lax.broadcasted_iota(jnp.int32, (rows, heads * width), 1) // width
    return jnp.where(row == block, 1.0, 0.0).astype(bf16)


def split(values, copies):
    terms = []
    for _ in range(copies):
        terms.append(values.astype(bf16).astype(f32))
        values = values - terms[-1]
    return jnp.concatenate(terms, axis=0).astype(bf16)


def column(row):
    count = row.shape[1]
    same = lax.broadcasted_iota(jnp.int32, (count, count), 0) == lax.broadcasted_iota(
        jnp.int32, (count, count), 1
    )
    return jnp.sum(jnp.where(same, row, 0.0), axis=1, keepdims=True)


def connect_kernel(
    arrived_ref,
    norm_gain_ref,
    conn_hbm,
    stream_hbm,
    normed,
    conn,
    rows,
    squares,
    result,
    sender_ref,
    conn_sem,
    stream_sem,
):
    parts, shards, frame_tokens, padded = arrived_ref.shape
    tokens, full_width = normed.shape
    conn_count, width, conn_width = conn.shape
    part_width = width // parts
    per_part = conn_count // parts
    frames = tokens // frame_tokens
    head = lax.axis_index("head")

    def conn_load(at):
        return pltpu.make_async_copy(
            conn_hbm.at[
                at // per_part,
                :,
                pl.ds(pl.multiple_of((at % per_part) * conn_width, conn_width), conn_width),
            ],
            conn.at[at],
            conn_sem.at[at],
        )

    def conn_start(at, carry):
        conn_load(at).start()
        return carry

    lax.fori_loop(0, conn_count, conn_start, 0)
    labelled = lax.broadcasted_iota(jnp.int32, (16, LANES), 1) >= part_width - (padded - LANES)
    for shard in range(shards):
        tile = arrived_ref[0, shard, :16, padded - LANES :].astype(f32)
        sender_ref[jnp.max(jnp.where(labelled, tile, 0.0)).astype(jnp.int32)] = shard

    def gather(frame, carry):
        place = pl.ds(pl.multiple_of(frame * frame_tokens, frame_tokens), frame_tokens)
        for part in range(parts):
            rows[place, part * part_width : (part + 1) * part_width] = arrived_ref[
                part, sender_ref[frame + 1], :, :part_width
            ]
        return carry

    lax.fori_loop(0, frames, gather, 0)
    squares[...] = jnp.zeros_like(squares)

    def connect(at, carry):
        conn_load(at).wait()
        columns = pl.ds(pl.multiple_of(at * conn_width, conn_width), conn_width)
        mine = pl.ds(
            pl.multiple_of((at % per_part) * conn_width, conn_width), conn_width
        )
        made = jnp.dot(rows[...], conn[at], preferred_element_type=f32).astype(bf16)
        normed[:, columns] = made

        @pl.when(at // per_part == head)
        def _():
            result[:, mine] = made

        made = made.astype(f32)
        made = made * made
        squares[...] += sum(
            made[:, lane : lane + LANES] for lane in range(0, conn_width, LANES)
        )
        return carry

    lax.fori_loop(0, conn_count, connect, 0)
    stream_copy = pltpu.make_async_copy(result, stream_hbm, stream_sem)
    stream_copy.start()

    def normalise(at, carry):
        span = pl.ds(pl.multiple_of(at * 64, 64), 64)
        total = jnp.sum(squares[span, :], axis=1, keepdims=True)
        scale = lax.rsqrt(total / full_width + 1e-05)
        normed[span, :] = (normed[span, :].astype(f32) * scale * norm_gain_ref[...]).astype(bf16)
        return carry

    lax.fori_loop(0, tokens // 64, normalise, 0)
    stream_copy.wait()


def connect(arrived, frames, weights, norm_gain, features):
    parts, _, frame_tokens, _ = arrived.shape
    _, width, columns = weights.shape
    tokens = frames * frame_tokens
    full_width = parts * columns
    conn_width = math.gcd(columns, features)
    conn_count = full_width // conn_width
    in_vmem = pl.BlockSpec(memory_space=VMEM)
    in_hbm = pl.BlockSpec(memory_space=pl.ANY)
    return pl.pallas_call(
        connect_kernel,
        out_shape=(
            jax.ShapeDtypeStruct((tokens, columns), bf16),
            jax.ShapeDtypeStruct((tokens, full_width), bf16),
        ),
        in_specs=[in_vmem, in_vmem, in_hbm],
        out_specs=(in_hbm, in_vmem),
        scratch_shapes=[
            VMEM((conn_count, width, conn_width), bf16),
            VMEM((tokens, width), bf16),
            VMEM((tokens, LANES), f32),
            VMEM((tokens, columns), bf16),
            pltpu.SMEM((frames + 1,), jnp.int32),
            pltpu.SemaphoreType.DMA((conn_count,)),
            pltpu.SemaphoreType.DMA(()),
        ],
        compiler_params=pltpu.CompilerParams(vmem_limit_bytes=36 << 20),
        name="connect",
    )(arrived, norm_gain.reshape(1, -1), weights)


def mix_kernel(
    normed,
    wdt_ref,
    bias_ref,
    alog_ref,
    skip_ref,
    out_gain_ref,
    wx_hbm,
    wb_hbm,
    wc_hbm,
    out_hbm,
    ring,
    inner,
    write,
    read,
    result,
    local_out,
    staged,
    down,
    across,
    state,
    saved,
    state_out,
    state_in,
    before,
    incoming,
    decay_out,
    decay_in,
    ring_sem,
    out_sem,
    decay_send,
    decay_recv,
    first_send,
    first_recv,
    second_send,
    second_recv,
):
    tokens = normed.shape[0]
    heads = wdt_ref.shape[0]
    groups = write.shape[1] // STATE
    per_group = heads // groups
    features = per_group * HDIM
    chunks = tokens // CHUNK
    block = 2 * CHUNK
    batches, shards, slice_rows, _ = state_in.shape
    batch_groups = groups // batches
    piece = features // shards
    unit = min(piece, HDIM)
    pieces = piece // unit
    tm, head = lax.axis_index("tm"), lax.axis_index("head")
    log2e = math.log2(math.e)

    def remote(source, target, send, recv, spot):
        return pltpu.make_async_remote_copy(
            src_ref=source,
            dst_ref=target,
            send_sem=send,
            recv_sem=recv,
            device_id=(partners(tm, spot, shards)[0], head),
            device_id_type=MESH,
        )

    def target_of(spot):
        return partners(tm, spot, shards)[0]

    def decay_copy(spot):
        return remote(
            decay_out.at[target_of(spot)],
            decay_in.at[tm],
            decay_send.at[spot],
            decay_recv.at[spot],
            spot,
        )

    def first_copy(batch, spot):
        return remote(
            state_out.at[batch, target_of(spot)],
            state_in.at[batch, tm],
            first_send.at[batch, spot],
            first_recv.at[batch, spot],
            spot,
        )

    def second_copy(batch, spot):
        return remote(
            before.at[batch, target_of(spot)],
            incoming.at[batch, tm],
            second_send.at[batch, spot],
            second_recv.at[batch, spot],
            spot,
        )

    def over_spots(act):
        def step(spot, carry):
            act(spot)
            return carry

        lax.fori_loop(0, shards - 1, step, 0)

    barrier = pltpu.get_barrier_semaphore()
    over_spots(
        lambda spot: pl.semaphore_signal(
            barrier,
            inc=1,
            device_id=(partners(tm, spot, shards)[1], head),
            device_id_type=MESH,
        )
    )

    def weight_load(which):
        slot = which % ring.shape[0]
        if which == 0 or which == groups + 1:
            source = wb_hbm if which == 0 else wc_hbm
            target = ring.at[slot, :, : groups * STATE]
        else:
            source = wx_hbm.at[:, (which - 1) * features : which * features]
            target = ring.at[slot]
        return pltpu.make_async_copy(source, target, ring_sem.at[slot])

    for which in range(ring.shape[0]):
        weight_load(which).start()

    raw = lax.dot_general(wdt_ref[...], normed[...], CONTRACT_LAST, preferred_element_type=f32)
    raw = raw + column(bias_ref[...])
    step_size = jnp.maximum(raw, 0.0) + jnp.log1p(jnp.exp(-jnp.abs(raw)))
    rate = -jnp.exp(column(alog_ref[...])) * log2e
    log_decay = step_size * rate
    log_step = jnp.log(step_size) * log2e
    upper = jnp.where(
        lax.broadcasted_iota(jnp.int32, (CHUNK, CHUNK), 0)
        <= lax.broadcasted_iota(jnp.int32, (CHUNK, CHUNK), 1),
        1.0,
        0.0,
    ).astype(f32)
    ends = []
    for chunk in range(chunks):
        span = slice(chunk * CHUNK, (chunk + 1) * CHUNK)
        sums = jnp.dot(
            log_decay[:, span],
            upper,
            preferred_element_type=f32,
            precision=lax.Precision.HIGHEST,
        )
        down[chunk] = sums
        across[chunk] = sums - log_step[:, span]
        ends.append(sums[:, CHUNK - 1 :])
    total = jnp.zeros_like(ends[0])
    for chunk in range(chunks):
        staged[chunk] = jnp.broadcast_to(total, (heads, LANES))
        total = total + ends[chunk]
    staged[chunks] = jnp.broadcast_to(jnp.exp2(total), (heads, LANES))
    decay_out[...] = jnp.zeros_like(decay_out)
    for target in range(shards):
        for group in range(groups):
            for part in range(pieces):
                at = group * per_group + (target * piece + part * unit) // HDIM
                row = group * pieces + part
                decay_out[target, row : row + 1] = staged[chunks, at : at + 1]
    decay_in[tm] = decay_out[tm]
    pl.semaphore_wait(barrier, shards - 1)
    over_spots(lambda spot: decay_copy(spot).start())

    def project(which, target, first_column, count):
        slot = which % ring.shape[0]
        weight_load(which).wait()

        def part(at, carry):
            span = pl.ds(pl.multiple_of(at * block, block), block)
            target[span, first_column : first_column + count] = jnp.dot(
                normed[span, :], ring[slot, :, :count], preferred_element_type=f32
            ).astype(bf16)
            return carry

        lax.fori_loop(0, tokens // block, part, 0)
        if which + ring.shape[0] <= groups + 1:
            weight_load(which + ring.shape[0]).start()

    spread_narrow = spread(2 * per_group, HDIM, 2)
    spread_wide = spread(3 * per_group, CHUNK, 3)
    head_row = lax.broadcasted_iota(jnp.int32, (per_group, features), 0)
    head_lane = lax.broadcasted_iota(jnp.int32, (per_group, features), 1) // HDIM

    def widen(values):
        return lax.dot_general(
            split(values, 2), spread_narrow, CONTRACT_FIRST, preferred_element_type=f32
        )

    def widen_row(values):
        return jnp.sum(jnp.where(head_row == head_lane, values, 0.0), axis=0, keepdims=True)

    def at_group(group, chunk):
        own = slice(group * per_group, (group + 1) * per_group)
        return (
            pl.ds(pl.multiple_of(chunk * CHUNK, CHUNK), CHUNK),
            slice(group * features, (group + 1) * features),
            slice(group * STATE, (group + 1) * STATE),
            own,
        )

    def states(group):
        state[...] = jnp.zeros_like(state)

        def step(chunk, carry):
            span, lanes, keys, own = at_group(group, chunk)
            sums, shifted = down[chunk, own], across[chunk, own]
            end = sums[:, CHUNK - 1 :]
            held = state[...]
            saved[group, chunk] = held.astype(bf16)
            scaled = (inner[span, lanes].astype(f32) * widen(jnp.exp2(end - shifted))).astype(bf16)
            state[...] = held * widen_row(jnp.exp2(end)) + lax.dot_general(
                write[span, keys], scaled, CONTRACT_FIRST, preferred_element_type=f32
            )
            return carry

        lax.fori_loop(0, chunks, step, 0, unroll=math.gcd(chunks, 3))
        batch, inside = group // batch_groups, group % batch_groups
        sideways = state[...].T.astype(bf16)
        for target in range(shards):
            state_out[batch, target, inside * piece : (inside + 1) * piece] = sideways[
                target * piece : (target + 1) * piece
            ]

    def send_first(batch):
        state_in[batch, tm] = state_out[batch, tm]
        over_spots(lambda spot: first_copy(batch, spot).start())

    def send_second(batch):
        if batch == 0:
            over_spots(lambda spot: decay_copy(spot).wait_recv())
        over_spots(lambda spot: first_copy(batch, spot).wait_recv())
        for inside in range(batch_groups):
            group = batch * batch_groups + inside
            for part in range(pieces):
                span = slice(inside * piece + part * unit, inside * piece + (part + 1) * unit)
                row = group * pieces + part
                current = jnp.zeros((unit, STATE), f32)
                for shard in range(shards):
                    before[batch, shard, span] = current.astype(bf16)
                    current = decay_in[shard, row : row + 1] * current + state_in[
                        batch, shard, span
                    ].astype(f32)
        incoming[batch, tm] = before[batch, tm]
        over_spots(lambda spot: second_copy(batch, spot).start())

    causal = lax.broadcasted_iota(jnp.int32, (CHUNK, CHUNK), 0) >= lax.broadcasted_iota(
        jnp.int32, (CHUNK, CHUNK), 1
    )
    lane = lax.broadcasted_iota(jnp.int32, (CHUNK, LANES), 1)
    skip_column = column(skip_ref[...])

    def local(group):
        skip = widen_row(skip_column[group * per_group : (group + 1) * per_group])

        def step(chunk, carry):
            span, lanes, keys, own = at_group(group, chunk)
            sums, shifted = down[chunk, own], across[chunk, own]
            readers = read[span, keys]
            crossing = lax.dot_general(
                readers, write[span, keys], CONTRACT_LAST, preferred_element_type=f32
            )
            crossing = jnp.where(causal, crossing, 0.0)
            downs = lax.dot_general(
                split(sums, 3), spread_wide, CONTRACT_FIRST, preferred_element_type=f32
            )
            grown = widen(jnp.exp2(sums))
            carried = jnp.dot(readers, saved[group, chunk], preferred_element_type=f32)
            for pair in range(features // LANES):
                at = slice(pair * LANES, (pair + 1) * LANES)
                here = slice(lanes.start + pair * LANES, lanes.start + (pair + 1) * LANES)
                values = inner[span, here]
                halves = []
                for one in (2 * pair, 2 * pair + 1):
                    spans = downs[:, one * CHUNK : (one + 1) * CHUNK] - shifted[one : one + 1]
                    halves.append((crossing * jnp.exp2(jnp.minimum(spans, 100.0))).astype(bf16))
                wide = values.astype(f32)
                stacked = jnp.concatenate(
                    [jnp.where(lane < HDIM, wide, 0.0), jnp.where(lane < HDIM, 0.0, wide)], axis=0
                ).astype(bf16)
                within = jnp.dot(
                    jnp.concatenate(halves, axis=1), stacked, preferred_element_type=f32
                )
                local_out[span, here] = within + carried[:, at] * grown[:, at] + skip[:, at] * wide
            return carry

        lax.fori_loop(0, chunks, step, 0, unroll=math.gcd(chunks, 3))

    def finish(group):
        batch, inside = group // batch_groups, group % batch_groups
        held = jnp.concatenate(
            [
                incoming[batch, shard, inside * piece : (inside + 1) * piece]
                for shard in range(shards)
            ],
            axis=0,
        )

        def step(chunk, carry):
            span, lanes, keys, own = at_group(group, chunk)
            grown = widen(jnp.exp2(down[chunk, own] + staged[chunk, own]))
            carried = lax.dot_general(
                read[span, keys], held, CONTRACT_LAST, preferred_element_type=f32
            )
            summed = local_out[span, lanes] + carried * grown
            mean = jnp.sum(summed * summed, axis=1, keepdims=True) / features
            result[span, lanes] = (
                summed * lax.rsqrt(mean + 1e-05) * out_gain_ref[:, lanes]
            ).astype(bf16)
            return carry

        lax.fori_loop(0, chunks, step, 0, unroll=math.gcd(chunks, 3))

    def out_copy(group):
        lanes = slice(group * features, (group + 1) * features)
        return pltpu.make_async_copy(
            result.at[:, lanes], out_hbm.at[:, lanes], out_sem.at[group]
        )

    project(0, write, 0, groups * STATE)
    for group in range(groups):
        project(group + 1, inner, group * features, features)
        states(group)
        if (group + 1) % batch_groups == 0:
            send_first(group // batch_groups)
    if batches > 1:
        send_second(0)
    project(groups + 1, read, 0, groups * STATE)
    for group in range(groups):
        if group == groups // 2:
            send_second(batches - 1)
        local(group)
    for group in range(groups):
        if group % batch_groups == 0:
            batch = group // batch_groups
            over_spots(lambda spot: second_copy(batch, spot).wait_recv())
        finish(group)
        out_copy(group).start()
    over_spots(lambda spot: decay_copy(spot).wait_send())
    for batch in range(batches):
        over_spots(lambda spot: first_copy(batch, spot).wait_send())
        over_spots(lambda spot: second_copy(batch, spot).wait_send())
    for group in range(groups):
        out_copy(group).wait()


def mix(normed, w_x, w_b, w_c, w_dt, dt_bias, a_log, d_skip, out_gain, shards):
    tokens = normed.shape[0]
    heads = w_dt.shape[1]
    groups = w_b.shape[1] // STATE
    features = heads // groups * HDIM
    chunks = tokens // CHUNK
    batches = math.gcd(groups, 2)
    piece = features // shards
    slice_rows = groups // batches * piece
    pieces = max(piece // HDIM, 1)
    decay_rows = -(-groups * pieces // 8) * 8
    in_vmem = pl.BlockSpec(memory_space=VMEM)
    in_hbm = pl.BlockSpec(memory_space=pl.ANY)
    dma = pltpu.SemaphoreType.DMA
    shape = jax.ShapeDtypeStruct((tokens, heads * HDIM), bf16)
    row = lambda member: member.reshape(1, -1)
    return pl.pallas_call(
        mix_kernel,
        out_shape=shape,
        in_specs=[in_vmem] * 6 + [in_hbm] * 3,
        out_specs=in_hbm,
        scratch_shapes=[
            VMEM((min(3, groups + 2), w_x.shape[0], features), bf16),
            VMEM((tokens, heads * HDIM), bf16),
            VMEM((tokens, groups * STATE), bf16),
            VMEM((tokens, groups * STATE), bf16),
            VMEM((tokens, heads * HDIM), bf16),
            VMEM((tokens, heads * HDIM), f32),
            VMEM((chunks + 1, heads, LANES), f32),
            VMEM((chunks, heads, CHUNK), f32),
            VMEM((chunks, heads, CHUNK), f32),
            VMEM((STATE, features), f32),
            VMEM((groups, chunks, STATE, features), bf16),
            VMEM((batches, shards, slice_rows, STATE), bf16),
            VMEM((batches, shards, slice_rows, STATE), bf16),
            VMEM((batches, shards, slice_rows, STATE), bf16),
            VMEM((batches, shards, slice_rows, STATE), bf16),
            VMEM((shards, decay_rows, LANES), f32),
            VMEM((shards, decay_rows, LANES), f32),
            dma((min(3, groups + 2),)),
            dma((groups,)),
            dma((shards,)),
            dma((shards,)),
            dma((batches, shards)),
            dma((batches, shards)),
            dma((batches, shards)),
            dma((batches, shards)),
        ],
        compiler_params=pltpu.CompilerParams(
            collective_id=1, has_side_effects=True, vmem_limit_bytes=36 << 20
        ),
        name="mix",
    )(
        normed,
        w_dt.T,
        row(dt_bias),
        row(a_log),
        row(d_skip),
        row(out_gain),
        w_x,
        w_b,
        w_c,
    )


def on_device(
    patches,
    grid_rows,
    frame_ids,
    ln_gain,
    w_qkv,
    w_out,
    w_conn,
    norm_gain,
    w_x,
    w_b,
    w_c,
    w_dt,
    dt_bias,
    a_log,
    d_skip,
    out_gain,
):
    part_width = patches.shape[2]
    shards = lax.axis_size("tm")
    my = lax.axis_index("head").astype(jnp.int32).reshape(1)
    parts = lax.axis_size("head")
    all_conn = lax.all_gather(w_conn, "head")
    order, valid, rank, label = routes(frame_ids, grid_rows, shards)
    arrived = vision(
        patches.swapaxes(1, 2),
        order,
        valid,
        rank,
        label,
        ln_gain.reshape(1, -1),
        w_qkv.swapaxes(1, 2),
        w_out,
        parts,
        shards,
    )
    features = w_dt.shape[1] // (w_b.shape[1] // STATE) * HDIM
    stream, normed = connect(arrived, frame_ids.shape[0], all_conn, norm_gain, features)
    return stream, mix(normed, w_x, w_b, w_c, w_dt, dt_bias, a_log, d_skip, out_gain, shards)


def solution(mesh):
    in_specs = (
        P("tm", None, "head"),
        P("tm"),
        P("tm"),
        P(),
        P(None, None, "head"),
        P("head", None),
        P(None, "head"),
        P(),
        P(None, "head"),
        P(None, "head"),
        P(None, "head"),
        P(None, "head"),
        P("head"),
        P("head"),
        P("head"),
        P("head"),
    )
    out_specs = (P("tm", "head"), P("tm", "head"))
    return jax.shard_map(
        on_device, mesh=mesh, in_specs=in_specs, out_specs=out_specs, check_vma=False
    )
```

```python
import math

import jax
import jax.numpy as jnp
from jax import lax
from jax.experimental import pallas as pl
from jax.experimental.pallas import tpu as pltpu
from jax.sharding import PartitionSpec as P

GRID = 16
POOL = 4
VHD = 72
HDIM = 64
STATE = 128
CHUNK = 128
LANES = 128

f32 = jnp.float32
bf16 = jnp.bfloat16
VMEM = pltpu.VMEM
MESH = pl.DeviceIdType.MESH
CONTRACT_LAST = (((1,), (1,)), ((), ()))
CONTRACT_FIRST = (((0,), (0,)), ((), ()))


def flipped(index, mask, count):
    result, bit = 0, 1
    while bit < count:
        result = result + bit * ((index // bit + mask // bit) % 2)
        bit *= 2
    return result


def partners(index, spot, count):
    if count & (count - 1):
        return (index + spot + 1) % count, (index + 2 * count - spot - 1) % count
    other = flipped(index, count - 1 - spot, count)
    return other, other


def vision_kernel(
    order_ref,
    valid_ref,
    rank_ref,
    label_ref,
    patches_ref,
    gain_ref,
    wqkv_ref,
    wout_ref,
    out_ref,
    full,
    gain,
    normed,
    qkv,
    context,
    partial,
    partial_in,
    mine,
    pooled_frames,
    outbox,
    patch_send,
    patch_recv,
    partial_send,
    partial_recv,
    frame_send,
    frame_recv,
    forward_send,
    forward_recv,
):
    parts, frames, part_width, patch_count = full.shape
    shards = out_ref.shape[1]
    width = parts * part_width
    local_width = wqkv_ref.shape[1]
    heads = local_width // VHD
    tokens = patch_count // POOL
    batch = normed.shape[1] // patch_count
    factor = VHD ** (-0.5) * math.log2(math.e)
    tm, head = lax.axis_index("tm"), lax.axis_index("head")
    peers = [(head + step) % parts for step in range(1, parts)]
    sources = [(head + parts - step) % parts for step in range(1, parts)]

    def remote(source, target, send, recv, to):
        return pltpu.make_async_remote_copy(
            src_ref=source,
            dst_ref=target,
            send_sem=send,
            recv_sem=recv,
            device_id=to,
            device_id_type=MESH,
        )

    def patch_copy(step, rank, part):
        return remote(
            full.at[part, rank],
            full.at[part, rank],
            patch_send.at[step, rank],
            patch_recv.at[step, rank],
            (tm, peers[step]),
        )

    def partial_copy(step, rank):
        return remote(
            partial.at[rank, peers[step]],
            partial_in.at[rank, step],
            partial_send.at[step, rank],
            partial_recv.at[step, rank],
            (tm, peers[step]),
        )

    def frame_copy(spot):
        return remote(
            outbox.at[spot],
            out_ref.at[head, spot],
            frame_send.at[spot],
            frame_recv.at[spot],
            (partners(tm, spot, shards)[0], head),
        )

    def forward_copy(step, spot, part):
        return remote(
            out_ref.at[part, spot],
            out_ref.at[part, spot],
            forward_send.at[step, spot],
            forward_recv.at[step, spot],
            (tm, peers[step]),
        )

    barrier = pltpu.get_barrier_semaphore()
    for peer in peers:
        pl.semaphore_signal(barrier, inc=1, device_id=(tm, peer), device_id_type=MESH)

    def greet(spot, carry):
        pl.semaphore_signal(
            barrier,
            inc=1,
            device_id=(partners(tm, spot, shards)[1], head),
            device_id_type=MESH,
        )
        return carry

    lax.fori_loop(0, shards - 1, greet, 0)

    def stage(rank, carry):
        full[head, rank] = patches_ref[order_ref[rank]]
        return carry

    lax.fori_loop(0, frames, stage, 0)
    for first in range(0, width, LANES):
        tile = jnp.broadcast_to(gain_ref[:, first : first + LANES], (LANES, LANES))
        gain[first : first + LANES] = tile.T
    pl.semaphore_wait(barrier, parts - 1 + shards - 1)

    def share(rank, carry):
        for step in range(parts - 1):
            patch_copy(step, rank, head).start()
        return carry

    lax.fori_loop(0, frames, share, 0)

    def normalise(rank, columns):
        total = 0.0
        for part in range(parts):
            total = total + jnp.sum(full[part, rank].astype(f32), axis=0, keepdims=True)
        centre = total / width
        spread = 0.0
        for part in range(parts):
            moved = full[part, rank].astype(f32) - centre
            spread = spread + jnp.sum(moved * moved, axis=0, keepdims=True)
        scale = lax.rsqrt(spread / width + 1e-06)
        for part in range(parts):
            rows = slice(part * part_width, (part + 1) * part_width)
            wide = jnp.concatenate([gain[rows]] * (patch_count // LANES), axis=1)
            normed[rows, columns] = (
                (full[part, rank].astype(f32) - centre) * scale * wide
            ).astype(bf16)

    spot_row = lax.broadcasted_iota(jnp.int32, (8, patch_count), 0)
    spot_key = lax.broadcasted_iota(jnp.int32, (8, patch_count), 1)
    ones_row = jnp.where(spot_row == 0, 1.0, 0.0).astype(f32)

    def extended(member, head_id, columns, extra):
        rows = slice(head_id * VHD, (head_id + 1) * VHD)
        return jnp.concatenate([qkv[member, rows, columns], extra], axis=0).astype(bf16)

    def score(head_id, columns, key_row):
        return lax.dot_general(
            extended(1, head_id, columns, key_row),
            extended(0, head_id, columns, ones_row),
            CONTRACT_FIRST,
            preferred_element_type=f32,
        )

    def mix(head_id, columns, scores):
        powered = jnp.exp2((scores - jnp.max(scores, axis=0, keepdims=True)) * factor)
        mixed = jnp.dot(
            extended(2, head_id, columns, ones_row),
            powered.astype(bf16),
            preferred_element_type=f32,
        )
        context[head_id * VHD : (head_id + 1) * VHD, columns] = mixed[:VHD] * (
            1.0 / mixed[VHD : VHD + 1]
        )

    pool_row = lax.broadcasted_iota(jnp.int32, (tokens, patch_count), 0)
    pool_column = lax.broadcasted_iota(jnp.int32, (tokens, patch_count), 1)
    pooling = jnp.where(pool_column // POOL == pool_row, 1.0 / POOL, 0.0).astype(bf16)
    token_spot = lax.broadcasted_iota(jnp.int32, (tokens, part_width), 0) * POOL
    spans = [slice(b * patch_count, (b + 1) * patch_count) for b in range(batch)]

    def post(spot):
        outbox[spot, :, :part_width] = pooled_frames[rank_ref[spot]]
        outbox[spot, :, part_width:] = jnp.full(
            (tokens, outbox.shape[2] - part_width), label_ref[spot].astype(f32)
        ).astype(bf16)

    def settle(rank):
        for step in range(parts - 1):
            partial_copy(step, rank).wait_recv()
        total = mine[rank]
        for step in range(parts - 1):
            total = total + partial_in[rank, step].astype(f32)
        pooled_frames[rank] = jnp.where(token_spot < valid_ref[rank], total, 0.0).astype(bf16)
        post(rank)
        frame_copy(rank).start()

    def forward(spot):
        frame_copy(spot).wait_recv()
        for step in range(parts - 1):
            forward_copy(step, spot, head).start()

    def body(turn, carry):
        ranks = [turn * batch + b for b in range(batch)]
        for rank, span in zip(ranks, spans):
            for step in range(parts - 1):
                patch_copy(step, rank, sources[step]).wait_recv()
            normalise(rank, span)
        for member in range(3):
            qkv[member] = jnp.dot(wqkv_ref[member], normed[...], preferred_element_type=f32)

        @pl.when(turn >= 1)
        def _():
            for b in range(batch):
                settle((turn - 1) * batch + b)

        @pl.when(turn >= 3)
        def _():
            for b in range(batch):
                forward((turn - 3) * batch + b)

        key_rows = [
            jnp.where((spot_row == 0) & (spot_key >= valid_ref[rank]), -1e30, 0.0).astype(f32)
            for rank in ranks
        ]
        todo = [(head_id, b) for head_id in range(heads) for b in range(batch)]
        ahead = 4
        ready = [score(h, spans[b], key_rows[b]) for h, b in todo[:ahead]]
        for at, (h, b) in enumerate(todo):
            if at + ahead < len(todo):
                later, which = todo[at + ahead]
                ready.append(score(later, spans[which], key_rows[which]))
            mix(h, spans[b], ready[at])
        pooled = jnp.concatenate(
            [
                lax.dot_general(
                    pooling,
                    context[:, span].astype(bf16),
                    CONTRACT_LAST,
                    preferred_element_type=f32,
                ).astype(bf16)
                for span in spans
            ],
            axis=0,
        )
        attended = jnp.dot(pooled, wout_ref[...], preferred_element_type=f32)
        for b, rank in enumerate(ranks):
            own = lax.dot_general(
                pooling, full[head, rank], CONTRACT_LAST, preferred_element_type=f32
            )
            for part in range(parts):
                block = attended[
                    b * tokens : (b + 1) * tokens, part * part_width : (part + 1) * part_width
                ]
                partial[rank, part] = block.astype(bf16)
                own = own + jnp.where(head == part, block, 0.0)
            mine[rank] = own
            for step in range(parts - 1):
                partial_copy(step, rank).start()
        return carry

    turns = frames // batch
    lax.fori_loop(0, turns, body, 0)
    for rank in range(frames - batch, frames):
        settle(rank)
    for spot in range(frames, shards):
        post(spot)
        if spot < shards - 1:
            frame_copy(spot).start()
    out_ref[head, shards - 1] = outbox[shards - 1]
    for step in range(parts - 1):
        forward_copy(step, shards - 1, head).start()

    def late_forward(spot, carry):
        forward(spot)
        return carry

    lax.fori_loop(max(turns - 3, 0) * batch, shards - 1, late_forward, 0)

    def drain_ranks(rank, carry):
        for step in range(parts - 1):
            patch_copy(step, rank, head).wait_send()
            partial_copy(step, rank).wait_send()
        return carry

    lax.fori_loop(0, frames, drain_ranks, 0)

    def drain_frames(spot, carry):
        frame_copy(spot).wait_send()
        return carry

    lax.fori_loop(0, shards - 1, drain_frames, 0)

    def drain_forwards(spot, carry):
        for step in range(parts - 1):
            forward_copy(step, spot, sources[step]).wait_recv()
            forward_copy(step, spot, head).wait_send()
        return carry

    lax.fori_loop(0, shards, drain_forwards, 0)


def vision(patches, order, valid, rank, label, gain, w_qkv, w_out, parts, shards):
    frames, part_width, patch_count = patches.shape
    width = parts * part_width
    local_width = w_qkv.shape[1]
    tokens = patch_count // POOL
    batch = math.gcd(frames, 2)
    in_smem = pl.BlockSpec(memory_space=pltpu.SMEM)
    in_vmem = pl.BlockSpec(memory_space=VMEM)
    peers = parts - 1
    padded = (part_width // LANES + 1) * LANES
    dma = pltpu.SemaphoreType.DMA
    return pl.pallas_call(
        vision_kernel,
        out_shape=jax.ShapeDtypeStruct((parts, shards, tokens, padded), bf16),
        in_specs=[in_smem] * 4 + [in_vmem] * 4,
        out_specs=in_vmem,
        scratch_shapes=[
            VMEM((parts, frames, part_width, patch_count), bf16),
            VMEM((width, LANES), f32),
            VMEM((width, batch * patch_count), bf16),
            VMEM((3, local_width, batch * patch_count), f32),
            VMEM((local_width, batch * patch_count), f32),
            VMEM((frames, parts, tokens, part_width), bf16),
            VMEM((frames, peers, tokens, part_width), bf16),
            VMEM((frames, tokens, part_width), f32),
            VMEM((frames, tokens, part_width), bf16),
            VMEM((shards, tokens, padded), bf16),
            dma((peers, frames)),
            dma((peers, frames)),
            dma((peers, frames)),
            dma((peers, frames)),
            dma((shards,)),
            dma((shards,)),
            dma((peers, shards)),
            dma((peers, shards)),
        ],
        compiler_params=pltpu.CompilerParams(
            collective_id=0, has_side_effects=True, vmem_limit_bytes=56 << 20
        ),
        cost_estimate=pl.CostEstimate(
            flops=frames * patch_count * width * local_width * 10,
            bytes_accessed=12_000_000,
            transcendentals=4_000_000,
        ),
        name="vision",
    )(order, valid, rank, label, patches, gain, w_qkv, w_out)


def routes(frame_ids, grid_rows, shards):
    frames = frame_ids.shape[0]
    tm = lax.axis_index("tm").astype(jnp.int32)
    spots = jnp.arange(shards, dtype=jnp.int32)
    targets = partners(tm, spots, shards)[0]
    slots = jnp.arange(frames, dtype=jnp.int32)
    total = lambda chosen, member, axis: jnp.sum(
        jnp.where(chosen, member, 0), axis=axis
    ).astype(jnp.int32)
    goes = (frame_ids // frames)[:, None] == targets[None, :]
    spot_of = total(goes, spots[None, :], 1)
    rank_of = jnp.sum(spot_of[None, :] < spot_of[:, None], axis=1).astype(jnp.int32)
    holds = rank_of[None, :] == slots[:, None]
    order = total(holds, slots[None, :], 1)
    valid = total(holds, (grid_rows * GRID)[None, :], 1)
    rank = total(goes, rank_of[:, None], 0)
    label = total(goes, (frame_ids % frames + 1)[:, None], 0)
    return order, valid, rank, label


def spread(rows, width, copies):
    heads = rows // copies
    row = lax.broadcasted_iota(jnp.int32, (rows, heads * width), 0) % heads
    block = lax.broadcasted_iota(jnp.int32, (rows, heads * width), 1) // width
    return jnp.where(row == block, 1.0, 0.0).astype(bf16)


def split(values, copies):
    terms = []
    for _ in range(copies):
        terms.append(values.astype(bf16).astype(f32))
        values = values - terms[-1]
    return jnp.concatenate(terms, axis=0).astype(bf16)


def column(row):
    count = row.shape[1]
    same = lax.broadcasted_iota(jnp.int32, (count, count), 0) == lax.broadcasted_iota(
        jnp.int32, (count, count), 1
    )
    return jnp.sum(jnp.where(same, row, 0.0), axis=1, keepdims=True)


def connect_kernel(
    arrived_hbm,
    norm_gain_ref,
    conn_hbm,
    stream_hbm,
    normed_hbm,
    squares,
    arrived_ref,
    conn,
    rows,
    gained,
    result,
    sender_ref,
    arrived_sem,
    conn_sem,
    normed_sem,
    stream_sem,
):
    parts, shards, frame_tokens, padded = arrived_ref.shape
    tokens = rows.shape[0]
    conn_count, width, conn_width = conn.shape
    part_width = width // parts
    per_part = conn_count // parts
    frames = tokens // frame_tokens
    head = lax.axis_index("head")
    arrived_copy = pltpu.make_async_copy(arrived_hbm, arrived_ref, arrived_sem)
    arrived_copy.start()

    def conn_load(at):
        return pltpu.make_async_copy(
            conn_hbm.at[
                at // per_part,
                :,
                pl.ds(pl.multiple_of((at % per_part) * conn_width, conn_width), conn_width),
            ],
            conn.at[at],
            conn_sem.at[at],
        )

    def conn_start(at, carry):
        conn_load(at).start()
        return carry

    lax.fori_loop(0, conn_count, conn_start, 0)
    arrived_copy.wait()
    labelled = lax.broadcasted_iota(jnp.int32, (16, LANES), 1) >= part_width - (padded - LANES)
    for shard in range(shards):
        tile = arrived_ref[0, shard, :16, padded - LANES :].astype(f32)
        sender_ref[jnp.max(jnp.where(labelled, tile, 0.0)).astype(jnp.int32)] = shard

    def gather(frame, carry):
        place = pl.ds(pl.multiple_of(frame * frame_tokens, frame_tokens), frame_tokens)
        for part in range(parts):
            rows[place, part * part_width : (part + 1) * part_width] = arrived_ref[
                part, sender_ref[frame + 1], :, :part_width
            ]
        return carry

    lax.fori_loop(0, frames, gather, 0)
    squares[...] = jnp.zeros_like(squares)

    def normed_copy(at):
        columns = pl.ds(pl.multiple_of(at * conn_width, conn_width), conn_width)
        return pltpu.make_async_copy(gained.at[at], normed_hbm.at[:, columns], normed_sem.at[at])

    def connect(at, carry):
        conn_load(at).wait()
        columns = pl.ds(pl.multiple_of(at * conn_width, conn_width), conn_width)
        mine = pl.ds(
            pl.multiple_of((at % per_part) * conn_width, conn_width), conn_width
        )
        made = jnp.dot(rows[...], conn[at], preferred_element_type=f32).astype(bf16)

        @pl.when(at // per_part == head)
        def _():
            result[:, mine] = made

        made = made.astype(f32)
        gained[at] = (made * norm_gain_ref[:, columns]).astype(bf16)
        normed_copy(at).start()
        made = made * made
        squares[...] += sum(
            made[:, lane : lane + LANES] for lane in range(0, conn_width, LANES)
        )
        return carry

    lax.fori_loop(0, conn_count, connect, 0)
    stream_copy = pltpu.make_async_copy(result, stream_hbm, stream_sem)
    stream_copy.start()

    def drain(at, carry):
        normed_copy(at).wait()
        return carry

    lax.fori_loop(0, conn_count, drain, 0)
    stream_copy.wait()


def connect(arrived, frames, weights, norm_gain, features):
    parts, _, frame_tokens, _ = arrived.shape
    _, width, columns = weights.shape
    tokens = frames * frame_tokens
    full_width = parts * columns
    conn_width = math.gcd(columns, features)
    conn_count = full_width // conn_width
    in_vmem = pl.BlockSpec(memory_space=VMEM)
    in_hbm = pl.BlockSpec(memory_space=pl.ANY)
    return pl.pallas_call(
        connect_kernel,
        out_shape=(
            jax.ShapeDtypeStruct((tokens, columns), bf16),
            jax.ShapeDtypeStruct((tokens, full_width), bf16),
            jax.ShapeDtypeStruct((tokens, LANES), f32),
        ),
        in_specs=[in_hbm, in_vmem, in_hbm],
        out_specs=(in_hbm, in_hbm, in_vmem),
        scratch_shapes=[
            VMEM(arrived.shape, bf16),
            VMEM((conn_count, width, conn_width), bf16),
            VMEM((tokens, width), bf16),
            VMEM((conn_count, tokens, conn_width), bf16),
            VMEM((tokens, columns), bf16),
            pltpu.SMEM((frames + 1,), jnp.int32),
            pltpu.SemaphoreType.DMA(()),
            pltpu.SemaphoreType.DMA((conn_count,)),
            pltpu.SemaphoreType.DMA((conn_count,)),
            pltpu.SemaphoreType.DMA(()),
        ],
        compiler_params=pltpu.CompilerParams(vmem_limit_bytes=60 << 20),
        name="connect",
    )(arrived, norm_gain.reshape(1, -1), weights)


def mix_kernel(
    squares_ref,
    wdt_ref,
    bias_ref,
    alog_ref,
    skip_ref,
    out_gain_ref,
    normed_hbm,
    wx_hbm,
    wb_hbm,
    wc_hbm,
    out_hbm,
    normed,
    scales,
    ring,
    inner,
    write,
    read,
    result,
    local_out,
    staged,
    down,
    across,
    state,
    saved,
    state_out,
    state_in,
    before,
    incoming,
    decay_out,
    decay_in,
    normed_sem,
    ring_sem,
    out_sem,
    decay_send,
    decay_recv,
    first_send,
    first_recv,
    second_send,
    second_recv,
):
    tokens, full_width = normed.shape
    heads = wdt_ref.shape[0]
    groups = write.shape[1] // STATE
    per_group = heads // groups
    features = per_group * HDIM
    chunks = tokens // CHUNK
    block = 2 * CHUNK
    batches, shards, slice_rows, _ = state_in.shape
    batch_groups = groups // batches
    piece = features // shards
    unit = min(piece, HDIM)
    pieces = piece // unit
    tm, head = lax.axis_index("tm"), lax.axis_index("head")
    log2e = math.log2(math.e)

    def remote(source, target, send, recv, spot):
        return pltpu.make_async_remote_copy(
            src_ref=source,
            dst_ref=target,
            send_sem=send,
            recv_sem=recv,
            device_id=(partners(tm, spot, shards)[0], head),
            device_id_type=MESH,
        )

    def target_of(spot):
        return partners(tm, spot, shards)[0]

    def decay_copy(spot):
        return remote(
            decay_out.at[target_of(spot)],
            decay_in.at[tm],
            decay_send.at[spot],
            decay_recv.at[spot],
            spot,
        )

    def first_copy(batch, spot):
        return remote(
            state_out.at[batch, target_of(spot)],
            state_in.at[batch, tm],
            first_send.at[batch, spot],
            first_recv.at[batch, spot],
            spot,
        )

    def second_copy(batch, spot):
        return remote(
            before.at[batch, target_of(spot)],
            incoming.at[batch, tm],
            second_send.at[batch, spot],
            second_recv.at[batch, spot],
            spot,
        )

    def over_spots(act):
        def step(spot, carry):
            act(spot)
            return carry

        lax.fori_loop(0, shards - 1, step, 0)

    barrier = pltpu.get_barrier_semaphore()
    over_spots(
        lambda spot: pl.semaphore_signal(
            barrier,
            inc=1,
            device_id=(partners(tm, spot, shards)[1], head),
            device_id_type=MESH,
        )
    )

    def weight_load(which):
        slot = which % ring.shape[0]
        if which == 0 or which == groups + 1:
            source = wb_hbm if which == 0 else wc_hbm
            target = ring.at[slot, :, : groups * STATE]
        else:
            source = wx_hbm.at[:, (which - 1) * features : which * features]
            target = ring.at[slot]
        return pltpu.make_async_copy(source, target, ring_sem.at[slot])

    normed_copy = pltpu.make_async_copy(normed_hbm, normed, normed_sem)
    normed_copy.start()
    for which in range(ring.shape[0]):
        weight_load(which).start()
    mean = jnp.sum(squares_ref[...], axis=1, keepdims=True) / full_width
    scales[...] = jnp.broadcast_to(lax.rsqrt(mean + 1e-05), scales.shape)
    mean_row = lax.dot_general(
        jnp.ones((8, LANES), f32),
        squares_ref[...],
        CONTRACT_LAST,
        preferred_element_type=f32,
        precision=lax.Precision.HIGHEST,
    )
    scale_row = lax.rsqrt(mean_row[:1] / full_width + 1e-05)
    normed_copy.wait()

    raw = lax.dot_general(wdt_ref[...], normed[...], CONTRACT_LAST, preferred_element_type=f32)
    raw = raw * scale_row + column(bias_ref[...])
    step_size = jnp.maximum(raw, 0.0) + jnp.log1p(jnp.exp(-jnp.abs(raw)))
    rate = -jnp.exp(column(alog_ref[...])) * log2e
    log_decay = step_size * rate
    log_step = jnp.log(step_size) * log2e
    upper = jnp.where(
        lax.broadcasted_iota(jnp.int32, (CHUNK, CHUNK), 0)
        <= lax.broadcasted_iota(jnp.int32, (CHUNK, CHUNK), 1),
        1.0,
        0.0,
    ).astype(f32)
    ends = []
    for chunk in range(chunks):
        span = slice(chunk * CHUNK, (chunk + 1) * CHUNK)
        sums = jnp.dot(
            log_decay[:, span],
            upper,
            preferred_element_type=f32,
            precision=lax.Precision.HIGHEST,
        )
        down[chunk] = sums
        across[chunk] = sums - log_step[:, span]
        ends.append(sums[:, CHUNK - 1 :])
    total = jnp.zeros_like(ends[0])
    for chunk in range(chunks):
        staged[chunk] = jnp.broadcast_to(total, (heads, LANES))
        total = total + ends[chunk]
    staged[chunks] = jnp.broadcast_to(jnp.exp2(total), (heads, LANES))
    decay_out[...] = jnp.zeros_like(decay_out)
    for target in range(shards):
        for group in range(groups):
            for part in range(pieces):
                at = group * per_group + (target * piece + part * unit) // HDIM
                row = group * pieces + part
                decay_out[target, row : row + 1] = staged[chunks, at : at + 1]
    decay_in[tm] = decay_out[tm]
    pl.semaphore_wait(barrier, shards - 1)
    over_spots(lambda spot: decay_copy(spot).start())

    def project(which, target, first_column, count):
        slot = which % ring.shape[0]
        weight_load(which).wait()

        def part(at, carry):
            span = pl.ds(pl.multiple_of(at * block, block), block)
            made = jnp.dot(normed[span, :], ring[slot, :, :count], preferred_element_type=f32)
            wide = jnp.concatenate([scales[span, :]] * (count // LANES), axis=1)
            target[span, first_column : first_column + count] = (made * wide).astype(bf16)
            return carry

        lax.fori_loop(0, tokens // block, part, 0)
        if which + ring.shape[0] <= groups + 1:
            weight_load(which + ring.shape[0]).start()

    spread_narrow = spread(2 * per_group, HDIM, 2)
    spread_wide = spread(3 * per_group, CHUNK, 3)
    head_row = lax.broadcasted_iota(jnp.int32, (per_group, features), 0)
    head_lane = lax.broadcasted_iota(jnp.int32, (per_group, features), 1) // HDIM

    def widen(values):
        return lax.dot_general(
            split(values, 2), spread_narrow, CONTRACT_FIRST, preferred_element_type=f32
        )

    def widen_row(values):
        return jnp.sum(jnp.where(head_row == head_lane, values, 0.0), axis=0, keepdims=True)

    def at_group(group, chunk):
        own = slice(group * per_group, (group + 1) * per_group)
        return (
            pl.ds(pl.multiple_of(chunk * CHUNK, CHUNK), CHUNK),
            slice(group * features, (group + 1) * features),
            slice(group * STATE, (group + 1) * STATE),
            own,
        )

    def states(group):
        state[...] = jnp.zeros_like(state)

        def step(chunk, carry):
            span, lanes, keys, own = at_group(group, chunk)
            sums, shifted = down[chunk, own], across[chunk, own]
            end = sums[:, CHUNK - 1 :]
            held = state[...]
            saved[group, chunk] = held.astype(bf16)
            scaled = (inner[span, lanes].astype(f32) * widen(jnp.exp2(end - shifted))).astype(bf16)
            state[...] = held * widen_row(jnp.exp2(end)) + lax.dot_general(
                write[span, keys], scaled, CONTRACT_FIRST, preferred_element_type=f32
            )
            return carry

        lax.fori_loop(0, chunks, step, 0, unroll=math.gcd(chunks, 3))
        batch, inside = group // batch_groups, group % batch_groups
        sideways = state[...].T.astype(bf16)
        for target in range(shards):
            state_out[batch, target, inside * piece : (inside + 1) * piece] = sideways[
                target * piece : (target + 1) * piece
            ]

    def send_first(batch):
        state_in[batch, tm] = state_out[batch, tm]
        over_spots(lambda spot: first_copy(batch, spot).start())

    def send_second(batch):
        if batch == 0:
            over_spots(lambda spot: decay_copy(spot).wait_recv())
        over_spots(lambda spot: first_copy(batch, spot).wait_recv())
        for inside in range(batch_groups):
            group = batch * batch_groups + inside
            for part in range(pieces):
                span = slice(inside * piece + part * unit, inside * piece + (part + 1) * unit)
                row = group * pieces + part
                current = jnp.zeros((unit, STATE), f32)
                for shard in range(shards):
                    before[batch, shard, span] = current.astype(bf16)
                    current = decay_in[shard, row : row + 1] * current + state_in[
                        batch, shard, span
                    ].astype(f32)
        incoming[batch, tm] = before[batch, tm]
        over_spots(lambda spot: second_copy(batch, spot).start())

    causal = lax.broadcasted_iota(jnp.int32, (CHUNK, CHUNK), 0) >= lax.broadcasted_iota(
        jnp.int32, (CHUNK, CHUNK), 1
    )
    lane = lax.broadcasted_iota(jnp.int32, (CHUNK, LANES), 1)
    skip_column = column(skip_ref[...])

    def local(group):
        skip = widen_row(skip_column[group * per_group : (group + 1) * per_group])

        def step(chunk, carry):
            span, lanes, keys, own = at_group(group, chunk)
            sums, shifted = down[chunk, own], across[chunk, own]
            readers = read[span, keys]
            crossing = lax.dot_general(
                readers, write[span, keys], CONTRACT_LAST, preferred_element_type=f32
            )
            crossing = jnp.where(causal, crossing, 0.0)
            downs = lax.dot_general(
                split(sums, 3), spread_wide, CONTRACT_FIRST, preferred_element_type=f32
            )
            grown = widen(jnp.exp2(sums))
            carried = jnp.dot(readers, saved[group, chunk], preferred_element_type=f32)
            for pair in range(features // LANES):
                at = slice(pair * LANES, (pair + 1) * LANES)
                here = slice(lanes.start + pair * LANES, lanes.start + (pair + 1) * LANES)
                values = inner[span, here]
                halves = []
                for one in (2 * pair, 2 * pair + 1):
                    spans = downs[:, one * CHUNK : (one + 1) * CHUNK] - shifted[one : one + 1]
                    halves.append((crossing * jnp.exp2(jnp.minimum(spans, 100.0))).astype(bf16))
                wide = values.astype(f32)
                stacked = jnp.concatenate(
                    [jnp.where(lane < HDIM, wide, 0.0), jnp.where(lane < HDIM, 0.0, wide)], axis=0
                ).astype(bf16)
                within = jnp.dot(
                    jnp.concatenate(halves, axis=1), stacked, preferred_element_type=f32
                )
                local_out[span, here] = within + carried[:, at] * grown[:, at] + skip[:, at] * wide
            return carry

        lax.fori_loop(0, chunks, step, 0, unroll=math.gcd(chunks, 3))

    def finish(group):
        batch, inside = group // batch_groups, group % batch_groups
        held = jnp.concatenate(
            [
                incoming[batch, shard, inside * piece : (inside + 1) * piece]
                for shard in range(shards)
            ],
            axis=0,
        )

        def step(chunk, carry):
            span, lanes, keys, own = at_group(group, chunk)
            grown = widen(jnp.exp2(down[chunk, own] + staged[chunk, own]))
            carried = lax.dot_general(
                read[span, keys], held, CONTRACT_LAST, preferred_element_type=f32
            )
            summed = local_out[span, lanes] + carried * grown
            mean = jnp.sum(summed * summed, axis=1, keepdims=True) / features
            result[span, lanes] = (
                summed * lax.rsqrt(mean + 1e-05) * out_gain_ref[:, lanes]
            ).astype(bf16)
            return carry

        lax.fori_loop(0, chunks, step, 0, unroll=math.gcd(chunks, 3))

    def out_copy(group):
        lanes = slice(group * features, (group + 1) * features)
        return pltpu.make_async_copy(
            result.at[:, lanes], out_hbm.at[:, lanes], out_sem.at[group]
        )

    project(0, write, 0, groups * STATE)
    for group in range(groups):
        project(group + 1, inner, group * features, features)
        states(group)
        if (group + 1) % batch_groups == 0:
            send_first(group // batch_groups)
    if batches > 1:
        send_second(0)
    project(groups + 1, read, 0, groups * STATE)
    for group in range(groups):
        if group == groups // 2:
            send_second(batches - 1)
        local(group)
    for group in range(groups):
        if group % batch_groups == 0:
            batch = group // batch_groups
            over_spots(lambda spot: second_copy(batch, spot).wait_recv())
        finish(group)
        out_copy(group).start()
    over_spots(lambda spot: decay_copy(spot).wait_send())
    for batch in range(batches):
        over_spots(lambda spot: first_copy(batch, spot).wait_send())
        over_spots(lambda spot: second_copy(batch, spot).wait_send())
    for group in range(groups):
        out_copy(group).wait()


def mix(normed, squares, w_x, w_b, w_c, w_dt, dt_bias, a_log, d_skip, out_gain, shards):
    tokens = normed.shape[0]
    heads = w_dt.shape[1]
    groups = w_b.shape[1] // STATE
    features = heads // groups * HDIM
    chunks = tokens // CHUNK
    batches = math.gcd(groups, 2)
    piece = features // shards
    slice_rows = groups // batches * piece
    pieces = max(piece // HDIM, 1)
    decay_rows = -(-groups * pieces // 8) * 8
    in_vmem = pl.BlockSpec(memory_space=VMEM)
    in_hbm = pl.BlockSpec(memory_space=pl.ANY)
    dma = pltpu.SemaphoreType.DMA
    shape = jax.ShapeDtypeStruct((tokens, heads * HDIM), bf16)
    row = lambda member: member.reshape(1, -1)
    return pl.pallas_call(
        mix_kernel,
        out_shape=shape,
        in_specs=[in_vmem] * 6 + [in_hbm] * 4,
        out_specs=in_hbm,
        scratch_shapes=[
            VMEM(normed.shape, bf16),
            VMEM((tokens, LANES), f32),
            VMEM((min(3, groups + 2), w_x.shape[0], features), bf16),
            VMEM((tokens, heads * HDIM), bf16),
            VMEM((tokens, groups * STATE), bf16),
            VMEM((tokens, groups * STATE), bf16),
            VMEM((tokens, heads * HDIM), bf16),
            VMEM((tokens, heads * HDIM), f32),
            VMEM((chunks + 1, heads, LANES), f32),
            VMEM((chunks, heads, CHUNK), f32),
            VMEM((chunks, heads, CHUNK), f32),
            VMEM((STATE, features), f32),
            VMEM((groups, chunks, STATE, features), bf16),
            VMEM((batches, shards, slice_rows, STATE), bf16),
            VMEM((batches, shards, slice_rows, STATE), bf16),
            VMEM((batches, shards, slice_rows, STATE), bf16),
            VMEM((batches, shards, slice_rows, STATE), bf16),
            VMEM((shards, decay_rows, LANES), f32),
            VMEM((shards, decay_rows, LANES), f32),
            dma(()),
            dma((min(3, groups + 2),)),
            dma((groups,)),
            dma((shards,)),
            dma((shards,)),
            dma((batches, shards)),
            dma((batches, shards)),
            dma((batches, shards)),
            dma((batches, shards)),
        ],
        compiler_params=pltpu.CompilerParams(
            collective_id=1, has_side_effects=True, vmem_limit_bytes=50 << 20
        ),
        name="mix",
    )(
        squares,
        w_dt.T,
        row(dt_bias),
        row(a_log),
        row(d_skip),
        row(out_gain),
        normed,
        w_x,
        w_b,
        w_c,
    )


def on_device(
    patches,
    grid_rows,
    frame_ids,
    ln_gain,
    w_qkv,
    w_out,
    w_conn,
    norm_gain,
    w_x,
    w_b,
    w_c,
    w_dt,
    dt_bias,
    a_log,
    d_skip,
    out_gain,
):
    part_width = patches.shape[2]
    shards = lax.axis_size("tm")
    my = lax.axis_index("head").astype(jnp.int32).reshape(1)
    parts = lax.axis_size("head")
    all_conn = lax.all_gather(w_conn, "head")
    order, valid, rank, label = routes(frame_ids, grid_rows, shards)
    arrived = vision(
        patches.swapaxes(1, 2),
        order,
        valid,
        rank,
        label,
        ln_gain.reshape(1, -1),
        w_qkv.swapaxes(1, 2),
        w_out,
        parts,
        shards,
    )
    features = w_dt.shape[1] // (w_b.shape[1] // STATE) * HDIM
    stream, normed, squares = connect(arrived, frame_ids.shape[0], all_conn, norm_gain, features)
    return stream, mix(
        normed, squares, w_x, w_b, w_c, w_dt, dt_bias, a_log, d_skip, out_gain, shards)


def solution(mesh):
    in_specs = (
        P("tm", None, "head"),
        P("tm"),
        P("tm"),
        P(),
        P(None, None, "head"),
        P("head", None),
        P(None, "head"),
        P(),
        P(None, "head"),
        P(None, "head"),
        P(None, "head"),
        P(None, "head"),
        P("head"),
        P("head"),
        P("head"),
        P("head"),
    )
    out_specs = (P("tm", "head"), P("tm", "head"))
    return jax.shard_map(
        on_device, mesh=mesh, in_specs=in_specs, out_specs=out_specs, check_vma=False
    )
```

```python
import math

import jax
import jax.numpy as jnp
from jax import lax
from jax.experimental import pallas as pl
from jax.experimental.pallas import tpu as pltpu
from jax.sharding import PartitionSpec as P

GRID = 16
POOL = 4
VHD = 72
HDIM = 64
STATE = 128
CHUNK = 128
LANES = 128

f32 = jnp.float32
bf16 = jnp.bfloat16
VMEM = pltpu.VMEM
MESH = pl.DeviceIdType.MESH
CONTRACT_LAST = (((1,), (1,)), ((), ()))
CONTRACT_FIRST = (((0,), (0,)), ((), ()))


def flipped(index, mask, count):
    result, bit = 0, 1
    while bit < count:
        result = result + bit * ((index // bit + mask // bit) % 2)
        bit *= 2
    return result


def partners(index, spot, count):
    if count & (count - 1):
        return (index + spot + 1) % count, (index + 2 * count - spot - 1) % count
    other = flipped(index, count - 1 - spot, count)
    return other, other


def vision_kernel(
    order_ref,
    valid_ref,
    rank_ref,
    label_ref,
    patches_ref,
    gain_ref,
    wqkv_hbm,
    wout_hbm,
    out_ref,
    labels,
    wqkv_ref,
    wout_ref,
    label_out,
    full,
    gain,
    normed,
    qkv,
    context,
    partial,
    partial_in,
    mine,
    pooled_frames,
    outbox,
    weight_sem,
    label_send,
    label_recv,
    patch_send,
    patch_recv,
    partial_send,
    partial_recv,
    frame_send,
    frame_recv,
    forward_send,
    forward_recv,
):
    parts, frames, part_width, patch_count = full.shape
    shards = out_ref.shape[1]
    width = parts * part_width
    local_width = wqkv_ref.shape[1]
    heads = local_width // VHD
    tokens = patch_count // POOL
    batch = normed.shape[1] // patch_count
    fold = out_ref.shape[3] // part_width
    lines = tokens // fold
    factor = VHD ** (-0.5) * math.log2(math.e)
    tm, head = lax.axis_index("tm"), lax.axis_index("head")
    peers = [(head + step) % parts for step in range(1, parts)]
    sources = [(head + parts - step) % parts for step in range(1, parts)]

    def remote(source, target, send, recv, to):
        return pltpu.make_async_remote_copy(
            src_ref=source,
            dst_ref=target,
            send_sem=send,
            recv_sem=recv,
            device_id=to,
            device_id_type=MESH,
        )

    def patch_copy(step, rank, part):
        return remote(
            full.at[part, rank],
            full.at[part, rank],
            patch_send.at[step, rank],
            patch_recv.at[step, rank],
            (tm, peers[step]),
        )

    def partial_copy(step, rank):
        return remote(
            partial.at[rank, peers[step]],
            partial_in.at[rank, step],
            partial_send.at[step, rank],
            partial_recv.at[step, rank],
            (tm, peers[step]),
        )

    def frame_copy(spot):
        return remote(
            outbox.at[spot],
            out_ref.at[head, spot],
            frame_send.at[spot],
            frame_recv.at[spot],
            (partners(tm, spot, shards)[0], head),
        )

    def label_copy(spot):
        return remote(
            label_out.at[spot],
            labels.at[spot],
            label_send.at[spot],
            label_recv.at[spot],
            (partners(tm, spot, shards)[0], head),
        )

    def forward_copy(step, spot, part):
        return remote(
            out_ref.at[part, spot],
            out_ref.at[part, spot],
            forward_send.at[step, spot],
            forward_recv.at[step, spot],
            (tm, peers[step]),
        )

    qkv_load = pltpu.make_async_copy(wqkv_hbm, wqkv_ref, weight_sem.at[0])
    out_load = pltpu.make_async_copy(wout_hbm, wout_ref, weight_sem.at[1])
    qkv_load.start()
    out_load.start()
    barrier = pltpu.get_barrier_semaphore()
    for peer in peers:
        pl.semaphore_signal(barrier, inc=1, device_id=(tm, peer), device_id_type=MESH)

    def greet(spot, carry):
        pl.semaphore_signal(
            barrier,
            inc=1,
            device_id=(partners(tm, spot, shards)[1], head),
            device_id_type=MESH,
        )
        return carry

    lax.fori_loop(0, shards - 1, greet, 0)

    def stage(rank, carry):
        full[head, rank] = patches_ref[order_ref[rank]]
        return carry

    lax.fori_loop(0, frames, stage, 0)
    for first in range(0, width, LANES):
        tile = jnp.broadcast_to(gain_ref[:, first : first + LANES], (LANES, LANES))
        gain[first : first + LANES] = tile.T
    pl.semaphore_wait(barrier, parts - 1 + shards - 1)

    def share(rank, carry):
        for step in range(parts - 1):
            patch_copy(step, rank, head).start()
        return carry

    lax.fori_loop(0, frames, share, 0)

    def name(spot, carry):
        label_out[spot] = jnp.full(label_out.shape[1:], label_ref[spot].astype(f32))
        label_copy(spot).start()
        return carry

    lax.fori_loop(0, shards - 1, name, 0)
    labels[shards - 1] = jnp.full(label_out.shape[1:], label_ref[shards - 1].astype(f32))

    def normalise(rank, columns):
        total = 0.0
        for part in range(parts):
            total = total + jnp.sum(full[part, rank].astype(f32), axis=0, keepdims=True)
        centre = total / width
        spread = 0.0
        for part in range(parts):
            moved = full[part, rank].astype(f32) - centre
            spread = spread + jnp.sum(moved * moved, axis=0, keepdims=True)
        scale = lax.rsqrt(spread / width + 1e-06)
        for part in range(parts):
            rows = slice(part * part_width, (part + 1) * part_width)
            wide = jnp.concatenate([gain[rows]] * (patch_count // LANES), axis=1)
            normed[rows, columns] = (
                (full[part, rank].astype(f32) - centre) * scale * wide
            ).astype(bf16)

    spot_row = lax.broadcasted_iota(jnp.int32, (8, patch_count), 0)
    spot_key = lax.broadcasted_iota(jnp.int32, (8, patch_count), 1)
    ones_row = jnp.where(spot_row == 0, 1.0, 0.0).astype(f32)

    def extended(member, head_id, columns, extra):
        rows = slice(head_id * VHD, (head_id + 1) * VHD)
        return jnp.concatenate([qkv[member, rows, columns], extra], axis=0).astype(bf16)

    def score(head_id, columns, key_row):
        return lax.dot_general(
            extended(1, head_id, columns, key_row),
            extended(0, head_id, columns, ones_row),
            CONTRACT_FIRST,
            preferred_element_type=f32,
        )

    def mix(head_id, columns, scores):
        powered = jnp.exp2((scores - jnp.max(scores, axis=0, keepdims=True)) * factor)
        mixed = jnp.dot(
            extended(2, head_id, columns, ones_row),
            powered.astype(bf16),
            preferred_element_type=f32,
        )
        context[head_id * VHD : (head_id + 1) * VHD, columns] = mixed[:VHD] * (
            1.0 / mixed[VHD : VHD + 1]
        )

    pool_row = lax.broadcasted_iota(jnp.int32, (tokens, patch_count), 0)
    pool_column = lax.broadcasted_iota(jnp.int32, (tokens, patch_count), 1)
    pooling = jnp.where(pool_column // POOL == pool_row, 1.0 / POOL, 0.0).astype(bf16)
    token_spot = lax.broadcasted_iota(jnp.int32, (tokens, part_width), 0) * POOL
    spans = [slice(b * patch_count, (b + 1) * patch_count) for b in range(batch)]

    def post(spot):
        outbox[spot] = pooled_frames[rank_ref[spot]]

    def settle(rank):
        for step in range(parts - 1):
            partial_copy(step, rank).wait_recv()
        total = mine[rank]
        for step in range(parts - 1):
            total = total + partial_in[rank, step].astype(f32)
        total = jnp.where(token_spot < valid_ref[rank], total, 0.0).astype(bf16)
        for at in range(fold):
            pooled_frames[rank, :, at * part_width : (at + 1) * part_width] = total[
                at * lines : (at + 1) * lines
            ]
        post(rank)
        frame_copy(rank).start()

    def forward(spot):
        frame_copy(spot).wait_recv()
        for step in range(parts - 1):
            forward_copy(step, spot, head).start()

    def body(turn, carry):
        ranks = [turn * batch + b for b in range(batch)]
        for rank, span in zip(ranks, spans):
            for step in range(parts - 1):
                patch_copy(step, rank, sources[step]).wait_recv()
            normalise(rank, span)

        @pl.when(turn >= 1)
        def _():
            for b in range(batch):
                settle((turn - 1) * batch + b)

        @pl.when(turn == 0)
        def _():
            qkv_load.wait()
            out_load.wait()

        for member in range(3):
            qkv[member] = jnp.dot(wqkv_ref[member], normed[...], preferred_element_type=f32)

        @pl.when(turn >= 3)
        def _():
            for b in range(batch):
                forward((turn - 3) * batch + b)

        key_rows = [
            jnp.where((spot_row == 0) & (spot_key >= valid_ref[rank]), -1e30, 0.0).astype(f32)
            for rank in ranks
        ]
        todo = [(head_id, b) for head_id in range(heads) for b in range(batch)]
        ahead = 4
        ready = [score(h, spans[b], key_rows[b]) for h, b in todo[:ahead]]
        for at, (h, b) in enumerate(todo):
            if at + ahead < len(todo):
                later, which = todo[at + ahead]
                ready.append(score(later, spans[which], key_rows[which]))
            mix(h, spans[b], ready[at])
        pooled = jnp.concatenate(
            [
                lax.dot_general(
                    pooling,
                    context[:, span].astype(bf16),
                    CONTRACT_LAST,
                    preferred_element_type=f32,
                ).astype(bf16)
                for span in spans
            ],
            axis=0,
        )
        attended = jnp.dot(pooled, wout_ref[...], preferred_element_type=f32)
        for b, rank in enumerate(ranks):
            own = lax.dot_general(
                pooling, full[head, rank], CONTRACT_LAST, preferred_element_type=f32
            )
            for part in range(parts):
                block = attended[
                    b * tokens : (b + 1) * tokens, part * part_width : (part + 1) * part_width
                ]
                partial[rank, part] = block.astype(bf16)
                own = own + jnp.where(head == part, block, 0.0)
            mine[rank] = own
            for step in range(parts - 1):
                partial_copy(step, rank).start()
        return carry

    turns = frames // batch
    lax.fori_loop(0, turns, body, 0)
    for rank in range(frames - batch, frames):
        settle(rank)
    for spot in range(frames, shards):
        post(spot)
        if spot < shards - 1:
            frame_copy(spot).start()
    out_ref[head, shards - 1] = outbox[shards - 1]
    for step in range(parts - 1):
        forward_copy(step, shards - 1, head).start()

    def late_forward(spot, carry):
        forward(spot)
        return carry

    lax.fori_loop(max(turns - 3, 0) * batch, shards - 1, late_forward, 0)

    def drain_ranks(rank, carry):
        for step in range(parts - 1):
            patch_copy(step, rank, head).wait_send()
            partial_copy(step, rank).wait_send()
        return carry

    lax.fori_loop(0, frames, drain_ranks, 0)

    def drain_frames(spot, carry):
        frame_copy(spot).wait_send()
        label_copy(spot).wait()
        return carry

    lax.fori_loop(0, shards - 1, drain_frames, 0)

    def drain_forwards(spot, carry):
        for step in range(parts - 1):
            forward_copy(step, spot, sources[step]).wait_recv()
            forward_copy(step, spot, head).wait_send()
        return carry

    lax.fori_loop(0, shards, drain_forwards, 0)


def vision(patches, order, valid, rank, label, gain, w_qkv, w_out, parts, shards):
    frames, part_width, patch_count = patches.shape
    width = parts * part_width
    local_width = w_qkv.shape[1]
    tokens = patch_count // POOL
    batch = math.gcd(frames, 2)
    in_smem = pl.BlockSpec(memory_space=pltpu.SMEM)
    in_vmem = pl.BlockSpec(memory_space=VMEM)
    in_hbm = pl.BlockSpec(memory_space=pl.ANY)
    peers = parts - 1
    fold = 2 if part_width % LANES == LANES // 2 and tokens % 32 == 0 else 1
    lines = (tokens // fold, part_width * fold)
    dma = pltpu.SemaphoreType.DMA
    return pl.pallas_call(
        vision_kernel,
        out_shape=(
            jax.ShapeDtypeStruct((parts, shards) + lines, bf16),
            jax.ShapeDtypeStruct((shards, 8, LANES), f32),
        ),
        in_specs=[in_smem] * 4 + [in_vmem] * 2 + [in_hbm] * 2,
        out_specs=(in_vmem, in_vmem),
        scratch_shapes=[
            VMEM(w_qkv.shape, bf16),
            VMEM(w_out.shape, bf16),
            VMEM((shards, 8, LANES), f32),
            VMEM((parts, frames, part_width, patch_count), bf16),
            VMEM((width, LANES), f32),
            VMEM((width, batch * patch_count), bf16),
            VMEM((3, local_width, batch * patch_count), f32),
            VMEM((local_width, batch * patch_count), f32),
            VMEM((frames, parts, tokens, part_width), bf16),
            VMEM((frames, peers, tokens, part_width), bf16),
            VMEM((frames, tokens, part_width), f32),
            VMEM((frames,) + lines, bf16),
            VMEM((shards,) + lines, bf16),
            dma((2,)),
            dma((shards,)),
            dma((shards,)),
            dma((peers, frames)),
            dma((peers, frames)),
            dma((peers, frames)),
            dma((peers, frames)),
            dma((shards,)),
            dma((shards,)),
            dma((peers, shards)),
            dma((peers, shards)),
        ],
        compiler_params=pltpu.CompilerParams(
            collective_id=0, has_side_effects=True, vmem_limit_bytes=56 << 20
        ),
        cost_estimate=pl.CostEstimate(
            flops=frames * patch_count * width * local_width * 10,
            bytes_accessed=12_000_000,
            transcendentals=4_000_000,
        ),
        name="vision",
    )(order, valid, rank, label, patches, gain, w_qkv, w_out)


def routes(frame_ids, grid_rows, shards):
    frames = frame_ids.shape[0]
    tm = lax.axis_index("tm").astype(jnp.int32)
    spots = jnp.arange(shards, dtype=jnp.int32)
    targets = partners(tm, spots, shards)[0]
    slots = jnp.arange(frames, dtype=jnp.int32)
    total = lambda chosen, member, axis: jnp.sum(
        jnp.where(chosen, member, 0), axis=axis
    ).astype(jnp.int32)
    goes = (frame_ids // frames)[:, None] == targets[None, :]
    spot_of = total(goes, spots[None, :], 1)
    rank_of = jnp.sum(spot_of[None, :] < spot_of[:, None], axis=1).astype(jnp.int32)
    holds = rank_of[None, :] == slots[:, None]
    order = total(holds, slots[None, :], 1)
    valid = total(holds, (grid_rows * GRID)[None, :], 1)
    rank = total(goes, rank_of[:, None], 0)
    label = total(goes, (frame_ids % frames + 1)[:, None], 0)
    return order, valid, rank, label


def spread(rows, width, copies):
    heads = rows // copies
    row = lax.broadcasted_iota(jnp.int32, (rows, heads * width), 0) % heads
    block = lax.broadcasted_iota(jnp.int32, (rows, heads * width), 1) // width
    return jnp.where(row == block, 1.0, 0.0).astype(bf16)


def split(values, copies):
    terms = []
    for _ in range(copies):
        terms.append(values.astype(bf16).astype(f32))
        values = values - terms[-1]
    return jnp.concatenate(terms, axis=0).astype(bf16)


def column(row):
    count = row.shape[1]
    same = lax.broadcasted_iota(jnp.int32, (count, count), 0) == lax.broadcasted_iota(
        jnp.int32, (count, count), 1
    )
    return jnp.sum(jnp.where(same, row, 0.0), axis=1, keepdims=True)


def connect_kernel(
    arrived_hbm,
    labels,
    norm_gain_ref,
    conn_hbm,
    stream_hbm,
    normed_hbm,
    squares,
    arrived_ref,
    conn,
    rows,
    gained,
    result,
    sender_ref,
    arrived_sem,
    conn_sem,
    normed_sem,
    stream_sem,
):
    parts, shards, lines, folded = arrived_ref.shape
    tokens = rows.shape[0]
    conn_count, width, conn_width = conn.shape
    part_width = width // parts
    per_part = conn_count // parts
    fold = folded // part_width
    frame_tokens = lines * fold
    frames = tokens // frame_tokens
    head = lax.axis_index("head")
    arrived_copy = pltpu.make_async_copy(arrived_hbm, arrived_ref, arrived_sem)
    arrived_copy.start()

    def conn_load(at):
        return pltpu.make_async_copy(
            conn_hbm.at[
                at // per_part,
                :,
                pl.ds(pl.multiple_of((at % per_part) * conn_width, conn_width), conn_width),
            ],
            conn.at[at],
            conn_sem.at[at],
        )

    def conn_start(at, carry):
        conn_load(at).start()
        return carry

    lax.fori_loop(0, conn_count, conn_start, 0)
    for shard in range(shards):
        sender_ref[jnp.max(labels[shard]).astype(jnp.int32)] = shard
    arrived_copy.wait()

    def gather(frame, carry):
        for at in range(fold):
            first = pl.multiple_of(frame * frame_tokens + at * lines, lines)
            for part in range(parts):
                rows[pl.ds(first, lines), part * part_width : (part + 1) * part_width] = (
                    arrived_ref[
                        part,
                        sender_ref[frame + 1],
                        :,
                        at * part_width : (at + 1) * part_width,
                    ]
                )
        return carry

    lax.fori_loop(0, frames, gather, 0)
    squares[...] = jnp.zeros_like(squares)

    def normed_copy(at):
        columns = pl.ds(pl.multiple_of(at * conn_width, conn_width), conn_width)
        return pltpu.make_async_copy(gained.at[at], normed_hbm.at[:, columns], normed_sem.at[at])

    def connect(at, carry):
        conn_load(at).wait()
        columns = pl.ds(pl.multiple_of(at * conn_width, conn_width), conn_width)
        mine = pl.ds(
            pl.multiple_of((at % per_part) * conn_width, conn_width), conn_width
        )
        made = jnp.dot(rows[...], conn[at], preferred_element_type=f32).astype(bf16)

        @pl.when(at // per_part == head)
        def _():
            result[:, mine] = made

        made = made.astype(f32)
        gained[at] = (made * norm_gain_ref[:, columns]).astype(bf16)
        normed_copy(at).start()
        made = made * made
        squares[...] += sum(
            made[:, lane : lane + LANES] for lane in range(0, conn_width, LANES)
        )
        return carry

    lax.fori_loop(0, conn_count, connect, 0)
    stream_copy = pltpu.make_async_copy(result, stream_hbm, stream_sem)
    stream_copy.start()

    def drain(at, carry):
        normed_copy(at).wait()
        return carry

    lax.fori_loop(0, conn_count, drain, 0)
    stream_copy.wait()


def connect(arrived, labels, frames, weights, norm_gain, features):
    parts, _, lines, folded = arrived.shape
    _, width, columns = weights.shape
    tokens = frames * lines * (folded * parts // width)
    full_width = parts * columns
    conn_width = math.gcd(columns, features)
    conn_count = full_width // conn_width
    in_vmem = pl.BlockSpec(memory_space=VMEM)
    in_hbm = pl.BlockSpec(memory_space=pl.ANY)
    return pl.pallas_call(
        connect_kernel,
        out_shape=(
            jax.ShapeDtypeStruct((tokens, columns), bf16),
            jax.ShapeDtypeStruct((tokens, full_width), bf16),
            jax.ShapeDtypeStruct((tokens, LANES), f32),
        ),
        in_specs=[in_hbm, in_vmem, in_vmem, in_hbm],
        out_specs=(in_hbm, in_hbm, in_vmem),
        scratch_shapes=[
            VMEM(arrived.shape, bf16),
            VMEM((conn_count, width, conn_width), bf16),
            VMEM((tokens, width), bf16),
            VMEM((conn_count, tokens, conn_width), bf16),
            VMEM((tokens, columns), bf16),
            pltpu.SMEM((frames + 1,), jnp.int32),
            pltpu.SemaphoreType.DMA(()),
            pltpu.SemaphoreType.DMA((conn_count,)),
            pltpu.SemaphoreType.DMA((conn_count,)),
            pltpu.SemaphoreType.DMA(()),
        ],
        compiler_params=pltpu.CompilerParams(vmem_limit_bytes=60 << 20),
        name="connect",
    )(arrived, labels, norm_gain.reshape(1, -1), weights)


def mix_kernel(
    squares_ref,
    wdt_ref,
    bias_ref,
    alog_ref,
    skip_ref,
    out_gain_ref,
    normed_hbm,
    wx_hbm,
    wb_hbm,
    wc_hbm,
    out_hbm,
    normed,
    scales,
    ring,
    inner,
    write,
    read,
    result,
    local_out,
    staged,
    down,
    across,
    state,
    saved,
    state_out,
    state_in,
    before,
    incoming,
    decay_out,
    decay_in,
    normed_sem,
    ring_sem,
    out_sem,
    decay_send,
    decay_recv,
    first_send,
    first_recv,
    second_send,
    second_recv,
):
    tokens, full_width = normed.shape
    heads = wdt_ref.shape[0]
    groups = write.shape[1] // STATE
    per_group = heads // groups
    features = per_group * HDIM
    chunks = tokens // CHUNK
    block = 2 * CHUNK
    batches, shards, slice_rows, _ = state_in.shape
    batch_groups = groups // batches
    piece = features // shards
    unit = min(piece, HDIM)
    pieces = piece // unit
    tm, head = lax.axis_index("tm"), lax.axis_index("head")
    log2e = math.log2(math.e)

    def remote(source, target, send, recv, spot):
        return pltpu.make_async_remote_copy(
            src_ref=source,
            dst_ref=target,
            send_sem=send,
            recv_sem=recv,
            device_id=(partners(tm, spot, shards)[0], head),
            device_id_type=MESH,
        )

    def target_of(spot):
        return partners(tm, spot, shards)[0]

    def decay_copy(spot):
        return remote(
            decay_out.at[target_of(spot)],
            decay_in.at[tm],
            decay_send.at[spot],
            decay_recv.at[spot],
            spot,
        )

    def first_copy(batch, spot):
        return remote(
            state_out.at[batch, target_of(spot)],
            state_in.at[batch, tm],
            first_send.at[batch, spot],
            first_recv.at[batch, spot],
            spot,
        )

    def second_copy(batch, spot):
        return remote(
            before.at[batch, target_of(spot)],
            incoming.at[batch, tm],
            second_send.at[batch, spot],
            second_recv.at[batch, spot],
            spot,
        )

    def over_spots(act):
        def step(spot, carry):
            act(spot)
            return carry

        lax.fori_loop(0, shards - 1, step, 0)

    barrier = pltpu.get_barrier_semaphore()
    over_spots(
        lambda spot: pl.semaphore_signal(
            barrier,
            inc=1,
            device_id=(partners(tm, spot, shards)[1], head),
            device_id_type=MESH,
        )
    )

    def weight_load(which):
        slot = which % ring.shape[0]
        if which == 0 or which == groups + 1:
            source = wb_hbm if which == 0 else wc_hbm
            target = ring.at[slot, :, : groups * STATE]
        else:
            source = wx_hbm.at[:, (which - 1) * features : which * features]
            target = ring.at[slot]
        return pltpu.make_async_copy(source, target, ring_sem.at[slot])

    normed_copy = pltpu.make_async_copy(normed_hbm, normed, normed_sem)
    normed_copy.start()
    for which in range(ring.shape[0]):
        weight_load(which).start()
    mean = jnp.sum(squares_ref[...], axis=1, keepdims=True) / full_width
    scales[...] = jnp.broadcast_to(lax.rsqrt(mean + 1e-05), scales.shape)
    mean_row = lax.dot_general(
        jnp.ones((8, LANES), f32),
        squares_ref[...],
        CONTRACT_LAST,
        preferred_element_type=f32,
        precision=lax.Precision.HIGHEST,
    )
    scale_row = lax.rsqrt(mean_row[:1] / full_width + 1e-05)
    normed_copy.wait()

    raw = lax.dot_general(wdt_ref[...], normed[...], CONTRACT_LAST, preferred_element_type=f32)
    raw = raw * scale_row + column(bias_ref[...])
    step_size = jnp.maximum(raw, 0.0) + jnp.log1p(jnp.exp(-jnp.abs(raw)))
    rate = -jnp.exp(column(alog_ref[...])) * log2e
    log_decay = step_size * rate
    log_step = jnp.log(step_size) * log2e
    upper = jnp.where(
        lax.broadcasted_iota(jnp.int32, (CHUNK, CHUNK), 0)
        <= lax.broadcasted_iota(jnp.int32, (CHUNK, CHUNK), 1),
        1.0,
        0.0,
    ).astype(f32)
    ends = []
    for chunk in range(chunks):
        span = slice(chunk * CHUNK, (chunk + 1) * CHUNK)
        sums = jnp.dot(
            log_decay[:, span],
            upper,
            preferred_element_type=f32,
            precision=lax.Precision.HIGHEST,
        )
        down[chunk] = sums
        across[chunk] = sums - log_step[:, span]
        ends.append(sums[:, CHUNK - 1 :])
    total = jnp.zeros_like(ends[0])
    for chunk in range(chunks):
        staged[chunk] = jnp.broadcast_to(total, (heads, LANES))
        total = total + ends[chunk]
    staged[chunks] = jnp.broadcast_to(jnp.exp2(total), (heads, LANES))
    decay_out[...] = jnp.zeros_like(decay_out)
    for target in range(shards):
        for group in range(groups):
            for part in range(pieces):
                at = group * per_group + (target * piece + part * unit) // HDIM
                row = group * pieces + part
                decay_out[target, row : row + 1] = staged[chunks, at : at + 1]
    decay_in[tm] = decay_out[tm]
    pl.semaphore_wait(barrier, shards - 1)
    over_spots(lambda spot: decay_copy(spot).start())

    def project(which, target, first_column, count):
        slot = which % ring.shape[0]
        weight_load(which).wait()

        def part(at, carry):
            span = pl.ds(pl.multiple_of(at * block, block), block)
            made = jnp.dot(normed[span, :], ring[slot, :, :count], preferred_element_type=f32)
            wide = jnp.concatenate([scales[span, :]] * (count // LANES), axis=1)
            target[span, first_column : first_column + count] = (made * wide).astype(bf16)
            return carry

        lax.fori_loop(0, tokens // block, part, 0)
        if which + ring.shape[0] <= groups + 1:
            weight_load(which + ring.shape[0]).start()

    spread_narrow = spread(2 * per_group, HDIM, 2)
    spread_wide = spread(3 * per_group, CHUNK, 3)
    head_row = lax.broadcasted_iota(jnp.int32, (per_group, features), 0)
    head_lane = lax.broadcasted_iota(jnp.int32, (per_group, features), 1) // HDIM

    def widen(values):
        return lax.dot_general(
            split(values, 2), spread_narrow, CONTRACT_FIRST, preferred_element_type=f32
        )

    def widen_row(values):
        return jnp.sum(jnp.where(head_row == head_lane, values, 0.0), axis=0, keepdims=True)

    def at_group(group, chunk):
        own = slice(group * per_group, (group + 1) * per_group)
        return (
            pl.ds(pl.multiple_of(chunk * CHUNK, CHUNK), CHUNK),
            slice(group * features, (group + 1) * features),
            slice(group * STATE, (group + 1) * STATE),
            own,
        )

    def states(group):
        state[...] = jnp.zeros_like(state)

        def step(chunk, carry):
            span, lanes, keys, own = at_group(group, chunk)
            sums, shifted = down[chunk, own], across[chunk, own]
            end = sums[:, CHUNK - 1 :]
            held = state[...]
            saved[group, chunk] = held.astype(bf16)
            scaled = (inner[span, lanes].astype(f32) * widen(jnp.exp2(end - shifted))).astype(bf16)
            state[...] = held * widen_row(jnp.exp2(end)) + lax.dot_general(
                write[span, keys], scaled, CONTRACT_FIRST, preferred_element_type=f32
            )
            return carry

        lax.fori_loop(0, chunks, step, 0, unroll=math.gcd(chunks, 3))
        batch, inside = group // batch_groups, group % batch_groups
        sideways = state[...].T.astype(bf16)
        for target in range(shards):
            state_out[batch, target, inside * piece : (inside + 1) * piece] = sideways[
                target * piece : (target + 1) * piece
            ]

    def send_first(batch):
        state_in[batch, tm] = state_out[batch, tm]
        over_spots(lambda spot: first_copy(batch, spot).start())

    def send_second(batch):
        if batch == 0:
            over_spots(lambda spot: decay_copy(spot).wait_recv())
        over_spots(lambda spot: first_copy(batch, spot).wait_recv())
        for inside in range(batch_groups):
            group = batch * batch_groups + inside
            for part in range(pieces):
                span = slice(inside * piece + part * unit, inside * piece + (part + 1) * unit)
                row = group * pieces + part
                current = jnp.zeros((unit, STATE), f32)
                for shard in range(shards):
                    before[batch, shard, span] = current.astype(bf16)
                    current = decay_in[shard, row : row + 1] * current + state_in[
                        batch, shard, span
                    ].astype(f32)
        incoming[batch, tm] = before[batch, tm]
        over_spots(lambda spot: second_copy(batch, spot).start())

    causal = lax.broadcasted_iota(jnp.int32, (CHUNK, CHUNK), 0) >= lax.broadcasted_iota(
        jnp.int32, (CHUNK, CHUNK), 1
    )
    lane = lax.broadcasted_iota(jnp.int32, (CHUNK, LANES), 1)
    skip_column = column(skip_ref[...])

    def local(group):
        skip = widen_row(skip_column[group * per_group : (group + 1) * per_group])

        def step(chunk, carry):
            span, lanes, keys, own = at_group(group, chunk)
            sums, shifted = down[chunk, own], across[chunk, own]
            readers = read[span, keys]
            crossing = lax.dot_general(
                readers, write[span, keys], CONTRACT_LAST, preferred_element_type=f32
            )
            crossing = jnp.where(causal, crossing, 0.0)
            downs = lax.dot_general(
                split(sums, 3), spread_wide, CONTRACT_FIRST, preferred_element_type=f32
            )
            grown = widen(jnp.exp2(sums))
            carried = jnp.dot(readers, saved[group, chunk], preferred_element_type=f32)
            for pair in range(features // LANES):
                at = slice(pair * LANES, (pair + 1) * LANES)
                here = slice(lanes.start + pair * LANES, lanes.start + (pair + 1) * LANES)
                values = inner[span, here]
                halves = []
                for one in (2 * pair, 2 * pair + 1):
                    spans = downs[:, one * CHUNK : (one + 1) * CHUNK] - shifted[one : one + 1]
                    halves.append((crossing * jnp.exp2(jnp.minimum(spans, 100.0))).astype(bf16))
                wide = values.astype(f32)
                stacked = jnp.concatenate(
                    [jnp.where(lane < HDIM, wide, 0.0), jnp.where(lane < HDIM, 0.0, wide)], axis=0
                ).astype(bf16)
                within = jnp.dot(
                    jnp.concatenate(halves, axis=1), stacked, preferred_element_type=f32
                )
                local_out[span, here] = within + carried[:, at] * grown[:, at] + skip[:, at] * wide
            return carry

        lax.fori_loop(0, chunks, step, 0, unroll=math.gcd(chunks, 3))

    def finish(group):
        batch, inside = group // batch_groups, group % batch_groups
        held = jnp.concatenate(
            [
                incoming[batch, shard, inside * piece : (inside + 1) * piece]
                for shard in range(shards)
            ],
            axis=0,
        )

        def step(chunk, carry):
            span, lanes, keys, own = at_group(group, chunk)
            grown = widen(jnp.exp2(down[chunk, own] + staged[chunk, own]))
            carried = lax.dot_general(
                read[span, keys], held, CONTRACT_LAST, preferred_element_type=f32
            )
            summed = local_out[span, lanes] + carried * grown
            mean = jnp.sum(summed * summed, axis=1, keepdims=True) / features
            result[span, lanes] = (
                summed * lax.rsqrt(mean + 1e-05) * out_gain_ref[:, lanes]
            ).astype(bf16)
            return carry

        lax.fori_loop(0, chunks, step, 0, unroll=math.gcd(chunks, 3))

    def out_copy(group):
        lanes = slice(group * features, (group + 1) * features)
        return pltpu.make_async_copy(
            result.at[:, lanes], out_hbm.at[:, lanes], out_sem.at[group]
        )

    project(0, write, 0, groups * STATE)
    for group in range(groups):
        project(group + 1, inner, group * features, features)
        states(group)
        if (group + 1) % batch_groups == 0:
            send_first(group // batch_groups)
    if batches > 1:
        send_second(0)
    project(groups + 1, read, 0, groups * STATE)
    for group in range(groups):
        if group == groups // 2:
            send_second(batches - 1)
        local(group)
    for group in range(groups):
        if group % batch_groups == 0:
            batch = group // batch_groups
            over_spots(lambda spot: second_copy(batch, spot).wait_recv())
        finish(group)
        out_copy(group).start()
    over_spots(lambda spot: decay_copy(spot).wait_send())
    for batch in range(batches):
        over_spots(lambda spot: first_copy(batch, spot).wait_send())
        over_spots(lambda spot: second_copy(batch, spot).wait_send())
    for group in range(groups):
        out_copy(group).wait()


def mix(normed, squares, w_x, w_b, w_c, w_dt, dt_bias, a_log, d_skip, out_gain, shards):
    tokens = normed.shape[0]
    heads = w_dt.shape[1]
    groups = w_b.shape[1] // STATE
    features = heads // groups * HDIM
    chunks = tokens // CHUNK
    batches = math.gcd(groups, 2)
    piece = features // shards
    slice_rows = groups // batches * piece
    pieces = max(piece // HDIM, 1)
    decay_rows = -(-groups * pieces // 8) * 8
    in_vmem = pl.BlockSpec(memory_space=VMEM)
    in_hbm = pl.BlockSpec(memory_space=pl.ANY)
    dma = pltpu.SemaphoreType.DMA
    shape = jax.ShapeDtypeStruct((tokens, heads * HDIM), bf16)
    row = lambda member: member.reshape(1, -1)
    return pl.pallas_call(
        mix_kernel,
        out_shape=shape,
        in_specs=[in_vmem] * 6 + [in_hbm] * 4,
        out_specs=in_hbm,
        scratch_shapes=[
            VMEM(normed.shape, bf16),
            VMEM((tokens, LANES), f32),
            VMEM((min(3, groups + 2), w_x.shape[0], features), bf16),
            VMEM((tokens, heads * HDIM), bf16),
            VMEM((tokens, groups * STATE), bf16),
            VMEM((tokens, groups * STATE), bf16),
            VMEM((tokens, heads * HDIM), bf16),
            VMEM((tokens, heads * HDIM), f32),
            VMEM((chunks + 1, heads, LANES), f32),
            VMEM((chunks, heads, CHUNK), f32),
            VMEM((chunks, heads, CHUNK), f32),
            VMEM((STATE, features), f32),
            VMEM((groups, chunks, STATE, features), bf16),
            VMEM((batches, shards, slice_rows, STATE), bf16),
            VMEM((batches, shards, slice_rows, STATE), bf16),
            VMEM((batches, shards, slice_rows, STATE), bf16),
            VMEM((batches, shards, slice_rows, STATE), bf16),
            VMEM((shards, decay_rows, LANES), f32),
            VMEM((shards, decay_rows, LANES), f32),
            dma(()),
            dma((min(3, groups + 2),)),
            dma((groups,)),
            dma((shards,)),
            dma((shards,)),
            dma((batches, shards)),
            dma((batches, shards)),
            dma((batches, shards)),
            dma((batches, shards)),
        ],
        compiler_params=pltpu.CompilerParams(
            collective_id=1, has_side_effects=True, vmem_limit_bytes=50 << 20
        ),
        name="mix",
    )(
        squares,
        w_dt.T,
        row(dt_bias),
        row(a_log),
        row(d_skip),
        row(out_gain),
        normed,
        w_x,
        w_b,
        w_c,
    )


def on_device(
    patches,
    grid_rows,
    frame_ids,
    ln_gain,
    w_qkv,
    w_out,
    w_conn,
    norm_gain,
    w_x,
    w_b,
    w_c,
    w_dt,
    dt_bias,
    a_log,
    d_skip,
    out_gain,
):
    part_width = patches.shape[2]
    shards = lax.axis_size("tm")
    my = lax.axis_index("head").astype(jnp.int32).reshape(1)
    parts = lax.axis_size("head")
    all_conn = lax.all_gather(w_conn, "head")
    order, valid, rank, label = routes(frame_ids, grid_rows, shards)
    arrived, labels = vision(
        patches.swapaxes(1, 2),
        order,
        valid,
        rank,
        label,
        ln_gain.reshape(1, -1),
        w_qkv.swapaxes(1, 2),
        w_out,
        parts,
        shards,
    )
    features = w_dt.shape[1] // (w_b.shape[1] // STATE) * HDIM
    stream, normed, squares = connect(
        arrived, labels, frame_ids.shape[0], all_conn, norm_gain, features)
    return stream, mix(
        normed, squares, w_x, w_b, w_c, w_dt, dt_bias, a_log, d_skip, out_gain, shards)


def solution(mesh):
    in_specs = (
        P("tm", None, "head"),
        P("tm"),
        P("tm"),
        P(),
        P(None, None, "head"),
        P("head", None),
        P(None, "head"),
        P(),
        P(None, "head"),
        P(None, "head"),
        P(None, "head"),
        P(None, "head"),
        P("head"),
        P("head"),
        P("head"),
        P("head"),
    )
    out_specs = (P("tm", "head"), P("tm", "head"))
    return jax.shard_map(
        on_device, mesh=mesh, in_specs=in_specs, out_specs=out_specs, check_vma=False
    )
```

```python
import math

import jax
import jax.numpy as jnp
from jax import lax
from jax.experimental import pallas as pl
from jax.experimental.pallas import tpu as pltpu
from jax.sharding import PartitionSpec as P

GRID = 16
POOL = 4
VHD = 72
HDIM = 64
STATE = 128
CHUNK = 128
LANES = 128

f32 = jnp.float32
bf16 = jnp.bfloat16
VMEM = pltpu.VMEM
MESH = pl.DeviceIdType.MESH
CONTRACT_LAST = (((1,), (1,)), ((), ()))
CONTRACT_FIRST = (((0,), (0,)), ((), ()))


def flipped(index, mask, count):
    result, bit = 0, 1
    while bit < count:
        result = result + bit * ((index // bit + mask // bit) % 2)
        bit *= 2
    return result


def partners(index, spot, count):
    if count & (count - 1):
        return (index + spot + 1) % count, (index + 2 * count - spot - 1) % count
    other = flipped(index, count - 1 - spot, count)
    return other, other


def vision_kernel(
    order_ref,
    valid_ref,
    rank_ref,
    label_ref,
    patches_ref,
    gain_ref,
    wqkv_hbm,
    wout_hbm,
    out_ref,
    labels,
    wqkv_ref,
    wout_ref,
    label_out,
    full,
    gain,
    normed,
    qkv,
    context,
    partial,
    partial_in,
    mine,
    pooled_frames,
    outbox,
    weight_sem,
    label_send,
    label_recv,
    patch_send,
    patch_recv,
    partial_send,
    partial_recv,
    frame_send,
    frame_recv,
    forward_send,
    forward_recv,
):
    parts, frames, part_width, patch_count = full.shape
    shards = out_ref.shape[1]
    width = parts * part_width
    local_width = wqkv_ref.shape[1]
    heads = local_width // VHD
    tokens = patch_count // POOL
    batch = normed.shape[1] // patch_count
    fold = out_ref.shape[3] // part_width
    lines = tokens // fold
    factor = VHD ** (-0.5) * math.log2(math.e)
    tm, head = lax.axis_index("tm"), lax.axis_index("head")
    peers = [(head + step) % parts for step in range(1, parts)]
    sources = [(head + parts - step) % parts for step in range(1, parts)]

    def remote(source, target, send, recv, to):
        return pltpu.make_async_remote_copy(
            src_ref=source,
            dst_ref=target,
            send_sem=send,
            recv_sem=recv,
            device_id=to,
            device_id_type=MESH,
        )

    def patch_copy(step, rank, part):
        return remote(
            full.at[part, rank],
            full.at[part, rank],
            patch_send.at[step, rank],
            patch_recv.at[step, rank],
            (tm, peers[step]),
        )

    def partial_copy(step, rank):
        return remote(
            partial.at[rank, peers[step]],
            partial_in.at[rank, step],
            partial_send.at[step, rank],
            partial_recv.at[step, rank],
            (tm, peers[step]),
        )

    def frame_copy(spot):
        return remote(
            outbox.at[spot],
            out_ref.at[head, spot],
            frame_send.at[spot],
            frame_recv.at[spot],
            (partners(tm, spot, shards)[0], head),
        )

    def label_copy(spot):
        return remote(
            label_out.at[spot],
            labels.at[spot],
            label_send.at[spot],
            label_recv.at[spot],
            (partners(tm, spot, shards)[0], head),
        )

    def forward_copy(step, spot, part):
        return remote(
            out_ref.at[part, spot],
            out_ref.at[part, spot],
            forward_send.at[step, spot],
            forward_recv.at[step, spot],
            (tm, peers[step]),
        )

    qkv_load = pltpu.make_async_copy(wqkv_hbm, wqkv_ref, weight_sem.at[0])
    out_load = pltpu.make_async_copy(wout_hbm, wout_ref, weight_sem.at[1])
    qkv_load.start()
    out_load.start()
    barrier = pltpu.get_barrier_semaphore()
    for peer in peers:
        pl.semaphore_signal(barrier, inc=1, device_id=(tm, peer), device_id_type=MESH)

    def greet(spot, carry):
        pl.semaphore_signal(
            barrier,
            inc=1,
            device_id=(partners(tm, spot, shards)[1], head),
            device_id_type=MESH,
        )
        return carry

    lax.fori_loop(0, shards - 1, greet, 0)

    def stage(rank, carry):
        full[head, rank] = patches_ref[order_ref[rank]]
        return carry

    lax.fori_loop(0, frames, stage, 0)
    for first in range(0, width, LANES):
        tile = jnp.broadcast_to(gain_ref[:, first : first + LANES], (LANES, LANES))
        gain[first : first + LANES] = tile.T
    pl.semaphore_wait(barrier, parts - 1 + shards - 1)

    def share(rank, carry):
        for step in range(parts - 1):
            patch_copy(step, rank, head).start()
        return carry

    lax.fori_loop(0, frames, share, 0)

    def name(spot, carry):
        label_out[spot] = jnp.full(label_out.shape[1:], label_ref[spot].astype(f32))
        label_copy(spot).start()
        return carry

    lax.fori_loop(0, shards - 1, name, 0)
    labels[shards - 1] = jnp.full(label_out.shape[1:], label_ref[shards - 1].astype(f32))

    def normalise(rank, columns):
        total = 0.0
        for part in range(parts):
            total = total + jnp.sum(full[part, rank].astype(f32), axis=0, keepdims=True)
        centre = total / width
        spread = 0.0
        for part in range(parts):
            moved = full[part, rank].astype(f32) - centre
            spread = spread + jnp.sum(moved * moved, axis=0, keepdims=True)
        scale = lax.rsqrt(spread / width + 1e-06)
        for part in range(parts):
            rows = slice(part * part_width, (part + 1) * part_width)
            wide = jnp.concatenate([gain[rows]] * (patch_count // LANES), axis=1)
            normed[rows, columns] = (
                (full[part, rank].astype(f32) - centre) * scale * wide
            ).astype(bf16)

    spot_row = lax.broadcasted_iota(jnp.int32, (8, patch_count), 0)
    spot_key = lax.broadcasted_iota(jnp.int32, (8, patch_count), 1)
    ones_row = jnp.where(spot_row == 0, 1.0, 0.0).astype(f32)

    def extended(member, head_id, columns, extra):
        rows = slice(head_id * VHD, (head_id + 1) * VHD)
        return jnp.concatenate([qkv[member, rows, columns], extra], axis=0).astype(bf16)

    def score(head_id, columns, key_row):
        return lax.dot_general(
            extended(1, head_id, columns, key_row),
            extended(0, head_id, columns, ones_row),
            CONTRACT_FIRST,
            preferred_element_type=f32,
        )

    def mix(head_id, columns, scores):
        powered = jnp.exp2((scores - jnp.max(scores, axis=0, keepdims=True)) * factor)
        mixed = jnp.dot(
            extended(2, head_id, columns, ones_row),
            powered.astype(bf16),
            preferred_element_type=f32,
        )
        context[head_id * VHD : (head_id + 1) * VHD, columns] = mixed[:VHD] * (
            1.0 / mixed[VHD : VHD + 1]
        )

    pool_row = lax.broadcasted_iota(jnp.int32, (tokens, patch_count), 0)
    pool_column = lax.broadcasted_iota(jnp.int32, (tokens, patch_count), 1)
    pooling = jnp.where(pool_column // POOL == pool_row, 1.0 / POOL, 0.0).astype(bf16)
    token_spot = lax.broadcasted_iota(jnp.int32, (tokens, part_width), 0) * POOL
    spans = [slice(b * patch_count, (b + 1) * patch_count) for b in range(batch)]

    def post(spot):
        outbox[spot] = pooled_frames[rank_ref[spot]]

    def settle(rank):
        for step in range(parts - 1):
            partial_copy(step, rank).wait_recv()
        total = mine[rank]
        for step in range(parts - 1):
            total = total + partial_in[rank, step].astype(f32)
        total = jnp.where(token_spot < valid_ref[rank], total, 0.0).astype(bf16)
        for at in range(fold):
            pooled_frames[rank, :, at * part_width : (at + 1) * part_width] = total[
                at * lines : (at + 1) * lines
            ]
        post(rank)
        frame_copy(rank).start()

    def forward(spot):
        frame_copy(spot).wait_recv()
        for step in range(parts - 1):
            forward_copy(step, spot, head).start()

    def body(turn, carry):
        ranks = [turn * batch + b for b in range(batch)]
        for rank, span in zip(ranks, spans):
            for step in range(parts - 1):
                patch_copy(step, rank, sources[step]).wait_recv()
            normalise(rank, span)

        @pl.when(turn >= 1)
        def _():
            for b in range(batch):
                settle((turn - 1) * batch + b)

        @pl.when(turn == 0)
        def _():
            qkv_load.wait()
            out_load.wait()

        for member in range(3):
            qkv[member] = jnp.dot(wqkv_ref[member], normed[...], preferred_element_type=f32)

        @pl.when(turn >= 3)
        def _():
            for b in range(batch):
                forward((turn - 3) * batch + b)

        key_rows = [
            jnp.where((spot_row == 0) & (spot_key >= valid_ref[rank]), -1e30, 0.0).astype(f32)
            for rank in ranks
        ]
        todo = [(head_id, b) for head_id in range(heads) for b in range(batch)]
        ahead = 4
        ready = [score(h, spans[b], key_rows[b]) for h, b in todo[:ahead]]
        for at, (h, b) in enumerate(todo):
            if at + ahead < len(todo):
                later, which = todo[at + ahead]
                ready.append(score(later, spans[which], key_rows[which]))
            mix(h, spans[b], ready[at])
        pooled = jnp.concatenate(
            [
                lax.dot_general(
                    pooling,
                    context[:, span].astype(bf16),
                    CONTRACT_LAST,
                    preferred_element_type=f32,
                ).astype(bf16)
                for span in spans
            ],
            axis=0,
        )
        attended = jnp.dot(pooled, wout_ref[...], preferred_element_type=f32)
        for b, rank in enumerate(ranks):
            own = lax.dot_general(
                pooling, full[head, rank], CONTRACT_LAST, preferred_element_type=f32
            )
            for part in range(parts):
                block = attended[
                    b * tokens : (b + 1) * tokens, part * part_width : (part + 1) * part_width
                ]
                partial[rank, part] = block.astype(bf16)
                own = own + jnp.where(head == part, block, 0.0)
            mine[rank] = own
            for step in range(parts - 1):
                partial_copy(step, rank).start()
        return carry

    turns = frames // batch
    lax.fori_loop(0, turns, body, 0)
    for rank in range(frames - batch, frames):
        settle(rank)
    for spot in range(frames, shards):
        post(spot)
        if spot < shards - 1:
            frame_copy(spot).start()
    out_ref[head, shards - 1] = outbox[shards - 1]
    for step in range(parts - 1):
        forward_copy(step, shards - 1, head).start()

    def late_forward(spot, carry):
        forward(spot)
        return carry

    lax.fori_loop(max(turns - 3, 0) * batch, shards - 1, late_forward, 0)

    def drain_ranks(rank, carry):
        for step in range(parts - 1):
            patch_copy(step, rank, head).wait_send()
            partial_copy(step, rank).wait_send()
        return carry

    lax.fori_loop(0, frames, drain_ranks, 0)

    def drain_frames(spot, carry):
        frame_copy(spot).wait_send()
        label_copy(spot).wait()
        return carry

    lax.fori_loop(0, shards - 1, drain_frames, 0)

    def drain_forwards(spot, carry):
        for step in range(parts - 1):
            forward_copy(step, spot, sources[step]).wait_recv()
            forward_copy(step, spot, head).wait_send()
        return carry

    lax.fori_loop(0, shards, drain_forwards, 0)


def vision(patches, order, valid, rank, label, gain, w_qkv, w_out, parts, shards):
    frames, part_width, patch_count = patches.shape
    width = parts * part_width
    local_width = w_qkv.shape[1]
    tokens = patch_count // POOL
    batch = math.gcd(frames, 2)
    in_smem = pl.BlockSpec(memory_space=pltpu.SMEM)
    in_vmem = pl.BlockSpec(memory_space=VMEM)
    in_hbm = pl.BlockSpec(memory_space=pl.ANY)
    peers = parts - 1
    fold = 2 if part_width % LANES == LANES // 2 and tokens % 32 == 0 else 1
    lines = (tokens // fold, part_width * fold)
    dma = pltpu.SemaphoreType.DMA
    return pl.pallas_call(
        vision_kernel,
        out_shape=(
            jax.ShapeDtypeStruct((parts, shards) + lines, bf16),
            jax.ShapeDtypeStruct((shards, 8, LANES), f32),
        ),
        in_specs=[in_smem] * 4 + [in_vmem] * 2 + [in_hbm] * 2,
        out_specs=(in_vmem, in_vmem),
        scratch_shapes=[
            VMEM(w_qkv.shape, bf16),
            VMEM(w_out.shape, bf16),
            VMEM((shards, 8, LANES), f32),
            VMEM((parts, frames, part_width, patch_count), bf16),
            VMEM((width, LANES), f32),
            VMEM((width, batch * patch_count), bf16),
            VMEM((3, local_width, batch * patch_count), f32),
            VMEM((local_width, batch * patch_count), f32),
            VMEM((frames, parts, tokens, part_width), bf16),
            VMEM((frames, peers, tokens, part_width), bf16),
            VMEM((frames, tokens, part_width), f32),
            VMEM((frames,) + lines, bf16),
            VMEM((shards,) + lines, bf16),
            dma((2,)),
            dma((shards,)),
            dma((shards,)),
            dma((peers, frames)),
            dma((peers, frames)),
            dma((peers, frames)),
            dma((peers, frames)),
            dma((shards,)),
            dma((shards,)),
            dma((peers, shards)),
            dma((peers, shards)),
        ],
        compiler_params=pltpu.CompilerParams(
            collective_id=0, has_side_effects=True, vmem_limit_bytes=56 << 20
        ),
        cost_estimate=pl.CostEstimate(
            flops=frames * patch_count * width * local_width * 10,
            bytes_accessed=12_000_000,
            transcendentals=4_000_000,
        ),
        name="vision",
    )(order, valid, rank, label, patches, gain, w_qkv, w_out)


def routes(frame_ids, grid_rows, shards):
    frames = frame_ids.shape[0]
    tm = lax.axis_index("tm").astype(jnp.int32)
    spots = jnp.arange(shards, dtype=jnp.int32)
    targets = partners(tm, spots, shards)[0]
    slots = jnp.arange(frames, dtype=jnp.int32)
    total = lambda chosen, member, axis: jnp.sum(
        jnp.where(chosen, member, 0), axis=axis
    ).astype(jnp.int32)
    goes = (frame_ids // frames)[:, None] == targets[None, :]
    spot_of = total(goes, spots[None, :], 1)
    rank_of = jnp.sum(spot_of[None, :] < spot_of[:, None], axis=1).astype(jnp.int32)
    holds = rank_of[None, :] == slots[:, None]
    order = total(holds, slots[None, :], 1)
    valid = total(holds, (grid_rows * GRID)[None, :], 1)
    rank = total(goes, rank_of[:, None], 0)
    label = total(goes, (frame_ids % frames + 1)[:, None], 0)
    return order, valid, rank, label


def spread(rows, width, copies):
    heads = rows // copies
    row = lax.broadcasted_iota(jnp.int32, (rows, heads * width), 0) % heads
    block = lax.broadcasted_iota(jnp.int32, (rows, heads * width), 1) // width
    return jnp.where(row == block, 1.0, 0.0).astype(bf16)


def split(values, copies):
    terms = []
    for _ in range(copies):
        terms.append(values.astype(bf16).astype(f32))
        values = values - terms[-1]
    return jnp.concatenate(terms, axis=0).astype(bf16)


def column(row):
    count = row.shape[1]
    same = lax.broadcasted_iota(jnp.int32, (count, count), 0) == lax.broadcasted_iota(
        jnp.int32, (count, count), 1
    )
    return jnp.sum(jnp.where(same, row, 0.0), axis=1, keepdims=True)


def connect_kernel(
    arrived_hbm,
    labels,
    norm_gain_ref,
    conn_hbm,
    stream_hbm,
    normed_hbm,
    squares,
    arrived_ref,
    conn,
    rows,
    even,
    odd,
    gained,
    plain,
    sender_ref,
    arrived_sem,
    conn_sem,
    normed_sem,
    stream_sem,
):
    parts, shards, lines, folded = arrived_ref.shape
    tokens = rows.shape[0]
    conn_count, width, conn_width = conn.shape
    part_width = width // parts
    per_part = conn_count // parts
    fold = folded // part_width
    frame_tokens = lines * fold
    frames = tokens // frame_tokens
    head = lax.axis_index("head")
    arrived_copy = pltpu.make_async_copy(arrived_hbm, arrived_ref, arrived_sem)
    arrived_copy.start()

    def conn_load(at):
        return pltpu.make_async_copy(
            conn_hbm.at[
                at // per_part,
                :,
                pl.ds(pl.multiple_of((at % per_part) * conn_width, conn_width), conn_width),
            ],
            conn.at[at],
            conn_sem.at[at],
        )

    def conn_start(at, carry):
        conn_load(at).start()
        return carry

    lax.fori_loop(0, conn_count, conn_start, 0)
    for shard in range(shards):
        sender_ref[jnp.max(labels[shard]).astype(jnp.int32)] = shard
    arrived_copy.wait()

    def gather(frame, carry):
        for at in range(fold):
            first = pl.multiple_of(frame * frame_tokens + at * lines, lines)
            for part in range(parts):
                rows[pl.ds(first, lines), part * part_width : (part + 1) * part_width] = (
                    arrived_ref[
                        part,
                        sender_ref[frame + 1],
                        :,
                        at * part_width : (at + 1) * part_width,
                    ]
                )
        return carry

    lax.fori_loop(0, frames, gather, 0)
    squares[...] = jnp.zeros_like(squares)

    def normed_copy(at):
        columns = pl.ds(pl.multiple_of(at * conn_width, conn_width), conn_width)
        return pltpu.make_async_copy(gained.at[at], normed_hbm.at[:, columns], normed_sem.at[at])

    def stream_copy(at):
        mine = pl.ds(pl.multiple_of((at % per_part) * conn_width, conn_width), conn_width)
        return pltpu.make_async_copy(
            plain.at[at], stream_hbm.at[:, mine], stream_sem.at[at % per_part]
        )

    def multiply(at, total):
        total[...] = jnp.dot(rows[...], conn[at], preferred_element_type=f32)

    def settle(at, total):
        columns = pl.ds(pl.multiple_of(at * conn_width, conn_width), conn_width)
        made = total[...].astype(bf16)
        plain[at] = made
        made = made.astype(f32)
        gained[at] = (made * norm_gain_ref[:, columns]).astype(bf16)
        made = made * made
        squares[...] += sum(
            made[:, lane : lane + LANES] for lane in range(0, conn_width, LANES)
        )

    def send(at):
        normed_copy(at).start()

        @pl.when(at // per_part == head)
        def _():
            stream_copy(at).start()

    def connect(turn, carry):
        at = turn * 2
        conn_load(at + 1).wait()
        conn_load(at + 2).wait()
        multiply(at + 1, odd)
        settle(at, even)
        multiply(at + 2, even)
        settle(at + 1, odd)
        send(at)
        send(at + 1)
        return carry

    conn_load(0).wait()
    multiply(0, even)
    pairs = (conn_count - 1) // 2
    lax.fori_loop(0, pairs, connect, 0)
    for at in range(2 * pairs, conn_count):
        if at > 2 * pairs:
            conn_load(at).wait()
            multiply(at, even)
        settle(at, even)
        send(at)

    def drain(at, carry):
        normed_copy(at).wait()
        return carry

    lax.fori_loop(0, conn_count, drain, 0)
    for at in range(per_part):
        stream_copy(head * per_part + at).wait()


def connect(arrived, labels, frames, weights, norm_gain, features):
    parts, _, lines, folded = arrived.shape
    _, width, columns = weights.shape
    tokens = frames * lines * (folded * parts // width)
    full_width = parts * columns
    conn_width = math.gcd(columns, features)
    conn_count = full_width // conn_width
    in_vmem = pl.BlockSpec(memory_space=VMEM)
    in_hbm = pl.BlockSpec(memory_space=pl.ANY)
    return pl.pallas_call(
        connect_kernel,
        out_shape=(
            jax.ShapeDtypeStruct((tokens, columns), bf16),
            jax.ShapeDtypeStruct((tokens, full_width), bf16),
            jax.ShapeDtypeStruct((tokens, LANES), f32),
        ),
        in_specs=[in_hbm, in_vmem, in_vmem, in_hbm],
        out_specs=(in_hbm, in_hbm, in_vmem),
        scratch_shapes=[
            VMEM(arrived.shape, bf16),
            VMEM((conn_count, width, conn_width), bf16),
            VMEM((tokens, width), bf16),
            VMEM((tokens, conn_width), f32),
            VMEM((tokens, conn_width), f32),
            VMEM((conn_count, tokens, conn_width), bf16),
            VMEM((conn_count, tokens, conn_width), bf16),
            pltpu.SMEM((frames + 1,), jnp.int32),
            pltpu.SemaphoreType.DMA(()),
            pltpu.SemaphoreType.DMA((conn_count,)),
            pltpu.SemaphoreType.DMA((conn_count,)),
            pltpu.SemaphoreType.DMA((columns // conn_width,)),
        ],
        compiler_params=pltpu.CompilerParams(vmem_limit_bytes=60 << 20),
        name="connect",
    )(arrived, labels, norm_gain.reshape(1, -1), weights)


def mix_kernel(
    squares_ref,
    wdt_ref,
    bias_ref,
    alog_ref,
    skip_ref,
    out_gain_ref,
    normed_hbm,
    wx_hbm,
    wb_hbm,
    wc_hbm,
    out_hbm,
    normed,
    scales,
    ring,
    inner,
    write,
    read,
    result,
    local_out,
    staged,
    down,
    across,
    state,
    saved,
    state_out,
    state_in,
    before,
    incoming,
    decay_out,
    decay_in,
    normed_sem,
    ring_sem,
    out_sem,
    decay_send,
    decay_recv,
    first_send,
    first_recv,
    second_send,
    second_recv,
):
    tokens, full_width = normed.shape
    heads = wdt_ref.shape[0]
    groups = write.shape[1] // STATE
    per_group = heads // groups
    features = per_group * HDIM
    chunks = tokens // CHUNK
    block = 2 * CHUNK
    batches, shards, slice_rows, _ = state_in.shape
    batch_groups = groups // batches
    piece = features // shards
    unit = min(piece, HDIM)
    pieces = piece // unit
    tm, head = lax.axis_index("tm"), lax.axis_index("head")
    log2e = math.log2(math.e)

    def remote(source, target, send, recv, spot):
        return pltpu.make_async_remote_copy(
            src_ref=source,
            dst_ref=target,
            send_sem=send,
            recv_sem=recv,
            device_id=(partners(tm, spot, shards)[0], head),
            device_id_type=MESH,
        )

    def target_of(spot):
        return partners(tm, spot, shards)[0]

    def decay_copy(spot):
        return remote(
            decay_out.at[target_of(spot)],
            decay_in.at[tm],
            decay_send.at[spot],
            decay_recv.at[spot],
            spot,
        )

    def first_copy(batch, spot):
        return remote(
            state_out.at[batch, target_of(spot)],
            state_in.at[batch, tm],
            first_send.at[batch, spot],
            first_recv.at[batch, spot],
            spot,
        )

    def second_copy(batch, spot):
        return remote(
            before.at[batch, target_of(spot)],
            incoming.at[batch, tm],
            second_send.at[batch, spot],
            second_recv.at[batch, spot],
            spot,
        )

    def over_spots(act):
        def step(spot, carry):
            act(spot)
            return carry

        lax.fori_loop(0, shards - 1, step, 0)

    barrier = pltpu.get_barrier_semaphore()
    over_spots(
        lambda spot: pl.semaphore_signal(
            barrier,
            inc=1,
            device_id=(partners(tm, spot, shards)[1], head),
            device_id_type=MESH,
        )
    )

    def weight_load(which):
        slot = which % ring.shape[0]
        if which == 0 or which == groups + 1:
            source = wb_hbm if which == 0 else wc_hbm
            target = ring.at[slot, :, : groups * STATE]
        else:
            source = wx_hbm.at[:, (which - 1) * features : which * features]
            target = ring.at[slot]
        return pltpu.make_async_copy(source, target, ring_sem.at[slot])

    normed_copy = pltpu.make_async_copy(normed_hbm, normed, normed_sem)
    normed_copy.start()
    for which in range(ring.shape[0]):
        weight_load(which).start()
    mean = jnp.sum(squares_ref[...], axis=1, keepdims=True) / full_width
    scales[...] = jnp.broadcast_to(lax.rsqrt(mean + 1e-05), scales.shape)
    mean_row = lax.dot_general(
        jnp.ones((8, LANES), f32),
        squares_ref[...],
        CONTRACT_LAST,
        preferred_element_type=f32,
        precision=lax.Precision.HIGHEST,
    )
    scale_row = lax.rsqrt(mean_row[:1] / full_width + 1e-05)
    normed_copy.wait()

    raw = lax.dot_general(wdt_ref[...], normed[...], CONTRACT_LAST, preferred_element_type=f32)
    raw = raw * scale_row + column(bias_ref[...])
    step_size = jnp.maximum(raw, 0.0) + jnp.log1p(jnp.exp(-jnp.abs(raw)))
    rate = -jnp.exp(column(alog_ref[...])) * log2e
    log_decay = step_size * rate
    log_step = jnp.log(step_size) * log2e
    upper = jnp.where(
        lax.broadcasted_iota(jnp.int32, (CHUNK, CHUNK), 0)
        <= lax.broadcasted_iota(jnp.int32, (CHUNK, CHUNK), 1),
        1.0,
        0.0,
    ).astype(f32)
    ends = []
    for chunk in range(chunks):
        span = slice(chunk * CHUNK, (chunk + 1) * CHUNK)
        sums = jnp.dot(
            log_decay[:, span],
            upper,
            preferred_element_type=f32,
            precision=lax.Precision.HIGHEST,
        )
        down[chunk] = sums
        across[chunk] = sums - log_step[:, span]
        ends.append(sums[:, CHUNK - 1 :])
    total = jnp.zeros_like(ends[0])
    for chunk in range(chunks):
        staged[chunk] = jnp.broadcast_to(total, (heads, LANES))
        total = total + ends[chunk]
    staged[chunks] = jnp.broadcast_to(jnp.exp2(total), (heads, LANES))
    decay_out[...] = jnp.zeros_like(decay_out)
    for target in range(shards):
        for group in range(groups):
            for part in range(pieces):
                at = group * per_group + (target * piece + part * unit) // HDIM
                row = group * pieces + part
                decay_out[target, row : row + 1] = staged[chunks, at : at + 1]
    decay_in[tm] = decay_out[tm]
    pl.semaphore_wait(barrier, shards - 1)
    over_spots(lambda spot: decay_copy(spot).start())

    def project(which, target, first_column, count):
        slot = which % ring.shape[0]
        weight_load(which).wait()

        firsts = list(range(0, tokens, block))

        def one(first):
            return jnp.dot(normed[first : first + block, :], ring[slot, :, :count], preferred_element_type=f32)

        def store(first, made):
            wide = jnp.concatenate([scales[first : first + block, :]] * (count // LANES), axis=1)
            target[first : first + block, first_column : first_column + count] = (made * wide).astype(bf16)

        held = one(0)
        for first in firsts[1:]:
            later = one(first)
            store(first - block, held)
            held = later
        store(firsts[-1], held)
        if which + ring.shape[0] <= groups + 1:
            weight_load(which + ring.shape[0]).start()

    spread_narrow = spread(2 * per_group, HDIM, 2)
    spread_wide = spread(3 * per_group, CHUNK, 3)
    head_row = lax.broadcasted_iota(jnp.int32, (per_group, features), 0)
    head_lane = lax.broadcasted_iota(jnp.int32, (per_group, features), 1) // HDIM

    def widen(values):
        return lax.dot_general(
            split(values, 2), spread_narrow, CONTRACT_FIRST, preferred_element_type=f32
        )

    def widen_row(values):
        return jnp.sum(jnp.where(head_row == head_lane, values, 0.0), axis=0, keepdims=True)

    def at_group(group, chunk):
        own = slice(group * per_group, (group + 1) * per_group)
        return (
            pl.ds(pl.multiple_of(chunk * CHUNK, CHUNK), CHUNK),
            slice(group * features, (group + 1) * features),
            slice(group * STATE, (group + 1) * STATE),
            own,
        )

    def states(group):
        state[...] = jnp.zeros_like(state)

        def step(chunk, carry):
            span, lanes, keys, own = at_group(group, chunk)
            sums, shifted = down[chunk, own], across[chunk, own]
            end = sums[:, CHUNK - 1 :]
            held = state[...]
            saved[group, chunk] = held.astype(bf16)
            scaled = (inner[span, lanes].astype(f32) * widen(jnp.exp2(end - shifted))).astype(bf16)
            state[...] = held * widen_row(jnp.exp2(end)) + lax.dot_general(
                write[span, keys], scaled, CONTRACT_FIRST, preferred_element_type=f32
            )
            return carry

        lax.fori_loop(0, chunks, step, 0, unroll=math.gcd(chunks, 3))
        batch, inside = group // batch_groups, group % batch_groups
        sideways = state[...].T.astype(bf16)
        for target in range(shards):
            state_out[batch, target, inside * piece : (inside + 1) * piece] = sideways[
                target * piece : (target + 1) * piece
            ]

    def send_first(batch):
        state_in[batch, tm] = state_out[batch, tm]
        over_spots(lambda spot: first_copy(batch, spot).start())

    def send_second(batch):
        if batch == 0:
            over_spots(lambda spot: decay_copy(spot).wait_recv())
        over_spots(lambda spot: first_copy(batch, spot).wait_recv())
        for inside in range(batch_groups):
            group = batch * batch_groups + inside
            for part in range(pieces):
                span = slice(inside * piece + part * unit, inside * piece + (part + 1) * unit)
                row = group * pieces + part
                current = jnp.zeros((unit, STATE), f32)
                for shard in range(shards):
                    before[batch, shard, span] = current.astype(bf16)
                    current = decay_in[shard, row : row + 1] * current + state_in[
                        batch, shard, span
                    ].astype(f32)
        incoming[batch, tm] = before[batch, tm]
        over_spots(lambda spot: second_copy(batch, spot).start())

    causal = lax.broadcasted_iota(jnp.int32, (CHUNK, CHUNK), 0) >= lax.broadcasted_iota(
        jnp.int32, (CHUNK, CHUNK), 1
    )
    lane = lax.broadcasted_iota(jnp.int32, (CHUNK, LANES), 1)
    skip_column = column(skip_ref[...])

    def local(group):
        skip = widen_row(skip_column[group * per_group : (group + 1) * per_group])

        def step(chunk, carry):
            span, lanes, keys, own = at_group(group, chunk)
            sums, shifted = down[chunk, own], across[chunk, own]
            readers = read[span, keys]
            crossing = lax.dot_general(
                readers, write[span, keys], CONTRACT_LAST, preferred_element_type=f32
            )
            crossing = jnp.where(causal, crossing, 0.0)
            downs = lax.dot_general(
                split(sums, 3), spread_wide, CONTRACT_FIRST, preferred_element_type=f32
            )
            grown = widen(jnp.exp2(sums))
            carried = jnp.dot(readers, saved[group, chunk], preferred_element_type=f32)
            for pair in range(features // LANES):
                at = slice(pair * LANES, (pair + 1) * LANES)
                here = slice(lanes.start + pair * LANES, lanes.start + (pair + 1) * LANES)
                values = inner[span, here]
                halves = []
                for one in (2 * pair, 2 * pair + 1):
                    spans = downs[:, one * CHUNK : (one + 1) * CHUNK] - shifted[one : one + 1]
                    halves.append((crossing * jnp.exp2(jnp.minimum(spans, 100.0))).astype(bf16))
                wide = values.astype(f32)
                stacked = jnp.concatenate(
                    [jnp.where(lane < HDIM, wide, 0.0), jnp.where(lane < HDIM, 0.0, wide)], axis=0
                ).astype(bf16)
                within = jnp.dot(
                    jnp.concatenate(halves, axis=1), stacked, preferred_element_type=f32
                )
                local_out[span, here] = within + carried[:, at] * grown[:, at] + skip[:, at] * wide
            return carry

        lax.fori_loop(0, chunks, step, 0, unroll=math.gcd(chunks, 3))

    def finish(group):
        batch, inside = group // batch_groups, group % batch_groups
        held = jnp.concatenate(
            [
                incoming[batch, shard, inside * piece : (inside + 1) * piece]
                for shard in range(shards)
            ],
            axis=0,
        )

        def step(chunk, carry):
            span, lanes, keys, own = at_group(group, chunk)
            grown = widen(jnp.exp2(down[chunk, own] + staged[chunk, own]))
            carried = lax.dot_general(
                read[span, keys], held, CONTRACT_LAST, preferred_element_type=f32
            )
            summed = local_out[span, lanes] + carried * grown
            mean = jnp.sum(summed * summed, axis=1, keepdims=True) / features
            result[span, lanes] = (
                summed * lax.rsqrt(mean + 1e-05) * out_gain_ref[:, lanes]
            ).astype(bf16)
            return carry

        lax.fori_loop(0, chunks, step, 0, unroll=math.gcd(chunks, 3))

    def out_copy(group):
        lanes = slice(group * features, (group + 1) * features)
        return pltpu.make_async_copy(
            result.at[:, lanes], out_hbm.at[:, lanes], out_sem.at[group]
        )

    project(0, write, 0, groups * STATE)
    for group in range(groups):
        project(group + 1, inner, group * features, features)
        states(group)
        if (group + 1) % batch_groups == 0:
            send_first(group // batch_groups)
    if batches > 1:
        send_second(0)
    project(groups + 1, read, 0, groups * STATE)
    for group in range(groups):
        if group == groups // 2:
            send_second(batches - 1)
        local(group)
    for group in range(groups):
        if group % batch_groups == 0:
            batch = group // batch_groups
            over_spots(lambda spot: second_copy(batch, spot).wait_recv())
        finish(group)
        out_copy(group).start()
    over_spots(lambda spot: decay_copy(spot).wait_send())
    for batch in range(batches):
        over_spots(lambda spot: first_copy(batch, spot).wait_send())
        over_spots(lambda spot: second_copy(batch, spot).wait_send())
    for group in range(groups):
        out_copy(group).wait()


def mix(normed, squares, w_x, w_b, w_c, w_dt, dt_bias, a_log, d_skip, out_gain, shards):
    tokens = normed.shape[0]
    heads = w_dt.shape[1]
    groups = w_b.shape[1] // STATE
    features = heads // groups * HDIM
    chunks = tokens // CHUNK
    batches = math.gcd(groups, 2)
    piece = features // shards
    slice_rows = groups // batches * piece
    pieces = max(piece // HDIM, 1)
    decay_rows = -(-groups * pieces // 8) * 8
    in_vmem = pl.BlockSpec(memory_space=VMEM)
    in_hbm = pl.BlockSpec(memory_space=pl.ANY)
    dma = pltpu.SemaphoreType.DMA
    shape = jax.ShapeDtypeStruct((tokens, heads * HDIM), bf16)
    row = lambda member: member.reshape(1, -1)
    return pl.pallas_call(
        mix_kernel,
        out_shape=shape,
        in_specs=[in_vmem] * 6 + [in_hbm] * 4,
        out_specs=in_hbm,
        scratch_shapes=[
            VMEM(normed.shape, bf16),
            VMEM((tokens, LANES), f32),
            VMEM((min(3, groups + 2), w_x.shape[0], features), bf16),
            VMEM((tokens, heads * HDIM), bf16),
            VMEM((tokens, groups * STATE), bf16),
            VMEM((tokens, groups * STATE), bf16),
            VMEM((tokens, heads * HDIM), bf16),
            VMEM((tokens, heads * HDIM), f32),
            VMEM((chunks + 1, heads, LANES), f32),
            VMEM((chunks, heads, CHUNK), f32),
            VMEM((chunks, heads, CHUNK), f32),
            VMEM((STATE, features), f32),
            VMEM((groups, chunks, STATE, features), bf16),
            VMEM((batches, shards, slice_rows, STATE), bf16),
            VMEM((batches, shards, slice_rows, STATE), bf16),
            VMEM((batches, shards, slice_rows, STATE), bf16),
            VMEM((batches, shards, slice_rows, STATE), bf16),
            VMEM((shards, decay_rows, LANES), f32),
            VMEM((shards, decay_rows, LANES), f32),
            dma(()),
            dma((min(3, groups + 2),)),
            dma((groups,)),
            dma((shards,)),
            dma((shards,)),
            dma((batches, shards)),
            dma((batches, shards)),
            dma((batches, shards)),
            dma((batches, shards)),
        ],
        compiler_params=pltpu.CompilerParams(
            collective_id=1, has_side_effects=True, vmem_limit_bytes=50 << 20
        ),
        name="mix",
    )(
        squares,
        w_dt.T,
        row(dt_bias),
        row(a_log),
        row(d_skip),
        row(out_gain),
        normed,
        w_x,
        w_b,
        w_c,
    )


def on_device(
    patches,
    grid_rows,
    frame_ids,
    ln_gain,
    w_qkv,
    w_out,
    w_conn,
    norm_gain,
    w_x,
    w_b,
    w_c,
    w_dt,
    dt_bias,
    a_log,
    d_skip,
    out_gain,
):
    part_width = patches.shape[2]
    shards = lax.axis_size("tm")
    my = lax.axis_index("head").astype(jnp.int32).reshape(1)
    parts = lax.axis_size("head")
    all_conn = lax.all_gather(w_conn, "head")
    order, valid, rank, label = routes(frame_ids, grid_rows, shards)
    arrived, labels = vision(
        patches.swapaxes(1, 2),
        order,
        valid,
        rank,
        label,
        ln_gain.reshape(1, -1),
        w_qkv.swapaxes(1, 2),
        w_out,
        parts,
        shards,
    )
    features = w_dt.shape[1] // (w_b.shape[1] // STATE) * HDIM
    stream, normed, squares = connect(
        arrived, labels, frame_ids.shape[0], all_conn, norm_gain, features)
    return stream, mix(
        normed, squares, w_x, w_b, w_c, w_dt, dt_bias, a_log, d_skip, out_gain, shards)


def solution(mesh):
    in_specs = (
        P("tm", None, "head"),
        P("tm"),
        P("tm"),
        P(),
        P(None, None, "head"),
        P("head", None),
        P(None, "head"),
        P(),
        P(None, "head"),
        P(None, "head"),
        P(None, "head"),
        P(None, "head"),
        P("head"),
        P("head"),
        P("head"),
        P("head"),
    )
    out_specs = (P("tm", "head"), P("tm", "head"))
    return jax.shard_map(
        on_device, mesh=mesh, in_specs=in_specs, out_specs=out_specs, check_vma=False
    )
```

```python
import math

import jax
import jax.numpy as jnp
from jax import lax
from jax.experimental import pallas as pl
from jax.experimental.pallas import tpu as pltpu
from jax.sharding import PartitionSpec as P

GRID = 16
POOL = 4
VHD = 72
HDIM = 64
STATE = 128
CHUNK = 128
LANES = 128

f32 = jnp.float32
bf16 = jnp.bfloat16
VMEM = pltpu.VMEM
MESH = pl.DeviceIdType.MESH
CONTRACT_LAST = (((1,), (1,)), ((), ()))
CONTRACT_FIRST = (((0,), (0,)), ((), ()))


def flipped(index, mask, count):
    result, bit = 0, 1
    while bit < count:
        result = result + bit * ((index // bit + mask // bit) % 2)
        bit *= 2
    return result


def partners(index, spot, count):
    if count & (count - 1):
        return (index + spot + 1) % count, (index + 2 * count - spot - 1) % count
    other = flipped(index, count - 1 - spot, count)
    return other, other


def vision_kernel(
    order_ref,
    valid_ref,
    rank_ref,
    label_ref,
    patches_ref,
    gain_ref,
    wqkv_hbm,
    wout_hbm,
    out_ref,
    labels,
    wqkv_ref,
    wout_ref,
    label_out,
    full,
    gain,
    normed,
    qkv,
    context,
    partial,
    partial_in,
    mine,
    pooled_frames,
    outbox,
    weight_sem,
    label_send,
    label_recv,
    patch_send,
    patch_recv,
    partial_send,
    partial_recv,
    frame_send,
    frame_recv,
    forward_send,
    forward_recv,
):
    parts, frames, part_width, patch_count = full.shape
    shards = out_ref.shape[1]
    width = parts * part_width
    local_width = wqkv_ref.shape[1]
    heads = local_width // VHD
    tokens = patch_count // POOL
    batch = normed.shape[1] // patch_count
    fold = out_ref.shape[3] // part_width
    lines = tokens // fold
    factor = VHD ** (-0.5) * math.log2(math.e)
    tm, head = lax.axis_index("tm"), lax.axis_index("head")
    peers = [(head + step) % parts for step in range(1, parts)]
    sources = [(head + parts - step) % parts for step in range(1, parts)]

    def remote(source, target, send, recv, to):
        return pltpu.make_async_remote_copy(
            src_ref=source,
            dst_ref=target,
            send_sem=send,
            recv_sem=recv,
            device_id=to,
            device_id_type=MESH,
        )

    def patch_copy(step, rank, part):
        return remote(
            full.at[part, rank],
            full.at[part, rank],
            patch_send.at[step, rank],
            patch_recv.at[step, rank],
            (tm, peers[step]),
        )

    def partial_copy(step, rank):
        return remote(
            partial.at[rank, peers[step]],
            partial_in.at[rank, step],
            partial_send.at[step, rank],
            partial_recv.at[step, rank],
            (tm, peers[step]),
        )

    def frame_copy(spot):
        return remote(
            outbox.at[spot],
            out_ref.at[head, spot],
            frame_send.at[spot],
            frame_recv.at[spot],
            (partners(tm, spot, shards)[0], head),
        )

    def label_copy(spot):
        return remote(
            label_out.at[spot],
            labels.at[spot],
            label_send.at[spot],
            label_recv.at[spot],
            (partners(tm, spot, shards)[0], head),
        )

    def forward_copy(step, spot, part):
        return remote(
            out_ref.at[part, spot],
            out_ref.at[part, spot],
            forward_send.at[step, spot],
            forward_recv.at[step, spot],
            (tm, peers[step]),
        )

    qkv_load = pltpu.make_async_copy(wqkv_hbm, wqkv_ref, weight_sem.at[0])
    out_load = pltpu.make_async_copy(wout_hbm, wout_ref, weight_sem.at[1])
    qkv_load.start()
    out_load.start()
    barrier = pltpu.get_barrier_semaphore()
    for peer in peers:
        pl.semaphore_signal(barrier, inc=1, device_id=(tm, peer), device_id_type=MESH)

    def greet(spot, carry):
        pl.semaphore_signal(
            barrier,
            inc=1,
            device_id=(partners(tm, spot, shards)[1], head),
            device_id_type=MESH,
        )
        return carry

    lax.fori_loop(0, shards - 1, greet, 0)

    def stage(rank, carry):
        full[head, rank] = patches_ref[order_ref[rank]]
        return carry

    lax.fori_loop(0, frames, stage, 0)
    for first in range(0, width, LANES):
        tile = jnp.broadcast_to(gain_ref[:, first : first + LANES], (LANES, LANES))
        gain[first : first + LANES] = tile.T
    pl.semaphore_wait(barrier, parts - 1 + shards - 1)

    def share(rank, carry):
        for step in range(parts - 1):
            patch_copy(step, rank, head).start()
        return carry

    lax.fori_loop(0, frames, share, 0)

    def name(spot, carry):
        label_out[spot] = jnp.full(label_out.shape[1:], label_ref[spot].astype(f32))
        label_copy(spot).start()
        return carry

    lax.fori_loop(0, shards - 1, name, 0)
    labels[shards - 1] = jnp.full(label_out.shape[1:], label_ref[shards - 1].astype(f32))

    def normalise(rank, columns):
        total = 0.0
        for part in range(parts):
            total = total + jnp.sum(full[part, rank].astype(f32), axis=0, keepdims=True)
        centre = total / width
        spread = 0.0
        for part in range(parts):
            moved = full[part, rank].astype(f32) - centre
            spread = spread + jnp.sum(moved * moved, axis=0, keepdims=True)
        scale = lax.rsqrt(spread / width + 1e-06)
        for part in range(parts):
            rows = slice(part * part_width, (part + 1) * part_width)
            wide = jnp.concatenate([gain[rows]] * (patch_count // LANES), axis=1)
            normed[rows, columns] = (
                (full[part, rank].astype(f32) - centre) * scale * wide
            ).astype(bf16)

    spot_row = lax.broadcasted_iota(jnp.int32, (8, patch_count), 0)
    spot_key = lax.broadcasted_iota(jnp.int32, (8, patch_count), 1)
    ones_row = jnp.where(spot_row == 0, 1.0, 0.0).astype(f32)

    def extended(member, head_id, columns, extra):
        rows = slice(head_id * VHD, (head_id + 1) * VHD)
        return jnp.concatenate([qkv[member, rows, columns], extra], axis=0).astype(bf16)

    def score(head_id, columns, key_row):
        return lax.dot_general(
            extended(1, head_id, columns, key_row),
            extended(0, head_id, columns, ones_row),
            CONTRACT_FIRST,
            preferred_element_type=f32,
        )

    def mix(head_id, columns, scores):
        powered = jnp.exp2((scores - jnp.max(scores, axis=0, keepdims=True)) * factor)
        mixed = jnp.dot(
            extended(2, head_id, columns, ones_row),
            powered.astype(bf16),
            preferred_element_type=f32,
        )
        context[head_id * VHD : (head_id + 1) * VHD, columns] = mixed[:VHD] * (
            1.0 / mixed[VHD : VHD + 1]
        )

    pool_row = lax.broadcasted_iota(jnp.int32, (tokens, patch_count), 0)
    pool_column = lax.broadcasted_iota(jnp.int32, (tokens, patch_count), 1)
    pooling = jnp.where(pool_column // POOL == pool_row, 1.0 / POOL, 0.0).astype(bf16)
    token_spot = lax.broadcasted_iota(jnp.int32, (tokens, part_width), 0) * POOL
    spans = [slice(b * patch_count, (b + 1) * patch_count) for b in range(batch)]

    def post(spot):
        outbox[spot] = pooled_frames[rank_ref[spot]]

    def settle(rank):
        for step in range(parts - 1):
            partial_copy(step, rank).wait_recv()
        total = mine[rank]
        for step in range(parts - 1):
            total = total + partial_in[rank, step].astype(f32)
        total = jnp.where(token_spot < valid_ref[rank], total, 0.0).astype(bf16)
        for at in range(fold):
            pooled_frames[rank, :, at * part_width : (at + 1) * part_width] = total[
                at * lines : (at + 1) * lines
            ]
        post(rank)
        frame_copy(rank).start()

    def forward(spot):
        frame_copy(spot).wait_recv()
        for step in range(parts - 1):
            forward_copy(step, spot, head).start()

    def body(turn, carry):
        ranks = [turn * batch + b for b in range(batch)]
        for rank, span in zip(ranks, spans):
            for step in range(parts - 1):
                patch_copy(step, rank, sources[step]).wait_recv()
            normalise(rank, span)

        @pl.when(turn >= 1)
        def _():
            for b in range(batch):
                settle((turn - 1) * batch + b)

        @pl.when(turn == 0)
        def _():
            qkv_load.wait()
            out_load.wait()

        for member in range(3):
            qkv[member] = jnp.dot(wqkv_ref[member], normed[...], preferred_element_type=f32)

        @pl.when(turn >= 3)
        def _():
            for b in range(batch):
                forward((turn - 3) * batch + b)

        key_rows = [
            jnp.where((spot_row == 0) & (spot_key >= valid_ref[rank]), -1e30, 0.0).astype(f32)
            for rank in ranks
        ]
        todo = [(head_id, b) for head_id in range(heads) for b in range(batch)]
        ahead = 4
        ready = [score(h, spans[b], key_rows[b]) for h, b in todo[:ahead]]
        for at, (h, b) in enumerate(todo):
            if at + ahead < len(todo):
                later, which = todo[at + ahead]
                ready.append(score(later, spans[which], key_rows[which]))
            mix(h, spans[b], ready[at])
        pooled = jnp.concatenate(
            [
                lax.dot_general(
                    pooling,
                    context[:, span].astype(bf16),
                    CONTRACT_LAST,
                    preferred_element_type=f32,
                ).astype(bf16)
                for span in spans
            ],
            axis=0,
        )
        attended = jnp.dot(pooled, wout_ref[...], preferred_element_type=f32)
        for b, rank in enumerate(ranks):
            own = lax.dot_general(
                pooling, full[head, rank], CONTRACT_LAST, preferred_element_type=f32
            )
            for part in range(parts):
                block = attended[
                    b * tokens : (b + 1) * tokens, part * part_width : (part + 1) * part_width
                ]
                partial[rank, part] = block.astype(bf16)
                own = own + jnp.where(head == part, block, 0.0)
            mine[rank] = own
            for step in range(parts - 1):
                partial_copy(step, rank).start()
        return carry

    turns = frames // batch
    lax.fori_loop(0, turns, body, 0)
    for rank in range(frames - batch, frames):
        settle(rank)
    for spot in range(frames, shards):
        post(spot)
        if spot < shards - 1:
            frame_copy(spot).start()
    out_ref[head, shards - 1] = outbox[shards - 1]
    for step in range(parts - 1):
        forward_copy(step, shards - 1, head).start()

    def late_forward(spot, carry):
        forward(spot)
        return carry

    lax.fori_loop(max(turns - 3, 0) * batch, shards - 1, late_forward, 0)

    def drain_ranks(rank, carry):
        for step in range(parts - 1):
            patch_copy(step, rank, head).wait_send()
            partial_copy(step, rank).wait_send()
        return carry

    lax.fori_loop(0, frames, drain_ranks, 0)

    def drain_frames(spot, carry):
        frame_copy(spot).wait_send()
        label_copy(spot).wait()
        return carry

    lax.fori_loop(0, shards - 1, drain_frames, 0)

    def drain_forwards(spot, carry):
        for step in range(parts - 1):
            forward_copy(step, spot, sources[step]).wait_recv()
            forward_copy(step, spot, head).wait_send()
        return carry

    lax.fori_loop(0, shards, drain_forwards, 0)


def vision(patches, order, valid, rank, label, gain, w_qkv, w_out, parts, shards):
    frames, part_width, patch_count = patches.shape
    width = parts * part_width
    local_width = w_qkv.shape[1]
    tokens = patch_count // POOL
    batch = math.gcd(frames, 2)
    in_smem = pl.BlockSpec(memory_space=pltpu.SMEM)
    in_vmem = pl.BlockSpec(memory_space=VMEM)
    in_hbm = pl.BlockSpec(memory_space=pl.ANY)
    peers = parts - 1
    fold = 2 if part_width % LANES == LANES // 2 and tokens % 32 == 0 else 1
    lines = (tokens // fold, part_width * fold)
    dma = pltpu.SemaphoreType.DMA
    return pl.pallas_call(
        vision_kernel,
        out_shape=(
            jax.ShapeDtypeStruct((parts, shards) + lines, bf16),
            jax.ShapeDtypeStruct((shards, 8, LANES), f32),
        ),
        in_specs=[in_smem] * 4 + [in_vmem] * 2 + [in_hbm] * 2,
        out_specs=(in_vmem, in_vmem),
        scratch_shapes=[
            VMEM(w_qkv.shape, bf16),
            VMEM(w_out.shape, bf16),
            VMEM((shards, 8, LANES), f32),
            VMEM((parts, frames, part_width, patch_count), bf16),
            VMEM((width, LANES), f32),
            VMEM((width, batch * patch_count), bf16),
            VMEM((3, local_width, batch * patch_count), f32),
            VMEM((local_width, batch * patch_count), f32),
            VMEM((frames, parts, tokens, part_width), bf16),
            VMEM((frames, peers, tokens, part_width), bf16),
            VMEM((frames, tokens, part_width), f32),
            VMEM((frames,) + lines, bf16),
            VMEM((shards,) + lines, bf16),
            dma((2,)),
            dma((shards,)),
            dma((shards,)),
            dma((peers, frames)),
            dma((peers, frames)),
            dma((peers, frames)),
            dma((peers, frames)),
            dma((shards,)),
            dma((shards,)),
            dma((peers, shards)),
            dma((peers, shards)),
        ],
        compiler_params=pltpu.CompilerParams(
            collective_id=0, has_side_effects=True, vmem_limit_bytes=56 << 20
        ),
        cost_estimate=pl.CostEstimate(
            flops=frames * patch_count * width * local_width * 10,
            bytes_accessed=12_000_000,
            transcendentals=4_000_000,
        ),
        name="vision",
    )(order, valid, rank, label, patches, gain, w_qkv, w_out)


def routes(frame_ids, grid_rows, shards):
    frames = frame_ids.shape[0]
    tm = lax.axis_index("tm").astype(jnp.int32)
    spots = jnp.arange(shards, dtype=jnp.int32)
    targets = partners(tm, spots, shards)[0]
    slots = jnp.arange(frames, dtype=jnp.int32)
    total = lambda chosen, member, axis: jnp.sum(
        jnp.where(chosen, member, 0), axis=axis
    ).astype(jnp.int32)
    goes = (frame_ids // frames)[:, None] == targets[None, :]
    spot_of = total(goes, spots[None, :], 1)
    rank_of = jnp.sum(spot_of[None, :] < spot_of[:, None], axis=1).astype(jnp.int32)
    holds = rank_of[None, :] == slots[:, None]
    order = total(holds, slots[None, :], 1)
    valid = total(holds, (grid_rows * GRID)[None, :], 1)
    rank = total(goes, rank_of[:, None], 0)
    label = total(goes, (frame_ids % frames + 1)[:, None], 0)
    return order, valid, rank, label


def spread(rows, width, copies):
    heads = rows // copies
    row = lax.broadcasted_iota(jnp.int32, (rows, heads * width), 0) % heads
    block = lax.broadcasted_iota(jnp.int32, (rows, heads * width), 1) // width
    return jnp.where(row == block, 1.0, 0.0).astype(bf16)


def split(values, copies):
    terms = []
    for _ in range(copies):
        terms.append(values.astype(bf16).astype(f32))
        values = values - terms[-1]
    return jnp.concatenate(terms, axis=0).astype(bf16)


def column(row):
    count = row.shape[1]
    same = lax.broadcasted_iota(jnp.int32, (count, count), 0) == lax.broadcasted_iota(
        jnp.int32, (count, count), 1
    )
    return jnp.sum(jnp.where(same, row, 0.0), axis=1, keepdims=True)


def connect_kernel(
    arrived_hbm,
    labels,
    norm_gain_ref,
    conn_hbm,
    stream_hbm,
    normed_hbm,
    squares,
    arrived_ref,
    conn,
    rows,
    even,
    odd,
    gained,
    plain,
    sender_ref,
    arrived_sem,
    conn_sem,
    normed_sem,
    stream_sem,
):
    parts, shards, lines, folded = arrived_ref.shape
    tokens = rows.shape[0]
    conn_count, width, conn_width = conn.shape
    part_width = width // parts
    per_part = conn_count // parts
    fold = folded // part_width
    frame_tokens = lines * fold
    frames = tokens // frame_tokens
    head = lax.axis_index("head")
    arrived_copy = pltpu.make_async_copy(arrived_hbm, arrived_ref, arrived_sem)
    arrived_copy.start()

    def conn_load(at):
        return pltpu.make_async_copy(
            conn_hbm.at[
                at // per_part,
                :,
                pl.ds(pl.multiple_of((at % per_part) * conn_width, conn_width), conn_width),
            ],
            conn.at[at],
            conn_sem.at[at],
        )

    def conn_start(at, carry):
        conn_load(at).start()
        return carry

    lax.fori_loop(0, conn_count, conn_start, 0)
    for shard in range(shards):
        sender_ref[jnp.max(labels[shard]).astype(jnp.int32)] = shard
    arrived_copy.wait()

    def gather(frame, carry):
        for at in range(fold):
            first = pl.multiple_of(frame * frame_tokens + at * lines, lines)
            for part in range(parts):
                rows[pl.ds(first, lines), part * part_width : (part + 1) * part_width] = (
                    arrived_ref[
                        part,
                        sender_ref[frame + 1],
                        :,
                        at * part_width : (at + 1) * part_width,
                    ]
                )
        return carry

    lax.fori_loop(0, frames, gather, 0)
    squares[...] = jnp.zeros_like(squares)

    def normed_copy(at):
        columns = pl.ds(pl.multiple_of(at * conn_width, conn_width), conn_width)
        return pltpu.make_async_copy(gained.at[at], normed_hbm.at[:, columns], normed_sem.at[at])

    def stream_copy(at):
        mine = pl.ds(pl.multiple_of((at % per_part) * conn_width, conn_width), conn_width)
        return pltpu.make_async_copy(
            plain.at[at], stream_hbm.at[:, mine], stream_sem.at[at % per_part]
        )

    def multiply(at, total):
        total[...] = jnp.dot(rows[...], conn[at], preferred_element_type=f32)

    def settle(at, total):
        columns = pl.ds(pl.multiple_of(at * conn_width, conn_width), conn_width)
        made = total[...].astype(bf16)
        plain[at] = made
        made = made.astype(f32)
        gained[at] = (made * norm_gain_ref[:, columns]).astype(bf16)
        made = made * made
        squares[...] += sum(
            made[:, lane : lane + LANES] for lane in range(0, conn_width, LANES)
        )

    def send(at):
        normed_copy(at).start()

        @pl.when(at // per_part == head)
        def _():
            stream_copy(at).start()

    def connect(turn, carry):
        at = turn * 2
        conn_load(at + 1).wait()
        conn_load(at + 2).wait()
        multiply(at + 1, odd)
        settle(at, even)
        multiply(at + 2, even)
        settle(at + 1, odd)
        send(at)
        send(at + 1)
        return carry

    conn_load(0).wait()
    multiply(0, even)
    pairs = (conn_count - 1) // 2
    lax.fori_loop(0, pairs, connect, 0)
    for at in range(2 * pairs, conn_count):
        if at > 2 * pairs:
            conn_load(at).wait()
            multiply(at, even)
        settle(at, even)
        send(at)

    def drain(at, carry):
        normed_copy(at).wait()
        return carry

    lax.fori_loop(0, conn_count, drain, 0)
    for at in range(per_part):
        stream_copy(head * per_part + at).wait()


def connect(arrived, labels, frames, weights, norm_gain, features):
    parts, _, lines, folded = arrived.shape
    _, width, columns = weights.shape
    tokens = frames * lines * (folded * parts // width)
    full_width = parts * columns
    conn_width = math.gcd(columns, features)
    conn_count = full_width // conn_width
    in_vmem = pl.BlockSpec(memory_space=VMEM)
    in_hbm = pl.BlockSpec(memory_space=pl.ANY)
    return pl.pallas_call(
        connect_kernel,
        out_shape=(
            jax.ShapeDtypeStruct((tokens, columns), bf16),
            jax.ShapeDtypeStruct((tokens, full_width), bf16),
            jax.ShapeDtypeStruct((tokens, LANES), f32),
        ),
        in_specs=[in_hbm, in_vmem, in_vmem, in_hbm],
        out_specs=(in_hbm, in_hbm, in_vmem),
        scratch_shapes=[
            VMEM(arrived.shape, bf16),
            VMEM((conn_count, width, conn_width), bf16),
            VMEM((tokens, width), bf16),
            VMEM((tokens, conn_width), f32),
            VMEM((tokens, conn_width), f32),
            VMEM((conn_count, tokens, conn_width), bf16),
            VMEM((conn_count, tokens, conn_width), bf16),
            pltpu.SMEM((frames + 1,), jnp.int32),
            pltpu.SemaphoreType.DMA(()),
            pltpu.SemaphoreType.DMA((conn_count,)),
            pltpu.SemaphoreType.DMA((conn_count,)),
            pltpu.SemaphoreType.DMA((columns // conn_width,)),
        ],
        compiler_params=pltpu.CompilerParams(vmem_limit_bytes=60 << 20),
        name="connect",
    )(arrived, labels, norm_gain.reshape(1, -1), weights)


def mix_kernel(
    squares_ref,
    wdt_ref,
    bias_ref,
    alog_ref,
    skip_ref,
    out_gain_ref,
    normed_hbm,
    wx_hbm,
    wb_hbm,
    wc_hbm,
    out_hbm,
    normed,
    scales,
    ring,
    inner,
    write,
    read,
    result,
    local_out,
    staged,
    down,
    across,
    state,
    saved,
    state_out,
    state_in,
    before,
    incoming,
    cross_out,
    cross_in,
    decay_out,
    decay_in,
    normed_sem,
    ring_sem,
    out_sem,
    decay_send,
    decay_recv,
    first_send,
    first_recv,
    second_send,
    second_recv,
    cross_send,
    cross_recv,
):
    tokens, full_width = normed.shape
    heads = wdt_ref.shape[0]
    groups = write.shape[1] // STATE
    per_group = heads // groups
    features = per_group * HDIM
    chunks = tokens // CHUNK
    block = 2 * CHUNK
    batches, shards, slice_rows, _ = state_in.shape
    every = lax.axis_size("tm")
    sides = every // shards
    batch_groups = groups // batches
    piece = features // shards
    unit = min(piece, HDIM)
    pieces = piece // unit
    whole_tm, head = lax.axis_index("tm"), lax.axis_index("head")
    side, tm = whole_tm // shards, whole_tm % shards
    log2e = math.log2(math.e)

    def remote(source, target, send, recv, spot):
        return pltpu.make_async_remote_copy(
            src_ref=source,
            dst_ref=target,
            send_sem=send,
            recv_sem=recv,
            device_id=(side * shards + partners(tm, spot, shards)[0], head),
            device_id_type=MESH,
        )

    def target_of(spot):
        return partners(tm, spot, shards)[0]

    def decay_copy(spot):
        return remote(
            decay_out.at[target_of(spot)],
            decay_in.at[tm],
            decay_send.at[spot],
            decay_recv.at[spot],
            spot,
        )

    def first_copy(batch, spot):
        return remote(
            state_out.at[batch, target_of(spot)],
            state_in.at[batch, tm],
            first_send.at[batch, spot],
            first_recv.at[batch, spot],
            spot,
        )

    def second_copy(batch, spot):
        return remote(
            before.at[batch, target_of(spot)],
            incoming.at[batch, tm],
            second_send.at[batch, spot],
            second_recv.at[batch, spot],
            spot,
        )

    def over_spots(act):
        def step(spot, carry):
            act(spot)
            return carry

        lax.fori_loop(0, shards - 1, step, 0)

    across_sides = (whole_tm + shards) % every

    def cross_copy(batch):
        return pltpu.make_async_remote_copy(
            src_ref=cross_out.at[batch],
            dst_ref=cross_in.at[batch],
            send_sem=cross_send.at[batch],
            recv_sem=cross_recv.at[batch],
            device_id=(across_sides, head),
            device_id_type=MESH,
        )

    barrier = pltpu.get_barrier_semaphore()
    over_spots(
        lambda spot: pl.semaphore_signal(
            barrier,
            inc=1,
            device_id=(side * shards + partners(tm, spot, shards)[1], head),
            device_id_type=MESH,
        )
    )
    if sides > 1:
        pl.semaphore_signal(
            barrier, inc=1, device_id=(across_sides, head), device_id_type=MESH
        )

    def weight_load(which):
        slot = which % ring.shape[0]
        if which == 0 or which == groups + 1:
            source = wb_hbm if which == 0 else wc_hbm
            target = ring.at[slot, :, : groups * STATE]
        else:
            source = wx_hbm.at[:, (which - 1) * features : which * features]
            target = ring.at[slot]
        return pltpu.make_async_copy(source, target, ring_sem.at[slot])

    normed_copy = pltpu.make_async_copy(normed_hbm, normed, normed_sem)
    normed_copy.start()
    for which in range(ring.shape[0]):
        weight_load(which).start()
    mean = jnp.sum(squares_ref[...], axis=1, keepdims=True) / full_width
    scales[...] = jnp.broadcast_to(lax.rsqrt(mean + 1e-05), scales.shape)
    mean_row = lax.dot_general(
        jnp.ones((8, LANES), f32),
        squares_ref[...],
        CONTRACT_LAST,
        preferred_element_type=f32,
        precision=lax.Precision.HIGHEST,
    )
    scale_row = lax.rsqrt(mean_row[:1] / full_width + 1e-05)
    normed_copy.wait()

    raw = lax.dot_general(wdt_ref[...], normed[...], CONTRACT_LAST, preferred_element_type=f32)
    raw = raw * scale_row + column(bias_ref[...])
    step_size = jnp.maximum(raw, 0.0) + jnp.log1p(jnp.exp(-jnp.abs(raw)))
    rate = -jnp.exp(column(alog_ref[...])) * log2e
    log_decay = step_size * rate
    log_step = jnp.log(step_size) * log2e
    upper = jnp.where(
        lax.broadcasted_iota(jnp.int32, (CHUNK, CHUNK), 0)
        <= lax.broadcasted_iota(jnp.int32, (CHUNK, CHUNK), 1),
        1.0,
        0.0,
    ).astype(f32)
    ends = []
    for chunk in range(chunks):
        span = slice(chunk * CHUNK, (chunk + 1) * CHUNK)
        sums = jnp.dot(
            log_decay[:, span],
            upper,
            preferred_element_type=f32,
            precision=lax.Precision.HIGHEST,
        )
        down[chunk] = sums
        across[chunk] = sums - log_step[:, span]
        ends.append(sums[:, CHUNK - 1 :])
    total = jnp.zeros_like(ends[0])
    for chunk in range(chunks):
        staged[chunk] = jnp.broadcast_to(total, (heads, LANES))
        total = total + ends[chunk]
    staged[chunks] = jnp.broadcast_to(jnp.exp2(total), (heads, LANES))
    decay_out[...] = jnp.zeros_like(decay_out)
    for target in range(shards):
        for group in range(groups):
            for part in range(pieces):
                at = group * per_group + (target * piece + part * unit) // HDIM
                row = group * pieces + part
                decay_out[target, row : row + 1] = staged[chunks, at : at + 1]
    decay_in[tm] = decay_out[tm]
    pl.semaphore_wait(barrier, shards - 1 + sides - 1)
    over_spots(lambda spot: decay_copy(spot).start())

    def project(which, target, first_column, count):
        slot = which % ring.shape[0]
        weight_load(which).wait()

        def part(at, carry):
            span = pl.ds(pl.multiple_of(at * block, block), block)
            made = jnp.dot(normed[span, :], ring[slot, :, :count], preferred_element_type=f32)
            wide = jnp.concatenate([scales[span, :]] * (count // LANES), axis=1)
            target[span, first_column : first_column + count] = (made * wide).astype(bf16)
            return carry

        lax.fori_loop(0, tokens // block, part, 0)
        if which + ring.shape[0] <= groups + 1:
            weight_load(which + ring.shape[0]).start()

    spread_narrow = spread(2 * per_group, HDIM, 2)
    spread_wide = spread(3 * per_group, CHUNK, 3)
    head_row = lax.broadcasted_iota(jnp.int32, (per_group, features), 0)
    head_lane = lax.broadcasted_iota(jnp.int32, (per_group, features), 1) // HDIM

    def widen(values):
        return lax.dot_general(
            split(values, 2), spread_narrow, CONTRACT_FIRST, preferred_element_type=f32
        )

    def widen_row(values):
        return jnp.sum(jnp.where(head_row == head_lane, values, 0.0), axis=0, keepdims=True)

    def at_group(group, chunk):
        own = slice(group * per_group, (group + 1) * per_group)
        return (
            pl.ds(pl.multiple_of(chunk * CHUNK, CHUNK), CHUNK),
            slice(group * features, (group + 1) * features),
            slice(group * STATE, (group + 1) * STATE),
            own,
        )

    def states(group):
        state[...] = jnp.zeros_like(state)

        def step(chunk, carry):
            span, lanes, keys, own = at_group(group, chunk)
            sums, shifted = down[chunk, own], across[chunk, own]
            end = sums[:, CHUNK - 1 :]
            held = state[...]
            saved[group, chunk] = held.astype(bf16)
            scaled = (inner[span, lanes].astype(f32) * widen(jnp.exp2(end - shifted))).astype(bf16)
            state[...] = held * widen_row(jnp.exp2(end)) + lax.dot_general(
                write[span, keys], scaled, CONTRACT_FIRST, preferred_element_type=f32
            )
            return carry

        lax.fori_loop(0, chunks, step, 0, unroll=math.gcd(chunks, 3))
        batch, inside = group // batch_groups, group % batch_groups
        sideways = state[...].T.astype(bf16)
        for target in range(shards):
            state_out[batch, target, inside * piece : (inside + 1) * piece] = sideways[
                target * piece : (target + 1) * piece
            ]

    def send_first(batch):
        state_in[batch, tm] = state_out[batch, tm]
        over_spots(lambda spot: first_copy(batch, spot).start())

    def send_second(batch):
        if batch == 0:
            over_spots(lambda spot: decay_copy(spot).wait_recv())
        over_spots(lambda spot: first_copy(batch, spot).wait_recv())
        if sides > 1:

            @pl.when(side == 0)
            def _():
                cross_in[batch] = jnp.zeros(cross_in.shape[1:], bf16)

            @pl.when(side > 0)
            def _():
                cross_copy(batch).wait_recv()

        for inside in range(batch_groups):
            group = batch * batch_groups + inside
            for part in range(pieces):
                span = slice(inside * piece + part * unit, inside * piece + (part + 1) * unit)
                row = group * pieces + part
                current = jnp.zeros((unit, STATE), f32)
                if sides > 1:
                    current = cross_in[batch, span].astype(f32)
                for shard in range(shards):
                    before[batch, shard, span] = current.astype(bf16)
                    current = decay_in[shard, row : row + 1] * current + state_in[
                        batch, shard, span
                    ].astype(f32)
                cross_out[batch, span] = current.astype(bf16)
        if sides > 1:

            @pl.when(side == 0)
            def _():
                cross_copy(batch).start()

        incoming[batch, tm] = before[batch, tm]
        over_spots(lambda spot: second_copy(batch, spot).start())

    causal = lax.broadcasted_iota(jnp.int32, (CHUNK, CHUNK), 0) >= lax.broadcasted_iota(
        jnp.int32, (CHUNK, CHUNK), 1
    )
    lane = lax.broadcasted_iota(jnp.int32, (CHUNK, LANES), 1)
    skip_column = column(skip_ref[...])

    def local(group):
        skip = widen_row(skip_column[group * per_group : (group + 1) * per_group])

        def step(chunk, carry):
            span, lanes, keys, own = at_group(group, chunk)
            sums, shifted = down[chunk, own], across[chunk, own]
            readers = read[span, keys]
            crossing = lax.dot_general(
                readers, write[span, keys], CONTRACT_LAST, preferred_element_type=f32
            )
            crossing = jnp.where(causal, crossing, 0.0)
            downs = lax.dot_general(
                split(sums, 3), spread_wide, CONTRACT_FIRST, preferred_element_type=f32
            )
            grown = widen(jnp.exp2(sums))
            carried = jnp.dot(readers, saved[group, chunk], preferred_element_type=f32)
            for pair in range(features // LANES):
                at = slice(pair * LANES, (pair + 1) * LANES)
                here = slice(lanes.start + pair * LANES, lanes.start + (pair + 1) * LANES)
                values = inner[span, here]
                halves = []
                for one in (2 * pair, 2 * pair + 1):
                    spans = downs[:, one * CHUNK : (one + 1) * CHUNK] - shifted[one : one + 1]
                    halves.append((crossing * jnp.exp2(jnp.minimum(spans, 100.0))).astype(bf16))
                wide = values.astype(f32)
                stacked = jnp.concatenate(
                    [jnp.where(lane < HDIM, wide, 0.0), jnp.where(lane < HDIM, 0.0, wide)], axis=0
                ).astype(bf16)
                within = jnp.dot(
                    jnp.concatenate(halves, axis=1), stacked, preferred_element_type=f32
                )
                local_out[span, here] = within + carried[:, at] * grown[:, at] + skip[:, at] * wide
            return carry

        lax.fori_loop(0, chunks, step, 0, unroll=math.gcd(chunks, 3))

    def finish(group):
        batch, inside = group // batch_groups, group % batch_groups
        held = jnp.concatenate(
            [
                incoming[batch, shard, inside * piece : (inside + 1) * piece]
                for shard in range(shards)
            ],
            axis=0,
        )

        def step(chunk, carry):
            span, lanes, keys, own = at_group(group, chunk)
            grown = widen(jnp.exp2(down[chunk, own] + staged[chunk, own]))
            carried = lax.dot_general(
                read[span, keys], held, CONTRACT_LAST, preferred_element_type=f32
            )
            summed = local_out[span, lanes] + carried * grown
            mean = jnp.sum(summed * summed, axis=1, keepdims=True) / features
            result[span, lanes] = (
                summed * lax.rsqrt(mean + 1e-05) * out_gain_ref[:, lanes]
            ).astype(bf16)
            return carry

        lax.fori_loop(0, chunks, step, 0, unroll=math.gcd(chunks, 3))

    def out_copy(group):
        lanes = slice(group * features, (group + 1) * features)
        return pltpu.make_async_copy(
            result.at[:, lanes], out_hbm.at[:, lanes], out_sem.at[group]
        )

    project(0, write, 0, groups * STATE)
    for group in range(groups):
        project(group + 1, inner, group * features, features)
        states(group)
        if (group + 1) % batch_groups == 0:
            send_first(group // batch_groups)
    if batches > 1:
        send_second(0)
    project(groups + 1, read, 0, groups * STATE)
    for group in range(groups):
        if group == groups // 2:
            send_second(batches - 1)
        local(group)
    for group in range(groups):
        if group % batch_groups == 0:
            batch = group // batch_groups
            over_spots(lambda spot: second_copy(batch, spot).wait_recv())
        finish(group)
        out_copy(group).start()
    over_spots(lambda spot: decay_copy(spot).wait_send())
    for batch in range(batches):
        over_spots(lambda spot: first_copy(batch, spot).wait_send())
        over_spots(lambda spot: second_copy(batch, spot).wait_send())
        if sides > 1:

            @pl.when(side == 0)
            def _():
                cross_copy(batch).wait_send()

    for group in range(groups):
        out_copy(group).wait()


def mix(normed, squares, w_x, w_b, w_c, w_dt, dt_bias, a_log, d_skip, out_gain, shards):
    tokens = normed.shape[0]
    heads = w_dt.shape[1]
    groups = w_b.shape[1] // STATE
    features = heads // groups * HDIM
    chunks = tokens // CHUNK
    batches = math.gcd(groups, 2)
    shards = shards // math.gcd(shards, 2)
    piece = features // shards
    slice_rows = groups // batches * piece
    pieces = max(piece // HDIM, 1)
    decay_rows = -(-groups * pieces // 8) * 8
    in_vmem = pl.BlockSpec(memory_space=VMEM)
    in_hbm = pl.BlockSpec(memory_space=pl.ANY)
    dma = pltpu.SemaphoreType.DMA
    shape = jax.ShapeDtypeStruct((tokens, heads * HDIM), bf16)
    row = lambda member: member.reshape(1, -1)
    return pl.pallas_call(
        mix_kernel,
        out_shape=shape,
        in_specs=[in_vmem] * 6 + [in_hbm] * 4,
        out_specs=in_hbm,
        scratch_shapes=[
            VMEM(normed.shape, bf16),
            VMEM((tokens, LANES), f32),
            VMEM((min(3, groups + 2), w_x.shape[0], features), bf16),
            VMEM((tokens, heads * HDIM), bf16),
            VMEM((tokens, groups * STATE), bf16),
            VMEM((tokens, groups * STATE), bf16),
            VMEM((tokens, heads * HDIM), bf16),
            VMEM((tokens, heads * HDIM), f32),
            VMEM((chunks + 1, heads, LANES), f32),
            VMEM((chunks, heads, CHUNK), f32),
            VMEM((chunks, heads, CHUNK), f32),
            VMEM((STATE, features), f32),
            VMEM((groups, chunks, STATE, features), bf16),
            VMEM((batches, shards, slice_rows, STATE), bf16),
            VMEM((batches, shards, slice_rows, STATE), bf16),
            VMEM((batches, shards, slice_rows, STATE), bf16),
            VMEM((batches, shards, slice_rows, STATE), bf16),
            VMEM((batches, slice_rows, STATE), bf16),
            VMEM((batches, slice_rows, STATE), bf16),
            VMEM((shards, decay_rows, LANES), f32),
            VMEM((shards, decay_rows, LANES), f32),
            dma(()),
            dma((min(3, groups + 2),)),
            dma((groups,)),
            dma((shards,)),
            dma((shards,)),
            dma((batches, shards)),
            dma((batches, shards)),
            dma((batches, shards)),
            dma((batches, shards)),
            dma((batches,)),
            dma((batches,)),
        ],
        compiler_params=pltpu.CompilerParams(
            collective_id=1, has_side_effects=True, vmem_limit_bytes=50 << 20
        ),
        name="mix",
    )(
        squares,
        w_dt.T,
        row(dt_bias),
        row(a_log),
        row(d_skip),
        row(out_gain),
        normed,
        w_x,
        w_b,
        w_c,
    )


def on_device(
    patches,
    grid_rows,
    frame_ids,
    ln_gain,
    w_qkv,
    w_out,
    w_conn,
    norm_gain,
    w_x,
    w_b,
    w_c,
    w_dt,
    dt_bias,
    a_log,
    d_skip,
    out_gain,
):
    part_width = patches.shape[2]
    shards = lax.axis_size("tm")
    my = lax.axis_index("head").astype(jnp.int32).reshape(1)
    parts = lax.axis_size("head")
    all_conn = lax.all_gather(w_conn, "head")
    order, valid, rank, label = routes(frame_ids, grid_rows, shards)
    arrived, labels = vision(
        patches.swapaxes(1, 2),
        order,
        valid,
        rank,
        label,
        ln_gain.reshape(1, -1),
        w_qkv.swapaxes(1, 2),
        w_out,
        parts,
        shards,
    )
    features = w_dt.shape[1] // (w_b.shape[1] // STATE) * HDIM
    stream, normed, squares = connect(
        arrived, labels, frame_ids.shape[0], all_conn, norm_gain, features)
    return stream, mix(
        normed, squares, w_x, w_b, w_c, w_dt, dt_bias, a_log, d_skip, out_gain, shards)


def solution(mesh):
    in_specs = (
        P("tm", None, "head"),
        P("tm"),
        P("tm"),
        P(),
        P(None, None, "head"),
        P("head", None),
        P(None, "head"),
        P(),
        P(None, "head"),
        P(None, "head"),
        P(None, "head"),
        P(None, "head"),
        P("head"),
        P("head"),
        P("head"),
        P("head"),
    )
    out_specs = (P("tm", "head"), P("tm", "head"))
    return jax.shard_map(
        on_device, mesh=mesh, in_specs=in_specs, out_specs=out_specs, check_vma=False
    )
```
